128 devices in a mesh: grp: 8 (over x_hi, y), blk: 16 (over z, x_lo, core).
Axes of the slice: x: 4 (x_hi: 2, x_lo: 2; x = x_hi * 2 + x_lo), y: 4, z: 4, core: 2. Of those that a mesh axis runs over, the one named last changes fastest.
Arguments:
- queries: bfloat16 [8, 2048, 4096], P('grp', 'blk'), may hold values from -5 to 5
- keys: bfloat16 [8, 2048, 256], P('grp', 'blk'), may hold values from -5 to 5
- values: bfloat16 [8, 2048, 256], P('grp', 'blk'), may hold values from -6 to 6
- stream: bfloat16 [8, 2048, 4096], P('grp', 'blk'), may hold values from -6 to 6
- norm_gain: float32 [4096], replicated, may hold values from 0.1 to 1.9
- router_weight: bfloat16 [4096, 128], replicated, may hold values from -0.09375 to 0.09375
- gate_weight: bfloat16 [128, 4096, 768], P(('grp', 'blk')), may hold values from -0.09375 to 0.09375
- up_weight: bfloat16 [128, 4096, 768], P(('grp', 'blk')), may hold values from -0.09375 to 0.09375
- down_weight: bfloat16 [128, 768, 4096], P(('grp', 'blk')), may hold values from -0.21875 to 0.21875
- doc_lengths: int32 [8, 4], P('grp'), may hold values from 1 to 1536, 2048 in all within a row
- expert_ids: int32 [8, 2048, 2], P('grp', 'blk'), may hold values from 0 to 127, all different within a row; in each aligned block of 128 rows (0 to 127, 128 to 255, ..., all dimensions but the last counted through in order) at most 3 rows name the same one
- out_grad: bfloat16 [8, 2048, 4096], P('grp', 'blk'), may hold values from -6 to 6
Outputs:
- query_grad: bfloat16 [8, 2048, 4096], P('grp', 'blk')
- key_gradient_rows: bfloat16 [8, 2048, 256], P('grp', 'blk')
- value_gradient_rows: bfloat16 [8, 2048, 256], P('grp', 'blk')
- residual_gradient: bfloat16 [8, 2048, 4096], P('grp', 'blk')
- router_grad: float32 [4096, 128], P(('grp', 'blk'))
The draws below stay inside these ranges and needn't reach their ends.
Inputs may be any that keep to these rules, and one draw needn't show every extreme that they name: `doc_lengths`: each row sums to 2048; the longest document of every sequence holds exactly (6144) // 4 tokens. `expert_ids`: each token names 2 different experts. Among the 128 tokens of one device no expert is named more than 3 times, and in some devices one expert is named exactly 3 times.
All inputs are finite; a program needn't handle non-finite values.
Results may differ from the reference program's by a relative error of at most 0.035.
Values may be sent and summed in bfloat16 or wider, within the bound.
No kernel may reach another device: no remote copies, remote signals or barrier semaphores. Data moves between devices by JAX's collectives and lax.ppermute only.
A program may use at most 128 MiB of HBM per device.

```python
import math
import jax
import jax.numpy as jnp
import numpy as np
from jax import lax

D = 4096
HEAD_SIZE = 128
QUERY_HEADS = 32
KEY_VALUE_HEADS = 2
F = 768
TOP = 2
DOCS = 4
TOK_DEV = 128
SEQUENCE_COUNT = 8
SEQUENCE_LENGTH = 2048
E = 128
CAP = 3


def draw_queries(key, part):
    offset_start = jnp.clip(jax.random.normal(jax.random.fold_in(key, 11), (SEQUENCE_COUNT, SEQUENCE_LENGTH, QUERY_HEADS, HEAD_SIZE), jnp.float32), -4.0, 4.0)
    return offset_start.reshape(SEQUENCE_COUNT, SEQUENCE_LENGTH, QUERY_HEADS * HEAD_SIZE).astype(jnp.bfloat16)


def draw_keys(key, part):
    offset_start = jnp.clip(jax.random.normal(jax.random.fold_in(key, 13), (SEQUENCE_COUNT, SEQUENCE_LENGTH, KEY_VALUE_HEADS, HEAD_SIZE), jnp.float32), -4.0, 4.0)
    return offset_start.reshape(SEQUENCE_COUNT, SEQUENCE_LENGTH, KEY_VALUE_HEADS * HEAD_SIZE).astype(jnp.bfloat16)


def level_of(stream_key, shape, pieces, smallest, top_value):
    factor_of = 1.0
    for axis_at, parts in pieces:
        draws = jax.random.uniform(jax.random.fold_in(jax.random.fold_in(stream_key, 6), axis_at), (parts,), jnp.float32, smallest / len(pieces), top_value / len(pieces))
        factor_of = factor_of * jnp.repeat(jnp.exp(draws), shape[axis_at] // parts).reshape((-1,) + (1,) * (len(shape) - 1 - axis_at))
    return factor_of


def length_profile(count, total, most, skew):
    loads = [(1 << 20) // math.isqrt(standing ** skew) + 1 for standing in range(2, count + 1)]
    surplus, holding = total - most - (count - 1), [1] * (count - 1)
    while surplus > 0:
        free = [i for i in range(count - 1) if holding[i] < most]
        whole, left = sum([loads[i] for i in free]), surplus
        for i in free:
            more = min(most - holding[i], max(1, left * loads[i] // whole), surplus)
            holding[i] = holding[i] + more
            surplus = surplus - more
    return np.array([most] + holding)


def uneven(rng, number_of, total, most, lean):
    if number_of == 2:
        one = jax.random.randint(rng, (), max(1, total - most), min(most, total - 1) + 1)
        return jnp.stack([one, total - one])
    lengths = jnp.asarray(length_profile(number_of, total, most, lean), jnp.int32)
    twos = (number_of - 1) // 2
    donor, receiver = lengths[1:1 + 2 * twos:2], lengths[2:2 + 2 * twos:2]
    slack = jnp.minimum(donor - 1, most - receiver)
    moved = jax.random.randint(jax.random.fold_in(rng, 1), (twos,), 0, 1 << 20) % (slack + 1)
    lengths = lengths.at[1:1 + 2 * twos:2].set(donor - moved).at[2:2 + 2 * twos:2].set(receiver + moved)
    return lengths[jax.random.permutation(jax.random.fold_in(rng, 2), number_of)]


def routed_block(stream_key, own, number, rows, count, top, reach, lean):
    order = jax.random.permutation(stream_key, count)
    packed, usual = load_shares(count, rows * top, reach, lean, True), load_shares(count, rows * top, reach, lean, False)
    places = jnp.arange(count)

    def named(lengths, turn):
        used = int((lengths > 0).sum())
        fixed = max(1, used // 4)
        shifted = fixed + (places - fixed + turn * (used - fixed)) % max(1, count - fixed)
        return jnp.zeros((count,), jnp.int32).at[order[jnp.where(places < fixed, places, shifted)]].set(jnp.asarray(lengths, jnp.int32))

    lengths = jnp.where(number % 4 == 0, named(packed, number // 4), named(usual, number - number // 4 - 1))
    mixed = jax.random.permutation(jax.random.fold_in(own, 3), count)
    donor, taker = mixed[0:count // 2 * 2:2], mixed[1:count // 2 * 2:2]
    margin = jnp.minimum(lengths[donor] - 1, reach - lengths[taker]) // 2
    margin = jnp.where((donor == order[0]) | (taker == order[0]) | (lengths[taker] == 0), 0, jnp.maximum(margin, 0))
    shifted = jax.random.randint(jax.random.fold_in(own, 4), (count // 2,), 0, 1 << 20) % (margin + 1)
    lengths = lengths.at[donor].add(-shifted).at[taker].add(shifted)
    members = jnp.searchsorted(jnp.cumsum(lengths), jnp.arange(rows * top), side="right").astype(jnp.int32)
    grid = members.reshape(top, rows).T
    grid = grid[jax.random.permutation(jax.random.fold_in(own, 1), rows)]
    turn = jax.random.randint(jax.random.fold_in(own, 2), (rows, 1), 0, top)
    return jnp.take_along_axis(grid, (jnp.arange(top)[None, :] + turn) % top, axis=1)


def load_shares(number_of, total, bound, lean, full):
    loads = [(1 << 20) // math.isqrt(standing ** lean) + 1 for standing in range(1, number_of + 1)]
    largest = bound if full else min(bound, max(-(-total // number_of), total * loads[0] // sum(loads)))
    least = 1 if total - largest >= number_of - 1 else 0
    holding, spare = [largest] + [least] * (number_of - 1), total - largest - least * (number_of - 1)
    while spare > 0:
        free = [i for i in range(1, number_of) if holding[i] < largest] or [i for i in range(1, number_of) if holding[i] < bound]
        whole, remaining = sum([loads[i] for i in free]), spare
        for i in free:
            more = min(bound - holding[i], max(1, remaining * loads[i] // whole), spare)
            holding[i] = holding[i] + more
            spare = spare - more
    return np.array(holding)


def bell_draw(key, dims, deviation, limit, shards=(), kind=jnp.bfloat16):
    gain = level_of(key, dims, shards, -0.22, 0.18) if shards else 1.0
    drawn = jax.random.normal(key, dims, jnp.float32) * deviation * gain
    return jnp.minimum(jnp.maximum(drawn, -limit), limit).astype(kind)


def setup_inputs(seed: int = 0) -> dict:
    arg_keys = jax.random.split(jax.random.key(seed), 13)
    queries = draw_queries(jax.random.fold_in(arg_keys[12], 71), 0)
    keys = draw_keys(jax.random.fold_in(arg_keys[12], 71), 0)
    values = bell_draw(arg_keys[2], (SEQUENCE_COUNT, SEQUENCE_LENGTH, KEY_VALUE_HEADS * HEAD_SIZE), 1.0, 6.0, ((0, 8), (1, 16)))
    stream = bell_draw(arg_keys[3], (SEQUENCE_COUNT, SEQUENCE_LENGTH, D), 1.0, 6.0, ((0, 8), (1, 16)))
    norm_gain = jnp.clip(1.0 + 0.18 * jax.random.normal(arg_keys[4], (D,), jnp.float32), 0.1, 1.9)
    router_weight = bell_draw(arg_keys[5], (D, E), D ** -0.5, 0.09375)
    gate_weight = bell_draw(arg_keys[6], (E, D, F), D ** -0.5, 0.09375, ((0, 128),))
    up_weight = bell_draw(arg_keys[7], (E, D, F), D ** -0.5, 0.09375, ((0, 128),))
    down_weight = bell_draw(arg_keys[8], (E, F, D), F ** -0.5, 0.21875, ((0, 128),))
    doc_lengths = jax.vmap(lambda own: uneven(own, DOCS, SEQUENCE_LENGTH, (3 * SEQUENCE_LENGTH) // 4, 2))(jax.random.split(arg_keys[9], SEQUENCE_COUNT)).reshape((SEQUENCE_COUNT, DOCS)).astype(jnp.int32)
    expert_ids_keys = jax.random.split(jax.random.fold_in(arg_keys[10], 1), SEQUENCE_COUNT * SEQUENCE_LENGTH // TOK_DEV)
    expert_ids_turns = jax.random.permutation(jax.random.fold_in(arg_keys[10], 3), SEQUENCE_COUNT * SEQUENCE_LENGTH // TOK_DEV)
    expert_ids = jax.vmap(lambda own, number: routed_block(jax.random.fold_in(arg_keys[10], 2), own, number, TOK_DEV, E, TOP, CAP, 1))(expert_ids_keys, expert_ids_turns).reshape((SEQUENCE_COUNT, SEQUENCE_LENGTH, TOP))
    out_grad = bell_draw(arg_keys[11], (SEQUENCE_COUNT, SEQUENCE_LENGTH, D), 1.0, 6.0, ((0, 8), (1, 16)))
    return {"queries": queries, "keys": keys, "values": values, "stream": stream, "norm_gain": norm_gain, "router_weight": router_weight, "gate_weight": gate_weight, "up_weight": up_weight, "down_weight": down_weight, "doc_lengths": doc_lengths, "expert_ids": expert_ids, "out_grad": out_grad}


NEGATIVE_HUGE = -1e+30
EPSILON = 1e-06

def segment_of(positions, doc_ends):
    return lax.optimization_barrier(jnp.sum((positions[:, None] >= doc_ends[None, :]).astype(jnp.int32), axis=1, dtype=jnp.int32))

def visible_table(lengths_row):
    positions = jnp.arange(SEQUENCE_LENGTH, dtype=jnp.int32)
    segment = segment_of(positions, jnp.cumsum(lengths_row, dtype=jnp.int32))
    return (positions[None, :] <= positions[:, None]) & (segment[None, :] == segment[:, None])

def low_round(array):
    return lax.optimization_barrier(array.astype(jnp.bfloat16)).astype(jnp.float32)

def forward_group(group_queries, group_keys, group_values, allowed):
    scores = jnp.einsum('ljd,nd->jln', group_queries.astype(jnp.float32), group_keys.astype(jnp.float32)) * HEAD_SIZE ** (-0.5)
    row_max = lax.optimization_barrier(jnp.max(jnp.where(allowed, scores, NEGATIVE_HUGE), axis=-1))
    weights = jnp.where(allowed, jnp.exp(scores - row_max[..., None]), 0.0)
    total = lax.optimization_barrier(jnp.sum(weights, axis=-1))
    mixed = jnp.einsum('jln,nd->ljd', low_round(weights), group_values.astype(jnp.float32))
    return (mixed / jnp.transpose(total)[:, :, None], row_max + jnp.log(total))

def forward_sequence(inputs):
    sequence_queries, sequence_keys, sequence_values, lengths_row = inputs
    allowed = visible_table(lengths_row)
    query_head_rows = sequence_queries.reshape(SEQUENCE_LENGTH, KEY_VALUE_HEADS, QUERY_HEADS // KEY_VALUE_HEADS, HEAD_SIZE)
    key_head_rows = sequence_keys.reshape(SEQUENCE_LENGTH, KEY_VALUE_HEADS, HEAD_SIZE)
    value_head_rows = sequence_values.reshape(SEQUENCE_LENGTH, KEY_VALUE_HEADS, HEAD_SIZE)
    mixed_list = []
    total_list = []
    for head_group in range(KEY_VALUE_HEADS):
        mixed, log_total = forward_group(query_head_rows[:, head_group], key_head_rows[:, head_group], value_head_rows[:, head_group], allowed)
        mixed_list.append(mixed)
        total_list.append(log_total)
    attended = jnp.stack(mixed_list, axis=1).reshape(SEQUENCE_LENGTH, D).astype(jnp.bfloat16)
    return (attended, jnp.stack(total_list, axis=0))

def backward_group(group_queries, group_keys, group_values, group_grads, group_attended, log_total, allowed):
    scale = HEAD_SIZE ** (-0.5)
    queries_wide = group_queries.astype(jnp.float32)
    keys_wide = group_keys.astype(jnp.float32)
    values_wide = group_values.astype(jnp.float32)
    grads_wide = group_grads.astype(jnp.float32)
    scores = jnp.einsum('ljd,nd->jln', queries_wide, keys_wide) * scale
    probabilities = jnp.where(allowed, jnp.exp(scores - log_total[..., None]), 0.0)
    gradient_value_rows = jnp.einsum('jln,ljd->nd', low_round(probabilities), grads_wide)
    grad_probs = jnp.einsum('ljd,nd->jln', grads_wide, values_wide)
    row_dot = jnp.einsum('ljd,ljd->jl', grads_wide, group_attended.astype(jnp.float32))
    grad_scores = low_round(probabilities * (grad_probs - row_dot[..., None]))
    grad_query = scale * jnp.einsum('jln,nd->ljd', grad_scores, keys_wide)
    gradient_key_rows = scale * jnp.einsum('jln,ljd->nd', grad_scores, queries_wide)
    return (grad_query, gradient_key_rows, gradient_value_rows)

def backward_sequence(inputs):
    sequence_queries, sequence_keys, sequence_values, sequence_gradients, sequence_attended, seq_totals, lengths_row = inputs
    allowed = visible_table(lengths_row)
    heads_per_group = QUERY_HEADS // KEY_VALUE_HEADS
    query_head_rows = sequence_queries.reshape(SEQUENCE_LENGTH, KEY_VALUE_HEADS, heads_per_group, HEAD_SIZE)
    key_head_rows = sequence_keys.reshape(SEQUENCE_LENGTH, KEY_VALUE_HEADS, HEAD_SIZE)
    value_head_rows = sequence_values.reshape(SEQUENCE_LENGTH, KEY_VALUE_HEADS, HEAD_SIZE)
    gradient_head_rows = sequence_gradients.reshape(SEQUENCE_LENGTH, KEY_VALUE_HEADS, heads_per_group, HEAD_SIZE)
    attended_head_rows = sequence_attended.reshape(SEQUENCE_LENGTH, KEY_VALUE_HEADS, heads_per_group, HEAD_SIZE)
    query_list = []
    key_collection = []
    value_collection = []
    for head_group in range(KEY_VALUE_HEADS):
        grad_query, gradient_key_rows, gradient_value_rows = backward_group(query_head_rows[:, head_group], key_head_rows[:, head_group], value_head_rows[:, head_group], gradient_head_rows[:, head_group], attended_head_rows[:, head_group], seq_totals[head_group], allowed)
        query_list.append(grad_query)
        key_collection.append(gradient_key_rows)
        value_collection.append(gradient_value_rows)
    query_grad = jnp.stack(query_list, axis=1).reshape(SEQUENCE_LENGTH, D).astype(jnp.bfloat16)
    key_gradient_rows = jnp.stack(key_collection, axis=1).reshape(SEQUENCE_LENGTH, KEY_VALUE_HEADS * HEAD_SIZE).astype(jnp.bfloat16)
    value_gradient_rows = jnp.stack(value_collection, axis=1).reshape(SEQUENCE_LENGTH, KEY_VALUE_HEADS * HEAD_SIZE).astype(jnp.bfloat16)
    return (query_grad, key_gradient_rows, value_gradient_rows)

def expert_math(rows, grads, gate_vals, gate_mat, up_mat, down_mat):
    pre_gate = jnp.dot(rows, gate_mat, preferred_element_type=jnp.float32)
    pre_up = jnp.dot(rows, up_mat, preferred_element_type=jnp.float32)
    sigmoid_gate = jax.nn.sigmoid(pre_gate)
    activated = pre_gate * sigmoid_gate
    inner_act = (activated * pre_up).astype(jnp.bfloat16)
    output = jnp.dot(inner_act, down_mat, preferred_element_type=jnp.float32)
    grads_wide = grads.astype(jnp.float32)
    score_row = lax.optimization_barrier(jnp.sum(grads_wide * output, axis=-1)).astype(jnp.bfloat16)
    grad_output = (gate_vals.astype(jnp.float32)[:, None] * grads_wide).astype(jnp.bfloat16)
    grad_inner = jnp.dot(grad_output, jnp.transpose(down_mat), preferred_element_type=jnp.float32)
    grad_gate = (grad_inner * pre_up * sigmoid_gate * (1.0 + pre_gate * (1.0 - sigmoid_gate))).astype(jnp.bfloat16)
    grad_up = (grad_inner * activated).astype(jnp.bfloat16)
    grad_rows = jnp.dot(grad_gate, jnp.transpose(gate_mat), preferred_element_type=jnp.float32)
    grad_rows = grad_rows + jnp.dot(grad_up, jnp.transpose(up_mat), preferred_element_type=jnp.float32)
    return (grad_rows.astype(jnp.bfloat16), score_row)

def reference(queries, keys, values, stream, norm_gain, router_weight, gate_weight, up_weight, down_weight, doc_lengths, expert_ids, out_grad):
    attended, log_totals = lax.map(forward_sequence, (queries, keys, values, doc_lengths))
    tokens_all = SEQUENCE_COUNT * SEQUENCE_LENGTH
    assigns = tokens_all * TOP
    hidden = (stream.astype(jnp.float32) + attended.astype(jnp.float32)).astype(jnp.bfloat16).reshape(tokens_all, D)
    hidden_wide = hidden.astype(jnp.float32)
    inv_rms = lax.rsqrt(lax.optimization_barrier(jnp.mean(hidden_wide * hidden_wide, axis=-1, keepdims=True)) + EPSILON)
    normed = (hidden_wide * inv_rms * norm_gain).astype(jnp.bfloat16)
    logits = jnp.dot(normed, router_weight, preferred_element_type=jnp.float32)
    flat_ids = expert_ids.reshape(tokens_all, TOP)
    chosen = jnp.take_along_axis(logits, flat_ids, axis=1)
    first_gate = jax.nn.sigmoid(chosen[:, 0] - chosen[:, 1])
    gate_pair = jnp.stack([first_gate, 1.0 - first_gate], axis=1)
    gate_low = gate_pair.astype(jnp.bfloat16)
    grads_flat = out_grad.reshape(tokens_all, D)
    flat_assign = flat_ids.reshape(assigns)
    hit_table = (flat_assign[:, None] == jnp.arange(E, dtype=jnp.int32)[None, :]).astype(jnp.int32)
    slot_rank = lax.optimization_barrier(jnp.sum((jnp.cumsum(hit_table, axis=0, dtype=jnp.int32) - hit_table) * hit_table, axis=1, dtype=jnp.int32))
    row_table = jnp.full((E, E * CAP), assigns, jnp.int32).at[flat_assign, slot_rank].set(jnp.arange(assigns, dtype=jnp.int32))

    def one_expert(carry, expert_args):
        grad_acc, score_acc = carry
        gate_mat, up_mat, down_mat, assigned = expert_args
        valid = assigned < assigns
        token_row = jnp.where(valid, assigned // TOP, 0).astype(jnp.int32)
        which_gate = (assigned % TOP).astype(jnp.int32)
        grad_rows, score_row = expert_math(normed[token_row], grads_flat[token_row], gate_low[token_row, which_gate], gate_mat, up_mat, down_mat)
        grad_acc = grad_acc.at[token_row].add(jnp.where(valid[:, None], grad_rows.astype(jnp.float32), 0.0))
        score_acc = score_acc.at[jnp.where(valid, assigned, assigns)].set(score_row.astype(jnp.float32), mode='drop')
        return ((grad_acc, score_acc), None)
    start_carry = (jnp.zeros((tokens_all, D), jnp.float32), jnp.zeros((assigns,), jnp.float32))
    (grad_expert, score_all), _ = lax.scan(one_expert, start_carry, (gate_weight, up_weight, down_weight, row_table))
    token_score = score_all.reshape(tokens_all, TOP)
    grad_first = first_gate * (1.0 - first_gate) * (token_score[:, 0] - token_score[:, 1])
    token_index = jnp.arange(tokens_all, dtype=jnp.int32)
    d_logits = jnp.zeros((tokens_all, E), jnp.float32).at[token_index, flat_ids[:, 0]].add(grad_first)
    d_logits = d_logits.at[token_index, flat_ids[:, 1]].add(-grad_first).astype(jnp.bfloat16)
    router_grad = jnp.dot(jnp.transpose(normed), d_logits, preferred_element_type=jnp.float32)
    d_normed = grad_expert + jnp.dot(d_logits, jnp.transpose(router_weight), preferred_element_type=jnp.float32)
    scaled = norm_gain * d_normed
    residual_gradient = grads_flat.astype(jnp.float32) + inv_rms * scaled - hidden_wide * inv_rms ** 3 * lax.optimization_barrier(jnp.mean(hidden_wide * scaled, axis=-1, keepdims=True))
    residual_gradient = residual_gradient.astype(jnp.bfloat16).reshape(SEQUENCE_COUNT, SEQUENCE_LENGTH, D)
    query_grad, key_gradient_rows, value_gradient_rows = lax.map(backward_sequence, (queries, keys, values, residual_gradient, attended, log_totals, doc_lengths))
    return (query_grad, key_gradient_rows, value_gradient_rows, residual_gradient, router_grad)
```

```python
import jax
import jax.numpy as jnp
from jax import lax
from jax.sharding import Mesh
from jax.sharding import PartitionSpec as P

HEAD_SIZE = 128
QUERY_HEADS = 32
KEY_VALUE_HEADS = 2
BLK = ("blk_0", "blk_1", "blk_2")
GRP_BLK = ("grp_0", "grp_1", "blk_0", "blk_1", "blk_2")
GRP = ("grp_0", "grp_1")


NEGATIVE_HUGE = -1e30
EPSILON = 1e-06


ZX = ("blk_0", "blk_1")
CORE = "blk_2"


def swap_cores(array):
    return lax.ppermute(array, CORE, [(0, 1), (1, 0)])


def gather_blocks(array):
    chips = lax.axis_size("blk_0") * lax.axis_size("blk_1")
    mine = lax.all_to_all(
        jnp.broadcast_to(array[None], (chips, *array.shape)), ZX, split_axis=0, concat_axis=0, tiled=True
    )
    theirs = swap_cores(mine)
    core = lax.axis_index(CORE)
    first = jnp.where(core == 0, mine, theirs)
    second = jnp.where(core == 0, theirs, mine)
    return jnp.stack([first, second], axis=1).reshape(-1, array.shape[-1])


def scatter_blocks(parts):
    chips = lax.axis_size("blk_0") * lax.axis_size("blk_1")
    pairs = parts.astype(jnp.bfloat16).reshape(chips, 2, *parts.shape[1:])
    core = lax.axis_index(CORE)
    keep = jnp.where(core == 0, pairs[:, 0], pairs[:, 1])
    give = jnp.where(core == 0, pairs[:, 1], pairs[:, 0])
    both = (keep.astype(jnp.float32) + swap_cores(give).astype(jnp.float32)).astype(jnp.bfloat16)
    got = lax.all_to_all(both, ZX, split_axis=0, concat_axis=0, tiled=True)
    return jnp.sum(got.astype(jnp.float32), axis=0)


def to_experts(rows, experts):
    count, width = rows.shape
    sent = rows.reshape(experts, count // experts * width // 128, 128)
    got = lax.all_to_all(sent, GRP_BLK, split_axis=0, concat_axis=0, tiled=True)
    return got.reshape(count, width)


def segment_of(positions, doc_ends):
    return jnp.sum(
        (positions[:, None] >= doc_ends[None, :]).astype(jnp.int32), axis=1, dtype=jnp.int32
    )


def visible_mask(query_pos, query_seg, key_pos, doc_ends):
    key_seg = segment_of(key_pos, doc_ends)
    return (key_pos[None, :] <= query_pos[:, None]) & (key_seg[None, :] == query_seg[:, None])


def block_width():
    return 512


def block_live(key_begin, present_width, query_pos, query_seg, doc_ends):
    last_key = jnp.reshape(key_begin + present_width - 1, (1,))
    return (key_begin <= query_pos[-1]) & (segment_of(last_key, doc_ends)[0] >= query_seg[0])


def attend_keys(
    running, key_rows_all, value_rows_all, query_head_rows, query_pos, query_seg, doc_ends
):
    key_count = key_rows_all.shape[0]
    present_width = block_width()
    scale = HEAD_SIZE ** (-0.5)

    def attend_one_block(carried, block_index):
        row_offset = block_index * present_width
        key_rows = lax.dynamic_slice_in_dim(key_rows_all, row_offset, present_width, 0).reshape(
            present_width, KEY_VALUE_HEADS, HEAD_SIZE
        )
        value_rows = lax.dynamic_slice_in_dim(value_rows_all, row_offset, present_width, 0).reshape(
            present_width, KEY_VALUE_HEADS, HEAD_SIZE
        )

        def attend_do_block(present_value):
            row_max, total, accumulated = present_value
            key_pos = row_offset + jnp.arange(present_width, dtype=jnp.int32)
            allowed = visible_mask(query_pos, query_seg, key_pos, doc_ends)
            scores = (
                jnp.einsum(
                    "tgjd,ngd->gjtn", query_head_rows, key_rows, preferred_element_type=jnp.float32
                )
                * scale
            )
            new_max = jnp.maximum(
                row_max, jnp.max(jnp.where(allowed, scores, NEGATIVE_HUGE), axis=-1)
            )
            weights = jnp.where(allowed, jnp.exp(scores - new_max[..., None]), 0.0)
            factor = jnp.exp(row_max - new_max)
            total = factor * total + jnp.sum(weights, axis=-1)
            accumulated = factor[..., None] * accumulated + jnp.einsum(
                "gjtn,ngd->gjtd",
                weights.astype(jnp.bfloat16),
                value_rows,
                preferred_element_type=jnp.float32,
            )
            return (new_max, total, accumulated)

        is_live = block_live(row_offset, present_width, query_pos, query_seg, doc_ends)
        return (
            lax.cond(is_live, attend_do_block, lambda present_value: present_value, carried),
            None,
        )

    running, _ = lax.scan(attend_one_block, running, jnp.arange(key_count // present_width))
    return running


def key_gradients(
    query_head_rows,
    gradient_head_rows,
    log_total,
    row_dot,
    key_rows_all,
    value_rows_all,
    query_pos,
    query_seg,
    doc_ends,
):
    key_count = key_rows_all.shape[0]
    present_width = block_width()
    scale = HEAD_SIZE ** (-0.5)
    token_rows = query_head_rows.shape[0]
    heads_per_group = query_head_rows.shape[2]

    def key_one_block(dq_acc, block_index):
        key_begin = block_index * present_width
        key_rows = lax.dynamic_slice_in_dim(key_rows_all, key_begin, present_width, 0).reshape(
            present_width, KEY_VALUE_HEADS, HEAD_SIZE
        )
        value_rows = lax.dynamic_slice_in_dim(value_rows_all, key_begin, present_width, 0).reshape(
            present_width, KEY_VALUE_HEADS, HEAD_SIZE
        )

        def key_do_block(present_value):
            key_pos = key_begin + jnp.arange(present_width, dtype=jnp.int32)
            allowed = visible_mask(query_pos, query_seg, key_pos, doc_ends)
            scores = (
                jnp.einsum(
                    "tgjd,ngd->gjtn", query_head_rows, key_rows, preferred_element_type=jnp.float32
                )
                * scale
            )
            probabilities = jnp.where(allowed, jnp.exp(scores - log_total[..., None]), 0.0)
            gradient_value_rows = jnp.einsum(
                "gjtn,tgjd->ngd",
                probabilities.astype(jnp.bfloat16),
                gradient_head_rows,
                preferred_element_type=jnp.float32,
            )
            grad_probs = jnp.einsum(
                "tgjd,ngd->gjtn", gradient_head_rows, value_rows, preferred_element_type=jnp.float32
            )
            grad_scores = (probabilities * (grad_probs - row_dot[..., None])).astype(jnp.bfloat16)
            present_value = present_value + scale * jnp.einsum(
                "gjtn,ngd->tgjd", grad_scores, key_rows, preferred_element_type=jnp.float32
            )
            gradient_key_rows = scale * jnp.einsum(
                "gjtn,tgjd->ngd", grad_scores, query_head_rows, preferred_element_type=jnp.float32
            )
            stacked = jnp.stack(
                [
                    gradient_key_rows.reshape(present_width, KEY_VALUE_HEADS * HEAD_SIZE),
                    gradient_value_rows.reshape(present_width, KEY_VALUE_HEADS * HEAD_SIZE),
                ],
                axis=1,
            )
            return (present_value, stacked)

        def no_block(present_value):
            return (
                present_value,
                jnp.zeros((present_width, 2, KEY_VALUE_HEADS * HEAD_SIZE), jnp.float32),
            )

        is_live = block_live(key_begin, present_width, query_pos, query_seg, doc_ends)
        return lax.cond(is_live, key_do_block, no_block, dq_acc)

    initial_gradient = jnp.zeros(
        (token_rows, KEY_VALUE_HEADS, heads_per_group, HEAD_SIZE), jnp.float32
    )
    return lax.scan(key_one_block, initial_gradient, jnp.arange(key_count // present_width))


def per_device(
    queries,
    keys,
    values,
    stream,
    norm_gain,
    router_weight,
    gate_weight,
    up_weight,
    down_weight,
    doc_lengths,
    expert_ids,
    out_grad,
):
    token_rows = queries.shape[1]
    model_width = queries.shape[2]
    heads_per_group = QUERY_HEADS // KEY_VALUE_HEADS
    doc_ends = jnp.cumsum(doc_lengths[0], dtype=jnp.int32)
    query_matrix = queries[0]
    query_pos = lax.axis_index(BLK) * token_rows + jnp.arange(token_rows, dtype=jnp.int32)
    query_head_rows = query_matrix.reshape(token_rows, KEY_VALUE_HEADS, heads_per_group, HEAD_SIZE)
    query_seg = segment_of(query_pos, doc_ends)
    both_all = gather_blocks(jnp.concatenate([keys[0], values[0]], axis=1))
    keys_all = both_all[:, : KEY_VALUE_HEADS * HEAD_SIZE]
    values_all = both_all[:, KEY_VALUE_HEADS * HEAD_SIZE :]
    start_state = (
        jnp.full((KEY_VALUE_HEADS, heads_per_group, token_rows), NEGATIVE_HUGE, jnp.float32),
        jnp.zeros((KEY_VALUE_HEADS, heads_per_group, token_rows), jnp.float32),
        jnp.zeros((KEY_VALUE_HEADS, heads_per_group, token_rows, HEAD_SIZE), jnp.float32),
    )
    row_max, total, accumulated = attend_keys(
        start_state,
        keys_all,
        values_all,
        query_head_rows,
        query_pos,
        query_seg,
        doc_ends,
    )
    attended_on_shard = (
        jnp.transpose(accumulated / total[..., None], (2, 0, 1, 3))
        .reshape(token_rows, model_width)
        .astype(jnp.bfloat16)
    )
    log_total = row_max + jnp.log(total)
    hidden = (stream[0].astype(jnp.float32) + attended_on_shard.astype(jnp.float32)).astype(
        jnp.bfloat16
    )
    hidden_wide = hidden.astype(jnp.float32)
    inv_rms = lax.rsqrt(jnp.mean(hidden_wide * hidden_wide, axis=-1, keepdims=True) + EPSILON)
    normed = (hidden_wide * inv_rms * norm_gain).astype(jnp.bfloat16)
    logits = jnp.dot(normed, router_weight, preferred_element_type=jnp.float32)
    experts = router_weight.shape[1]
    chosen_ids = expert_ids[0]
    top_count = chosen_ids.shape[1]
    capacity = max(2, 3 * token_rows * top_count // (2 * experts))
    hit_table = (
        chosen_ids[:, :, None] == jnp.arange(experts, dtype=jnp.int32)[None, None, :]
    ).astype(jnp.int32)
    hit_wide = hit_table.astype(jnp.float32)
    chosen = jnp.sum(hit_wide * logits[:, None, :], axis=-1)
    first_gate = jax.nn.sigmoid(chosen[:, 0] - chosen[:, 1])
    gate_pair = jnp.stack([first_gate, 1.0 - first_gate], axis=1)
    flat_hits = hit_table.reshape(token_rows * top_count, experts)
    slot_rank = jnp.sum(
        (jnp.cumsum(flat_hits, axis=0, dtype=jnp.int32) - flat_hits) * flat_hits,
        axis=1,
        dtype=jnp.int32,
    ).reshape(token_rows, top_count)
    slot_index = chosen_ids * capacity + slot_rank
    slot_pick = (
        slot_index[:, :, None] == jnp.arange(experts * capacity, dtype=jnp.int32)[None, None, :]
    ).astype(jnp.float32)
    slot_select = jnp.sum(slot_pick, axis=1).astype(jnp.bfloat16)
    contract_rows = (((0,), (0,)), ((), ()))
    contract_cols = (((1,), (1,)), ((), ()))
    send_grads = lax.dot_general(
        slot_select, out_grad[0], contract_rows, preferred_element_type=jnp.float32
    ).astype(jnp.bfloat16)
    got_grads = to_experts(send_grads, experts)
    send_rows = lax.dot_general(
        slot_select, normed, contract_rows, preferred_element_type=jnp.float32
    ).astype(jnp.bfloat16)
    got_rows = to_experts(send_rows, experts)
    gate_mat = gate_weight[0]
    up_mat = up_weight[0]
    down_mat = down_weight[0]

    grad_inner = lax.dot_general(
        got_grads, down_mat, contract_cols, preferred_element_type=jnp.float32
    )
    pre_gate = jnp.dot(got_rows, gate_mat, preferred_element_type=jnp.float32)
    pre_up = jnp.dot(got_rows, up_mat, preferred_element_type=jnp.float32)
    sigmoid_gate = jax.nn.sigmoid(pre_gate)
    activated = pre_gate * sigmoid_gate
    score_row = jnp.sum((activated * pre_up) * grad_inner, axis=-1).astype(jnp.bfloat16)
    grad_gate = (
        grad_inner * pre_up * sigmoid_gate * (1.0 + pre_gate * (1.0 - sigmoid_gate))
    ).astype(jnp.bfloat16)
    grad_up = (grad_inner * activated).astype(jnp.bfloat16)
    grad_rows = lax.dot_general(
        grad_gate, gate_mat, contract_cols, preferred_element_type=jnp.float32
    )
    grad_rows = grad_rows + lax.dot_general(
        grad_up, up_mat, contract_cols, preferred_element_type=jnp.float32
    )
    back_rows = grad_rows.astype(jnp.bfloat16).reshape(experts, -1, 128)
    back_score = jnp.pad(score_row.reshape(experts, 1, capacity), ((0, 0), (0, 7), (0, 128 - capacity)))
    returned = lax.all_to_all(
        jnp.concatenate([back_rows, back_score], axis=1), GRP_BLK, split_axis=0, concat_axis=0, tiled=True
    )
    return_rows = returned[:, : back_rows.shape[1]].reshape(experts * capacity, model_width)
    return_score = returned[:, back_rows.shape[1], :capacity].reshape(-1).astype(jnp.float32)
    gate_select = jnp.einsum("tks,tk->ts", slot_pick, gate_pair).astype(jnp.bfloat16)
    grad_expert = jnp.dot(gate_select, return_rows, preferred_element_type=jnp.float32)
    token_score = jnp.einsum("tks,s->tk", slot_pick, return_score)
    grad_first = first_gate * (1.0 - first_gate) * (token_score[:, 0] - token_score[:, 1])
    grad_chosen = jnp.stack([grad_first, -grad_first], axis=1)
    d_logits = jnp.sum(hit_wide * grad_chosen[:, :, None], axis=1).astype(jnp.bfloat16)
    d_normed = grad_expert + lax.dot_general(
        d_logits, router_weight, contract_cols, preferred_element_type=jnp.float32
    )
    scaled = norm_gain * d_normed
    stream_wide = (
        out_grad[0].astype(jnp.float32)
        + inv_rms * scaled
        - hidden_wide * inv_rms**3 * jnp.mean(hidden_wide * scaled, axis=-1, keepdims=True)
    )
    residual_gradient = stream_wide.astype(jnp.bfloat16)
    router_parts = lax.dot_general(
        normed, d_logits, contract_rows, preferred_element_type=jnp.float32
    ).astype(jnp.bfloat16)
    router_grad = jnp.sum(
        lax.all_to_all(
            router_parts.reshape(experts, -1, experts), GRP_BLK, split_axis=0, concat_axis=0, tiled=True
        ).astype(jnp.float32),
        axis=0,
    )
    gradient_head_rows = residual_gradient.reshape(
        token_rows, KEY_VALUE_HEADS, heads_per_group, HEAD_SIZE
    )
    attended_head_rows = attended_on_shard.reshape(
        token_rows, KEY_VALUE_HEADS, heads_per_group, HEAD_SIZE
    )
    row_dot = jnp.einsum(
        "tgjd,tgjd->gjt", gradient_head_rows, attended_head_rows, preferred_element_type=jnp.float32
    )
    dq_acc, shard_parts = key_gradients(
        query_head_rows,
        gradient_head_rows,
        log_total,
        row_dot,
        keys_all,
        values_all,
        query_pos,
        query_seg,
        doc_ends,
    )
    summed = scatter_blocks(
        shard_parts.reshape(-1, token_rows, 2 * KEY_VALUE_HEADS * HEAD_SIZE)
    ).reshape(token_rows, 2, KEY_VALUE_HEADS * HEAD_SIZE)
    query_local = dq_acc.reshape(token_rows, model_width).astype(jnp.bfloat16)
    key_gradient_rows = summed[:, 0].astype(jnp.bfloat16)
    value_gradient_rows = summed[:, 1].astype(jnp.bfloat16)
    return (
        query_local[None],
        key_gradient_rows[None],
        value_gradient_rows[None],
        residual_gradient[None],
        router_grad,
    )


def solution(mesh):
    split = Mesh(mesh.devices.reshape(2, 4, 4, 2, 2), ("grp_0", "grp_1", "blk_0", "blk_1", "blk_2"))
    return jax.shard_map(
        per_device,
        mesh=split,
        in_specs=(
            P(GRP, BLK, None),
            P(GRP, BLK, None),
            P(GRP, BLK, None),
            P(GRP, BLK, None),
            P(),
            P(),
            P(GRP_BLK, None, None),
            P(GRP_BLK, None, None),
            P(GRP_BLK, None, None),
            P(GRP, None),
            P(GRP, BLK, None),
            P(GRP, BLK, None),
        ),
        out_specs=(
            P(GRP, BLK, None),
            P(GRP, BLK, None),
            P(GRP, BLK, None),
            P(GRP, BLK, None),
            P(GRP_BLK, None),
        ),
        check_vma=False,
    )
```

```python
import functools
import math

import jax
import jax.numpy as jnp
from jax import lax
from jax.experimental import pallas as pl
from jax.experimental.pallas import tpu as pltpu
from jax.sharding import Mesh
from jax.sharding import PartitionSpec as P

HEAD_SIZE = 128
QUERY_HEADS = 32
KEY_VALUE_HEADS = 2
HEADS_PER_GROUP = QUERY_HEADS // KEY_VALUE_HEADS
BLK = ("blk_0", "blk_1", "blk_2")
GRP_BLK = ("grp_0", "grp_1", "blk_0", "blk_1", "blk_2")
GRP = ("grp_0", "grp_1")
ZX = ("blk_0", "blk_1")
CORE = "blk_2"

NEGATIVE_HUGE = -1e30
EPSILON = 1e-06
SCALE = HEAD_SIZE ** (-0.5)
KEY_BLOCK = 256
OCTET = 8
VMEM_LIMIT = 60 * 1024 * 1024

NT = (((1,), (1,)), ((), ()))
TN = (((0,), (0,)), ((), ()))


def dot32(a, b, dims=(((1,), (0,)), ((), ()))):
    return lax.dot_general(a, b, dims, preferred_element_type=jnp.float32)


def lanes(start, size):
    return pl.ds(pl.multiple_of(start, 128), size)


def order_blocks(mine_ref, theirs_ref, core, kv_scr):
    is_first = jnp.full((128, mine_ref.shape[2]), core, jnp.int32) == 0

    def place(b, _):
        mine = mine_ref[b].astype(jnp.float32)
        theirs = theirs_ref[b].astype(jnp.float32)
        start = pl.multiple_of(b * KEY_BLOCK, KEY_BLOCK)
        kv_scr[pl.ds(start, 128), :] = jnp.where(is_first, mine, theirs).astype(jnp.bfloat16)
        kv_scr[pl.ds(start + 128, 128), :] = jnp.where(is_first, theirs, mine).astype(jnp.bfloat16)
        return 0

    lax.fori_loop(0, mine_ref.shape[0], place, 0)


def attend_kernel(
    meta,
    slots,
    q_ref,
    mine_ref,
    theirs_ref,
    stream_ref,
    gain_ref,
    w_ref,
    linv_ref,
    att_ref,
    hid_ref,
    norm_ref,
    rms_ref,
    send_ref,
    kv_scr,
    vt_scr,
    bias_scr,
    s_scr,
    ot_scr,
    ss_scr,
    rows_scr,
):
    octet = pl.program_id(0)
    group = octet // (HEADS_PER_GROUP // OCTET)
    low, high, core, first_query = meta[0], meta[1], meta[2], meta[3]
    tokens = q_ref.shape[0]
    factor = SCALE * math.log2(math.e)

    @pl.when(octet == 0)
    def _():
        order_blocks(mine_ref, theirs_ref, core, kv_scr)
        ss_scr[...] = jnp.zeros_like(ss_scr)
        send_ref[...] = jnp.zeros_like(send_ref)
        query = first_query + lax.broadcasted_iota(jnp.int32, (KEY_BLOCK, tokens), 1)
        start = jnp.zeros((KEY_BLOCK, tokens), jnp.int32)
        for d in range(4):
            start = jnp.maximum(start, jnp.where(query >= meta[4 + d], meta[4 + d], 0))

        def prepare(kb, _):
            rows = pl.ds(pl.multiple_of(kb * KEY_BLOCK, KEY_BLOCK), KEY_BLOCK)
            vt_scr[kb] = kv_scr[rows, 256:512].T
            key = kb * KEY_BLOCK + lax.broadcasted_iota(jnp.int32, (KEY_BLOCK, tokens), 0)
            seen = (key <= query) & (key >= start)
            bias_scr[kb] = jnp.where(seen, 0.0, NEGATIVE_HUGE)
            return 0

        lax.fori_loop(low, high + 1, prepare, 0)

    pairs = OCTET // 2
    wide = 2 * tokens

    def score(kb, tops):
        rows = pl.ds(pl.multiple_of(kb * KEY_BLOCK, KEY_BLOCK), KEY_BLOCK)
        key_rows = kv_scr[rows, lanes(group * HEAD_SIZE, HEAD_SIZE)]
        bias = bias_scr[kb]
        bias = jnp.concatenate([bias, bias], axis=1)
        new = []
        for p in range(pairs):
            c = 2 * p * HEAD_SIZE
            both = jnp.concatenate(
                [q_ref[:, c : c + HEAD_SIZE], q_ref[:, c + HEAD_SIZE : c + 2 * HEAD_SIZE]], axis=0
            )
            s = dot32(key_rows, both, NT) + bias
            s_scr[kb, :, p * wide : (p + 1) * wide] = s
            new.append(jnp.maximum(tops[p], jnp.max(s.reshape(-1, 8, wide), axis=0)))
        return tuple(new)

    tops = lax.fori_loop(
        low, high + 1, score, tuple(jnp.full((8, wide), NEGATIVE_HUGE, jnp.float32) for _ in range(pairs))
    )
    tops = tuple(jnp.max(t, axis=0, keepdims=True) * factor for t in tops)
    ot_scr[...] = jnp.zeros_like(ot_scr)

    def weigh(kb, sums):
        value_cols = vt_scr[kb, pl.ds(pl.multiple_of(group * HEAD_SIZE, HEAD_SIZE), HEAD_SIZE), :]
        new = []
        for p in range(pairs):
            span = slice(p * wide, (p + 1) * wide)
            w = jnp.exp2(s_scr[kb, :, span] * factor - tops[p])
            new.append(sums[p] + jnp.sum(w.reshape(-1, 8, wide), axis=0))
            low_w = w.astype(jnp.bfloat16)
            w_ref[0, kb, :, span] = low_w
            ot_scr[:, span] += dot32(value_cols, low_w)
        return tuple(new)

    sums = lax.fori_loop(
        low, high + 1, weigh, tuple(jnp.zeros((8, wide), jnp.float32) for _ in range(pairs))
    )
    for p in range(pairs):
        inverse = 1.0 / jnp.sum(sums[p], axis=0, keepdims=True)
        mixed = ot_scr[:, p * wide : (p + 1) * wide] * inverse
        for i in range(2):
            h = 2 * p + i
            linv_ref[h : h + 1, :] = inverse[:, i * tokens : (i + 1) * tokens]
            columns = lanes((octet * OCTET + h) * HEAD_SIZE, HEAD_SIZE)
            att = mixed[:, i * tokens : (i + 1) * tokens].T.astype(jnp.bfloat16)
            att_ref[:, columns] = att
            hid = (stream_ref[:, columns].astype(jnp.float32) + att.astype(jnp.float32)).astype(
                jnp.bfloat16
            )
            hid_ref[:, columns] = hid
            wide_hid = hid.astype(jnp.float32)
            ss_scr[...] += wide_hid * wide_hid

    @pl.when(octet == pl.num_programs(0) - 1)
    def _():
        mean = jnp.sum(ss_scr[...], axis=1, keepdims=True) * (1.0 / (QUERY_HEADS * HEAD_SIZE))
        inv_rms = jnp.broadcast_to(lax.rsqrt(mean + EPSILON), (tokens, HEAD_SIZE))
        rms_ref[...] = inv_rms

        def norm(h, _):
            columns = lanes(h * HEAD_SIZE, HEAD_SIZE)
            n = (hid_ref[:, columns].astype(jnp.float32) * inv_rms * gain_ref[:, columns]).astype(
                jnp.bfloat16
            )
            norm_ref[:, columns] = n
            rows_scr[pl.ds(h, tokens, stride=QUERY_HEADS), :] = n.astype(jnp.float32)
            return 0

        lax.fori_loop(0, QUERY_HEADS, norm, 0, unroll=2)
        scatter_rows(slots, rows_scr, send_ref, tokens)


def scatter_rows(slots, rows_scr, send_ref, tokens):
    def send(t, _):
        row = rows_scr[pl.ds(pl.multiple_of(t * QUERY_HEADS, QUERY_HEADS), QUERY_HEADS), :].astype(
            jnp.bfloat16
        )
        send_ref[slots[2 * t]] = row
        send_ref[slots[2 * t + 1]] = row
        return 0

    lax.fori_loop(0, tokens, send, 0, unroll=8)


def whole(shape, dims=1):
    zero = (0,) * len(shape)
    return pl.BlockSpec(shape, lambda *_: zero)


def attend(meta, slots, queries, mine, theirs, stream, gain, slot_count):
    tokens, width = queries.shape
    octets = QUERY_HEADS // OCTET
    blocks = mine.shape[0]
    span = OCTET * tokens
    bf16, f32 = jnp.bfloat16, jnp.float32
    return pl.pallas_call(
        attend_kernel,
        grid_spec=pltpu.PrefetchScalarGridSpec(
            num_scalar_prefetch=2,
            grid=(octets,),
            in_specs=[
                pl.BlockSpec((tokens, OCTET * HEAD_SIZE), lambda o, *_: (0, o)),
                whole(mine.shape),
                whole(theirs.shape),
                whole(stream.shape),
                whole((1, width)),
            ],
            out_specs=[
                pl.BlockSpec((1, blocks, KEY_BLOCK, span), lambda o, *_: (o, 0, 0, 0)),
                pl.BlockSpec((OCTET, tokens), lambda o, *_: (o, 0)),
                whole((tokens, width)),
                whole((tokens, width)),
                whole((tokens, width)),
                whole((tokens, HEAD_SIZE)),
                whole((slot_count, QUERY_HEADS, HEAD_SIZE)),
            ],
            scratch_shapes=[
                pltpu.VMEM((blocks * KEY_BLOCK, mine.shape[2]), bf16),
                pltpu.VMEM((blocks, mine.shape[2] // 2, KEY_BLOCK), bf16),
                pltpu.VMEM((blocks, KEY_BLOCK, tokens), f32),
                pltpu.VMEM((blocks, KEY_BLOCK, span), f32),
                pltpu.VMEM((HEAD_SIZE, span), f32),
                pltpu.VMEM((tokens, HEAD_SIZE), f32),
                pltpu.VMEM((tokens * QUERY_HEADS, HEAD_SIZE), f32),
            ],
        ),
        out_shape=[
            jax.ShapeDtypeStruct((octets, blocks, KEY_BLOCK, span), bf16),
            jax.ShapeDtypeStruct((QUERY_HEADS, tokens), f32),
            jax.ShapeDtypeStruct((tokens, width), bf16),
            jax.ShapeDtypeStruct((tokens, width), bf16),
            jax.ShapeDtypeStruct((tokens, width), bf16),
            jax.ShapeDtypeStruct((tokens, HEAD_SIZE), f32),
            jax.ShapeDtypeStruct((slot_count, QUERY_HEADS, HEAD_SIZE), bf16),
        ],
        compiler_params=pltpu.CompilerParams(
            dimension_semantics=("arbitrary",), vmem_limit_bytes=VMEM_LIMIT
        ),
        cost_estimate=pl.CostEstimate(
            flops=4 * tokens * width * 1536, bytes_accessed=24 << 20, transcendentals=tokens * 32 * 1536
        ),
        name="attend",
    )(meta, slots, queries, mine, theirs, stream, gain)


def place_kernel(slots, rows_ref, send_ref, rows_scr):
    tokens = rows_ref.shape[0]
    send_ref[...] = jnp.zeros_like(send_ref)

    def turn(h, _):
        rows_scr[pl.ds(h, tokens, stride=QUERY_HEADS), :] = rows_ref[
            :, lanes(h * HEAD_SIZE, HEAD_SIZE)
        ].astype(jnp.float32)
        return 0

    lax.fori_loop(0, QUERY_HEADS, turn, 0, unroll=2)
    scatter_rows(slots, rows_scr, send_ref, tokens)


def place(slots, rows, slot_count):
    tokens, width = rows.shape
    return pl.pallas_call(
        place_kernel,
        grid_spec=pltpu.PrefetchScalarGridSpec(
            num_scalar_prefetch=1,
            grid=(1,),
            in_specs=[whole(rows.shape)],
            out_specs=whole((slot_count, QUERY_HEADS, HEAD_SIZE)),
            scratch_shapes=[pltpu.VMEM((tokens * QUERY_HEADS, HEAD_SIZE), jnp.float32)],
        ),
        out_shape=jax.ShapeDtypeStruct((slot_count, QUERY_HEADS, HEAD_SIZE), jnp.bfloat16),
        compiler_params=pltpu.CompilerParams(vmem_limit_bytes=VMEM_LIMIT),
        cost_estimate=pl.CostEstimate(flops=0, bytes_accessed=4 << 20, transcendentals=0),
        name="place",
    )(slots, rows)


def attend_back_kernel(
    meta,
    q_ref,
    grad_ref,
    att_ref,
    linv_ref,
    mine_ref,
    theirs_ref,
    w_ref,
    dq_ref,
    keep_ref,
    give_ref,
    kv_scr,
    kt_scr,
    q_scr,
    do_scr,
    rd_scr,
    ds_scr,
    dqt_scr,
):
    group, step = pl.program_id(0), pl.program_id(1)
    low, high, core = meta[0], meta[1], meta[2]
    tokens = q_ref.shape[0]
    wide = 2 * tokens
    per_group = HEADS_PER_GROUP * tokens
    f32, bf16 = jnp.float32, jnp.bfloat16

    @pl.when((group == 0) & (step == 0))
    def _():
        order_blocks(mine_ref, theirs_ref, core, kv_scr)
        keep_ref[...] = jnp.zeros_like(keep_ref)
        give_ref[...] = jnp.zeros_like(give_ref)

        def prepare(kb, _):
            rows = pl.ds(pl.multiple_of(kb * KEY_BLOCK, KEY_BLOCK), KEY_BLOCK)
            kt_scr[kb] = kv_scr[rows, 0:256].T
            return 0

        lax.fori_loop(low, high + 1, prepare, 0)
        inverse = jnp.concatenate(
            [linv_ref[...], jnp.zeros((128 - QUERY_HEADS, tokens), f32)], axis=0
        ).T
        ones = jnp.ones((8, HEAD_SIZE), bf16)
        for h in range(QUERY_HEADS):
            columns = slice(h * HEAD_SIZE, (h + 1) * HEAD_SIZE)
            rows = slice(h * tokens, (h + 1) * tokens)
            q_scr[rows, :] = q_ref[:, columns]
            scaled = (grad_ref[:, columns].astype(f32) * inverse[:, h : h + 1]).astype(bf16)
            do_scr[rows, :] = scaled
            product = scaled.astype(f32) * att_ref[:, columns].astype(f32)
            head = product.astype(bf16)
            tail = (product - head.astype(f32)).astype(bf16)
            rd_scr[:, rows] = dot32(ones, head, NT) + dot32(ones, tail, NT)

    @pl.when(step == 0)
    def _():
        dqt_scr[...] = jnp.zeros_like(dqt_scr)

    @pl.when(low + step <= high)
    def _():
        kb = low + step
        rows = pl.ds(pl.multiple_of(kb * KEY_BLOCK, KEY_BLOCK), KEY_BLOCK)
        value_rows = kv_scr[rows, lanes(256 + group * HEAD_SIZE, HEAD_SIZE)]
        key_cols = kt_scr[kb, pl.ds(pl.multiple_of(group * HEAD_SIZE, HEAD_SIZE), HEAD_SIZE), :]
        for p in range(HEADS_PER_GROUP // 2):
            here = pl.multiple_of(group * per_group + p * wide, wide)
            grads = do_scr[pl.ds(here, wide), :]
            dp = dot32(value_rows, grads, NT)
            per_octet = OCTET // 2
            c = (p % per_octet) * wide
            w = w_ref[p // per_octet, 0, :, c : c + wide].astype(f32)
            ds = (w * (dp - rd_scr[0:1, pl.ds(here, wide)])).astype(bf16)
            ds_scr[:, p * wide : (p + 1) * wide] = ds
            dqt_scr[:, p * wide : (p + 1) * wide] += dot32(key_cols, ds)
        base = pl.multiple_of(group * per_group, per_group)
        half = per_group // 2
        dv = dot32(w_ref[0, 0], do_scr[pl.ds(base, half), :]) + dot32(
            w_ref[1, 0], do_scr[pl.ds(base + half, half), :]
        )
        dk = dot32(ds_scr[...], q_scr[pl.ds(base, per_group), :]) * SCALE
        is_first = jnp.full((128, HEAD_SIZE), core, jnp.int32) == 0
        for part, column in ((dk, 0), (dv, 256)):
            columns = lanes(column + group * HEAD_SIZE, HEAD_SIZE)
            keep_ref[kb, :, columns] = jnp.where(is_first, part[:128], part[128:]).astype(bf16)
            give_ref[kb, :, columns] = jnp.where(is_first, part[128:], part[:128]).astype(bf16)

    @pl.when(step == pl.num_programs(1) - 1)
    def _():
        for h in range(HEADS_PER_GROUP):
            dq = dqt_scr[:, h * tokens : (h + 1) * tokens] * SCALE
            dq_ref[:, lanes(group * per_group + h * HEAD_SIZE, HEAD_SIZE)] = dq.T.astype(bf16)


def attend_back(meta, queries, grads, attended, linv, mine, theirs, weights):
    tokens, width = queries.shape
    blocks = mine.shape[0]
    bf16, f32 = jnp.bfloat16, jnp.float32
    per_group = HEADS_PER_GROUP * tokens
    octets_per_group = HEADS_PER_GROUP // OCTET
    span = OCTET * tokens
    return pl.pallas_call(
        attend_back_kernel,
        grid_spec=pltpu.PrefetchScalarGridSpec(
            num_scalar_prefetch=1,
            grid=(KEY_VALUE_HEADS, blocks),
            in_specs=[
                whole(queries.shape),
                whole(grads.shape),
                whole(attended.shape),
                whole(linv.shape),
                whole(mine.shape),
                whole(theirs.shape),
                pl.BlockSpec(
                    (octets_per_group, 1, KEY_BLOCK, span),
                    lambda g, j, meta: (g, jnp.minimum(meta[0] + j, meta[1]), 0, 0),
                ),
            ],
            out_specs=[whole((tokens, width)), whole(mine.shape), whole(mine.shape)],
            scratch_shapes=[
                pltpu.VMEM((blocks * KEY_BLOCK, mine.shape[2]), bf16),
                pltpu.VMEM((blocks, mine.shape[2] // 2, KEY_BLOCK), bf16),
                pltpu.VMEM((QUERY_HEADS * tokens, HEAD_SIZE), bf16),
                pltpu.VMEM((QUERY_HEADS * tokens, HEAD_SIZE), bf16),
                pltpu.VMEM((8, QUERY_HEADS * tokens), f32),
                pltpu.VMEM((KEY_BLOCK, per_group), bf16),
                pltpu.VMEM((HEAD_SIZE, per_group), f32),
            ],
        ),
        out_shape=[
            jax.ShapeDtypeStruct((tokens, width), bf16),
            jax.ShapeDtypeStruct(mine.shape, bf16),
            jax.ShapeDtypeStruct(mine.shape, bf16),
        ],
        compiler_params=pltpu.CompilerParams(
            dimension_semantics=("arbitrary", "arbitrary"), vmem_limit_bytes=VMEM_LIMIT
        ),
        cost_estimate=pl.CostEstimate(
            flops=8 * tokens * width * 1536, bytes_accessed=20 << 20, transcendentals=0
        ),
        name="attend_back",
    )(meta, queries, grads, attended, linv, mine, theirs, weights)


def expert_kernel(
    rows_ref,
    inner_grad_ref,
    gate_hbm,
    up_hbm,
    out_ref,
    gate_scr,
    up_scr,
    turn_scr,
    x_scr,
    da_scr,
    db_scr,
    score_scr,
    sems,
):
    f32, bf16 = jnp.float32, jnp.bfloat16
    peers, per_peer = rows_ref.shape[0], rows_ref.shape[1]
    count = x_scr.shape[0]
    hidden_units = gate_scr.shape[1]
    capacity = count // peers
    loads = [
        pltpu.make_async_copy(gate_hbm, gate_scr, sems.at[0]),
        pltpu.make_async_copy(up_hbm, up_scr, sems.at[1]),
    ]
    for load in loads:
        load.start()

    def widen(i, _):
        rows = pl.ds(pl.multiple_of(i * per_peer, per_peer), per_peer)
        turn_scr[rows, :] = rows_ref[i].astype(f32)
        return 0

    lax.fori_loop(0, peers, widen, 0, unroll=2)

    def turn(j, _):
        x_scr[:, lanes(j * HEAD_SIZE, HEAD_SIZE)] = turn_scr[
            pl.ds(j, count, stride=QUERY_HEADS), :
        ].astype(bf16)
        return 0

    lax.fori_loop(0, QUERY_HEADS, turn, 0, unroll=2)
    for load in loads:
        load.wait()
    score_scr[...] = jnp.zeros_like(score_scr)
    span = 256

    def hidden_part(n, _):
        columns = lanes(n * span, span)
        a = dot32(x_scr[...], gate_scr[:, columns])
        b = dot32(x_scr[...], up_scr[:, columns])
        u = inner_grad_ref[:, columns]
        sig = 1.0 / (1.0 + jnp.exp(-a))
        act = a * sig
        product = u * b
        scores = jnp.sum(product * act, axis=1, keepdims=True)
        score_scr[0:count, :] += jnp.broadcast_to(scores, (count, HEAD_SIZE))
        da_scr[:, columns] = (product * sig * (1.0 + a * (1.0 - sig))).astype(bf16)
        db_scr[:, columns] = (u * act).astype(bf16)
        return 0

    lax.fori_loop(0, hidden_units // span, hidden_part, 0)

    def grad_part(j, _):
        rows = pl.ds(pl.multiple_of(j * span, span), span)
        d = dot32(da_scr[...], gate_scr[rows, :], NT) + dot32(db_scr[...], up_scr[rows, :], NT)
        turn_scr[pl.ds(2 * j, count, stride=QUERY_HEADS), :] = d[:, :HEAD_SIZE]
        turn_scr[pl.ds(2 * j + 1, count, stride=QUERY_HEADS), :] = d[:, HEAD_SIZE:]
        return 0

    lax.fori_loop(0, QUERY_HEADS // 2, grad_part, 0)

    def narrow(i, _):
        rows = pl.ds(pl.multiple_of(i * per_peer, per_peer), per_peer)
        out_ref[i, 0:per_peer, :] = turn_scr[rows, :].astype(bf16)
        out_ref[i, per_peer : per_peer + 8, :] = score_scr[pl.ds(capacity * i, 8), :].astype(bf16)
        return 0

    lax.fori_loop(0, peers, narrow, 0, unroll=2)


def expert(rows, inner_grad, gate_mat, up_mat):
    peers, per_peer, _ = rows.shape
    count = inner_grad.shape[0]
    width, hidden_units = gate_mat.shape
    f32, bf16 = jnp.float32, jnp.bfloat16
    return pl.pallas_call(
        expert_kernel,
        in_specs=[
            pl.BlockSpec(memory_space=pltpu.VMEM),
            pl.BlockSpec(memory_space=pltpu.VMEM),
            pl.BlockSpec(memory_space=pltpu.HBM),
            pl.BlockSpec(memory_space=pltpu.HBM),
        ],
        out_specs=pl.BlockSpec(memory_space=pltpu.VMEM),
        scratch_shapes=[
            pltpu.VMEM((width, hidden_units), bf16),
            pltpu.VMEM((width, hidden_units), bf16),
            pltpu.VMEM((count * QUERY_HEADS, HEAD_SIZE), f32),
            pltpu.VMEM((count, width), bf16),
            pltpu.VMEM((count, hidden_units), bf16),
            pltpu.VMEM((count, hidden_units), bf16),
            pltpu.VMEM((count + 16, HEAD_SIZE), f32),
            pltpu.SemaphoreType.DMA((2,)),
        ],
        out_shape=jax.ShapeDtypeStruct((peers, per_peer + 8, HEAD_SIZE), bf16),
        compiler_params=pltpu.CompilerParams(vmem_limit_bytes=VMEM_LIMIT),
        cost_estimate=pl.CostEstimate(
            flops=8 * count * width * hidden_units, bytes_accessed=20 << 20, transcendentals=count * hidden_units
        ),
        name="expert",
    )(rows, inner_grad, gate_mat, up_mat)


def combine_kernel(
    slots,
    gates_smem,
    back_ref,
    gates_ref,
    ids_ref,
    hid_ref,
    norm_ref,
    rms_ref,
    og_ref,
    gain_ref,
    router_ref,
    res_ref,
    part_ref,
    rows_scr,
    score_scr,
    dn_scr,
    acc_scr,
):
    f32, bf16 = jnp.float32, jnp.bfloat16
    tokens = hid_ref.shape[0]
    capacity = 3
    per_peer = capacity * QUERY_HEADS

    def pick(t, _):
        total = None
        scores = []
        for k in range(2):
            slot = slots[2 * t + k]
            e = slot // capacity
            c = slot - e * capacity
            start = pl.multiple_of(c * QUERY_HEADS, QUERY_HEADS)
            row = back_ref[e, pl.ds(start, QUERY_HEADS), :].astype(f32) * gates_smem[2 * t + k]
            total = row if total is None else total + row
            tail = back_ref[e, per_peer : per_peer + 8, :].astype(f32)
            which = lax.broadcasted_iota(jnp.int32, tail.shape, 0) == c
            scores.append(jnp.sum(jnp.where(which, tail, 0.0), axis=0, keepdims=True))
        rows_scr[pl.ds(pl.multiple_of(t * QUERY_HEADS, QUERY_HEADS), QUERY_HEADS), :] = total
        score_scr[pl.ds(t, 1), :] = scores[0] - scores[1]
        return 0

    lax.fori_loop(0, tokens, pick, 0, unroll=8)
    first = gates_ref[:, 0:1]
    value = first * (1.0 - first) * score_scr[...]
    lane = lax.broadcasted_iota(jnp.int32, (tokens, HEAD_SIZE), 1)
    d_logits = jnp.where(lane == ids_ref[:, 0:1], value, 0.0) - jnp.where(
        lane == ids_ref[:, 1:2], value, 0.0
    )
    d_logits = d_logits.astype(bf16)
    acc_scr[...] = jnp.zeros_like(acc_scr)

    def gather(h, _):
        columns = lanes(h * HEAD_SIZE, HEAD_SIZE)
        rows = pl.ds(pl.multiple_of(h * HEAD_SIZE, HEAD_SIZE), HEAD_SIZE)
        dn = rows_scr[pl.ds(h, tokens, stride=QUERY_HEADS), :] + dot32(
            d_logits, router_ref[rows, :], NT
        )
        scaled = dn * gain_ref[:, columns]
        dn_scr[:, columns] = scaled
        acc_scr[...] += hid_ref[:, columns].astype(f32) * scaled
        part_ref[rows, :] = dot32(norm_ref[:, columns], d_logits, TN).astype(bf16)
        return 0

    lax.fori_loop(0, QUERY_HEADS, gather, 0, unroll=2)
    r = rms_ref[...]
    mean = jnp.sum(acc_scr[...], axis=1, keepdims=True) * (1.0 / (QUERY_HEADS * HEAD_SIZE))
    pull = r * r * r * mean

    def finish(h, _):
        columns = lanes(h * HEAD_SIZE, HEAD_SIZE)
        res = og_ref[:, columns].astype(f32) + r * dn_scr[:, columns] - hid_ref[:, columns].astype(f32) * pull
        res_ref[:, columns] = res.astype(bf16)
        return 0

    lax.fori_loop(0, QUERY_HEADS, finish, 0, unroll=2)


def combine(slots, gates, ids, back, hidden, normed, inv_rms, out_grad, gain, router):
    tokens, width = hidden.shape
    experts = router.shape[1]
    f32, bf16 = jnp.float32, jnp.bfloat16
    return pl.pallas_call(
        combine_kernel,
        grid_spec=pltpu.PrefetchScalarGridSpec(
            num_scalar_prefetch=2,
            grid=(1,),
            in_specs=[
                whole(back.shape),
                whole(gates.shape),
                whole(ids.shape),
                whole(hidden.shape),
                whole(normed.shape),
                whole(inv_rms.shape),
                whole(out_grad.shape),
                whole((1, width)),
                whole(router.shape),
            ],
            out_specs=[whole((tokens, width)), whole((width, experts))],
            scratch_shapes=[
                pltpu.VMEM((tokens * QUERY_HEADS, HEAD_SIZE), f32),
                pltpu.VMEM((tokens, HEAD_SIZE), f32),
                pltpu.VMEM((tokens, width), f32),
                pltpu.VMEM((tokens, HEAD_SIZE), f32),
            ],
        ),
        out_shape=[
            jax.ShapeDtypeStruct((tokens, width), bf16),
            jax.ShapeDtypeStruct((width, experts), bf16),
        ],
        compiler_params=pltpu.CompilerParams(vmem_limit_bytes=VMEM_LIMIT),
        cost_estimate=pl.CostEstimate(
            flops=4 * tokens * width * experts, bytes_accessed=9 << 20, transcendentals=0
        ),
        name="combine",
    )(slots, gates.reshape(-1), back, gates, ids, hidden, normed, inv_rms, out_grad, gain, router)


def swap_cores(array):
    return lax.ppermute(array, CORE, [(0, 1), (1, 0)])


def exchange(array, axes):
    return lax.all_to_all(array, axes, split_axis=0, concat_axis=0, tiled=True)


def per_device(
    queries,
    keys,
    values,
    stream,
    norm_gain,
    router_weight,
    gate_weight,
    up_weight,
    down_weight,
    doc_lengths,
    expert_ids,
    out_grad,
):
    token_rows = queries.shape[1]
    model_width = queries.shape[2]
    chips = lax.axis_size("blk_0") * lax.axis_size("blk_1")
    core = lax.axis_index(CORE)
    both = jnp.concatenate([keys[0], values[0]], axis=1)
    mine = exchange(jnp.broadcast_to(both[None], (chips, *both.shape)), ZX)
    theirs = swap_cores(mine)

    doc_ends = jnp.cumsum(doc_lengths[0], dtype=jnp.int32)
    first_query = lax.axis_index(BLK) * token_rows
    first_start = jnp.max(jnp.where(doc_ends <= first_query, doc_ends, 0))
    meta = jnp.concatenate(
        [
            jnp.stack(
                [
                    first_start // KEY_BLOCK,
                    (first_query + token_rows - 1) // KEY_BLOCK,
                    core,
                    first_query,
                ]
            ).astype(jnp.int32),
            doc_ends,
        ]
    )
    experts = router_weight.shape[1]
    chosen_ids = expert_ids[0]
    top_count = chosen_ids.shape[1]
    capacity = max(2, 3 * token_rows * top_count // (2 * experts))
    flat_ids = chosen_ids.reshape(-1)
    same = flat_ids[:, None] == flat_ids[None, :]
    order = jnp.arange(flat_ids.shape[0], dtype=jnp.int32)
    slot_rank = jnp.sum((same & (order[None, :] < order[:, None])).astype(jnp.int32), axis=1, dtype=jnp.int32)
    slots = flat_ids * capacity + slot_rank
    slot_count = experts * capacity

    send_grads = place(slots, out_grad[0], slot_count)
    got_grads = exchange(send_grads.reshape(experts, -1, HEAD_SIZE), GRP_BLK)

    weights, linv, attended, hidden, normed, inv_rms, send_rows = attend(
        meta, slots, queries[0], mine, theirs, stream[0], norm_gain[None], slot_count
    )
    got_rows = exchange(send_rows.reshape(experts, -1, HEAD_SIZE), GRP_BLK)

    logits = jnp.dot(normed, router_weight, preferred_element_type=jnp.float32)
    hits = chosen_ids[:, :, None] == jnp.arange(experts, dtype=jnp.int32)[None, None, :]
    chosen = jnp.sum(jnp.where(hits, logits[:, None, :], 0.0), axis=-1)
    first_gate = jax.nn.sigmoid(chosen[:, 0] - chosen[:, 1])
    gates = jnp.stack([first_gate, 1.0 - first_gate], axis=1)

    inner_grad = dot32(got_grads.reshape(slot_count, model_width), down_weight[0], NT)
    back = exchange(expert(got_rows, inner_grad, gate_weight[0], up_weight[0]), GRP_BLK)
    residual_gradient, router_parts = combine(
        slots, gates, chosen_ids, back, hidden, normed, inv_rms, out_grad[0], norm_gain[None], router_weight
    )
    query_grad, keep, give = attend_back(
        meta, queries[0], residual_gradient, attended, linv, mine, theirs, weights
    )
    pair_sum = (keep.astype(jnp.float32) + swap_cores(give).astype(jnp.float32)).astype(jnp.bfloat16)
    summed = jnp.sum(exchange(pair_sum, ZX).astype(jnp.float32), axis=0).astype(jnp.bfloat16)
    got_parts = exchange(router_parts.reshape(experts, -1, experts), GRP_BLK)
    router_grad = jnp.sum(got_parts.astype(jnp.float32), axis=0)
    half = KEY_VALUE_HEADS * HEAD_SIZE
    return (
        query_grad[None],
        summed[None, :, :half],
        summed[None, :, half:],
        residual_gradient[None],
        router_grad,
    )


def solution(mesh):
    split = Mesh(mesh.devices.reshape(2, 4, 4, 2, 2), ("grp_0", "grp_1", "blk_0", "blk_1", "blk_2"))
    return jax.shard_map(
        per_device,
        mesh=split,
        in_specs=(
            P(GRP, BLK, None),
            P(GRP, BLK, None),
            P(GRP, BLK, None),
            P(GRP, BLK, None),
            P(),
            P(),
            P(GRP_BLK, None, None),
            P(GRP_BLK, None, None),
            P(GRP_BLK, None, None),
            P(GRP, None),
            P(GRP, BLK, None),
            P(GRP, BLK, None),
        ),
        out_specs=(
            P(GRP, BLK, None),
            P(GRP, BLK, None),
            P(GRP, BLK, None),
            P(GRP, BLK, None),
            P(GRP_BLK, None),
        ),
        check_vma=False,
    )
```

```python
import math

import jax
import jax.numpy as jnp
from jax import lax
from jax.experimental import pallas as pl
from jax.experimental.pallas import tpu as pltpu
from jax.sharding import Mesh
from jax.sharding import PartitionSpec as P


HEAD_SIZE = 128
QUERY_HEADS = 32
KEY_VALUE_HEADS = 2
HEADS_PER_GROUP = QUERY_HEADS // KEY_VALUE_HEADS
BLK = ("blk_0", "blk_1", "blk_2")
GRP_BLK = ("grp_0", "grp_1", "blk_0", "blk_1", "blk_2")
GRP = ("grp_0", "grp_1")
ZX = ("blk_0", "blk_1")
CORE = "blk_2"

NEGATIVE_HUGE = -1e30
EPSILON = 1e-06
SCALE = HEAD_SIZE ** (-0.5)
KEY_BLOCK = 256
OCTET = 8
VMEM_LIMIT = 60 * 1024 * 1024
PITCH = QUERY_HEADS + 1

NT = (((1,), (1,)), ((), ()))
TN = (((0,), (0,)), ((), ()))


def dot32(a, b, dims=(((1,), (0,)), ((), ()))):
    return lax.dot_general(a, b, dims, preferred_element_type=jnp.float32)


def lanes(start, size):
    return pl.ds(pl.multiple_of(start, 128), size)


def order_blocks(mine_ref, theirs_ref, core, kv_scr):
    is_first = jnp.full((128, mine_ref.shape[2]), core, jnp.int32) == 0

    def place(b, _):
        mine = mine_ref[b].astype(jnp.float32)
        theirs = theirs_ref[b].astype(jnp.float32)
        start = pl.multiple_of(b * KEY_BLOCK, KEY_BLOCK)
        kv_scr[pl.ds(start, 128), :] = jnp.where(is_first, mine, theirs).astype(jnp.bfloat16)
        kv_scr[pl.ds(start + 128, 128), :] = jnp.where(is_first, theirs, mine).astype(jnp.bfloat16)
        return 0

    lax.fori_loop(0, mine_ref.shape[0], place, 0)


def attend_kernel(
    meta,
    slots,
    q_ref,
    mine_ref,
    theirs_ref,
    stream_ref,
    gain_ref,
    w_ref,
    linv_ref,
    att_ref,
    hid_ref,
    norm_ref,
    rms_ref,
    send_ref,
    kv_scr,
    vt_scr,
    bias_scr,
    s_scr,
    ot_scr,
    ss_scr,
    rows_scr,
):
    octet = pl.program_id(0)
    group = octet // (HEADS_PER_GROUP // OCTET)
    low, high, core, first_query = meta[0], meta[1], meta[2], meta[3]
    tokens = q_ref.shape[0]
    factor = SCALE * math.log2(math.e)

    @pl.when(octet == 0)
    def _():
        order_blocks(mine_ref, theirs_ref, core, kv_scr)
        ss_scr[...] = jnp.zeros_like(ss_scr)
        query = first_query + lax.broadcasted_iota(jnp.int32, (KEY_BLOCK, tokens), 1)
        start = jnp.zeros((KEY_BLOCK, tokens), jnp.int32)
        for d in range(4):
            start = jnp.maximum(start, jnp.where(query >= meta[4 + d], meta[4 + d], 0))

        def prepare(kb, _):
            rows = pl.ds(pl.multiple_of(kb * KEY_BLOCK, KEY_BLOCK), KEY_BLOCK)
            vt_scr[kb] = kv_scr[rows, 256:512].T
            key = kb * KEY_BLOCK + lax.broadcasted_iota(jnp.int32, (KEY_BLOCK, tokens), 0)
            seen = (key <= query) & (key >= start)
            bias_scr[kb] = jnp.where(seen, 0.0, NEGATIVE_HUGE)
            return 0

        lax.fori_loop(low, high + 1, prepare, 0)

    pairs = OCTET // 2
    wide = 2 * tokens

    def score(kb, tops):
        rows = pl.ds(pl.multiple_of(kb * KEY_BLOCK, KEY_BLOCK), KEY_BLOCK)
        key_rows = kv_scr[rows, lanes(group * HEAD_SIZE, HEAD_SIZE)]
        bias = bias_scr[kb]
        bias = jnp.concatenate([bias, bias], axis=1)
        new = []
        for p in range(pairs):
            c = 2 * p * HEAD_SIZE
            both = jnp.concatenate(
                [q_ref[:, c : c + HEAD_SIZE], q_ref[:, c + HEAD_SIZE : c + 2 * HEAD_SIZE]], axis=0
            )
            s = dot32(key_rows, both, NT) + bias
            s_scr[kb, :, p * wide : (p + 1) * wide] = s
            new.append(jnp.maximum(tops[p], jnp.max(s.reshape(-1, 8, wide), axis=0)))
        return tuple(new)

    tops = lax.fori_loop(
        low, high + 1, score, tuple(jnp.full((8, wide), NEGATIVE_HUGE, jnp.float32) for _ in range(pairs))
    )
    tops = tuple(jnp.max(t, axis=0, keepdims=True) * factor for t in tops)
    ot_scr[...] = jnp.zeros_like(ot_scr)

    def weigh(kb, sums):
        value_cols = vt_scr[kb, pl.ds(pl.multiple_of(group * HEAD_SIZE, HEAD_SIZE), HEAD_SIZE), :]
        new = []
        for p in range(pairs):
            span = slice(p * wide, (p + 1) * wide)
            w = jnp.exp2(s_scr[kb, :, span] * factor - tops[p])
            new.append(sums[p] + jnp.sum(w.reshape(-1, 8, wide), axis=0))
            low_w = w.astype(jnp.bfloat16)
            w_ref[0, kb, :, span] = low_w
            ot_scr[:, span] += dot32(value_cols, low_w)
        return tuple(new)

    sums = lax.fori_loop(
        low, high + 1, weigh, tuple(jnp.zeros((8, wide), jnp.float32) for _ in range(pairs))
    )
    for p in range(pairs):
        inverse = 1.0 / jnp.sum(sums[p], axis=0, keepdims=True)
        mixed = ot_scr[:, p * wide : (p + 1) * wide] * inverse
        for i in range(2):
            h = 2 * p + i
            linv_ref[h : h + 1, :] = inverse[:, i * tokens : (i + 1) * tokens]
            columns = lanes((octet * OCTET + h) * HEAD_SIZE, HEAD_SIZE)
            att = mixed[:, i * tokens : (i + 1) * tokens].T.astype(jnp.bfloat16)
            att_ref[:, columns] = att
            hid = (stream_ref[:, columns].astype(jnp.float32) + att.astype(jnp.float32)).astype(
                jnp.bfloat16
            )
            hid_ref[:, columns] = hid
            wide_hid = hid.astype(jnp.float32)
            ss_scr[...] += wide_hid * wide_hid

    @pl.when(octet == pl.num_programs(0) - 1)
    def _():
        mean = jnp.sum(ss_scr[...], axis=1, keepdims=True) * (1.0 / (QUERY_HEADS * HEAD_SIZE))
        inv_rms = jnp.broadcast_to(lax.rsqrt(mean + EPSILON), (tokens, HEAD_SIZE))
        rms_ref[...] = inv_rms

        def norm(h, _):
            columns = lanes(h * HEAD_SIZE, HEAD_SIZE)
            n = (hid_ref[:, columns].astype(jnp.float32) * inv_rms * gain_ref[:, columns]).astype(
                jnp.bfloat16
            )
            norm_ref[:, columns] = n
            rows_scr[pl.ds(h, tokens, stride=PITCH), :] = n.astype(jnp.float32)
            return 0

        lax.fori_loop(0, QUERY_HEADS, norm, 0, unroll=2)
        scatter_rows(slots, rows_scr, send_ref, tokens)


def scatter_rows(slots, rows_scr, send_ref, tokens):
    def send(t, _):
        row = rows_scr[pl.ds(t * PITCH, QUERY_HEADS), :].astype(jnp.bfloat16)
        send_ref[slots[2 * t]] = row
        send_ref[slots[2 * t + 1]] = row
        return 0

    lax.fori_loop(0, tokens, send, 0, unroll=8)


def whole(shape):
    zero = (0,) * len(shape)
    return pl.BlockSpec(shape, lambda *_: zero)


def attend(meta, slots, queries, mine, theirs, stream, gain, slot_count):
    tokens, width = queries.shape
    octets = QUERY_HEADS // OCTET
    blocks = mine.shape[0]
    span = OCTET * tokens
    bf16, f32 = jnp.bfloat16, jnp.float32
    return pl.pallas_call(
        attend_kernel,
        grid_spec=pltpu.PrefetchScalarGridSpec(
            num_scalar_prefetch=2,
            grid=(octets,),
            in_specs=[
                pl.BlockSpec((tokens, OCTET * HEAD_SIZE), lambda o, *_: (0, o)),
                whole(mine.shape),
                whole(theirs.shape),
                whole(stream.shape),
                whole((1, width)),
            ],
            out_specs=[
                pl.BlockSpec((1, blocks, KEY_BLOCK, span), lambda o, *_: (o, 0, 0, 0)),
                pl.BlockSpec((OCTET, tokens), lambda o, *_: (o, 0)),
                whole((tokens, width)),
                whole((tokens, width)),
                whole((tokens, width)),
                whole((tokens, HEAD_SIZE)),
                whole((slot_count, QUERY_HEADS, HEAD_SIZE)),
            ],
            scratch_shapes=[
                pltpu.VMEM((blocks * KEY_BLOCK, mine.shape[2]), bf16),
                pltpu.VMEM((blocks, mine.shape[2] // 2, KEY_BLOCK), bf16),
                pltpu.VMEM((blocks, KEY_BLOCK, tokens), f32),
                pltpu.VMEM((blocks, KEY_BLOCK, span), f32),
                pltpu.VMEM((HEAD_SIZE, span), f32),
                pltpu.VMEM((tokens, HEAD_SIZE), f32),
                pltpu.VMEM((tokens * PITCH, HEAD_SIZE), f32),
            ],
        ),
        out_shape=[
            jax.ShapeDtypeStruct((octets, blocks, KEY_BLOCK, span), bf16),
            jax.ShapeDtypeStruct((QUERY_HEADS, tokens), f32),
            jax.ShapeDtypeStruct((tokens, width), bf16),
            jax.ShapeDtypeStruct((tokens, width), bf16),
            jax.ShapeDtypeStruct((tokens, width), bf16),
            jax.ShapeDtypeStruct((tokens, HEAD_SIZE), f32),
            jax.ShapeDtypeStruct((slot_count, QUERY_HEADS, HEAD_SIZE), bf16),
        ],
        compiler_params=pltpu.CompilerParams(
            dimension_semantics=("arbitrary",), vmem_limit_bytes=VMEM_LIMIT
        ),
        cost_estimate=pl.CostEstimate(
            flops=4 * tokens * width * 1536, bytes_accessed=24 << 20, transcendentals=tokens * 32 * 1536
        ),
        name="attend",
    )(meta, slots, queries, mine, theirs, stream, gain)


def place_kernel(slots, rows_ref, send_ref, rows_scr):
    tokens = rows_ref.shape[0]

    def turn(h, _):
        rows_scr[pl.ds(h, tokens, stride=PITCH), :] = rows_ref[
            :, lanes(h * HEAD_SIZE, HEAD_SIZE)
        ].astype(jnp.float32)
        return 0

    lax.fori_loop(0, QUERY_HEADS, turn, 0, unroll=2)
    scatter_rows(slots, rows_scr, send_ref, tokens)


def place(slots, rows, slot_count):
    tokens, _ = rows.shape
    return pl.pallas_call(
        place_kernel,
        grid_spec=pltpu.PrefetchScalarGridSpec(
            num_scalar_prefetch=1,
            grid=(1,),
            in_specs=[whole(rows.shape)],
            out_specs=whole((slot_count, QUERY_HEADS, HEAD_SIZE)),
            scratch_shapes=[pltpu.VMEM((tokens * PITCH, HEAD_SIZE), jnp.float32)],
        ),
        out_shape=jax.ShapeDtypeStruct((slot_count, QUERY_HEADS, HEAD_SIZE), jnp.bfloat16),
        compiler_params=pltpu.CompilerParams(vmem_limit_bytes=VMEM_LIMIT),
        cost_estimate=pl.CostEstimate(flops=0, bytes_accessed=4 << 20, transcendentals=0),
        name="place",
    )(slots, rows)


def attend_back_kernel(
    meta,
    q_ref,
    grad_ref,
    att_ref,
    linv_ref,
    mine_ref,
    theirs_ref,
    w_ref,
    dq_ref,
    keep_ref,
    give_ref,
    kv_scr,
    kt_scr,
    q_scr,
    do_scr,
    rd_scr,
    ds_scr,
    dqt_scr,
):
    group, step = pl.program_id(0), pl.program_id(1)
    low, high, core = meta[0], meta[1], meta[2]
    tokens = q_ref.shape[0]
    wide = 2 * tokens
    per_group = HEADS_PER_GROUP * tokens
    f32, bf16 = jnp.float32, jnp.bfloat16

    @pl.when((group == 0) & (step == 0))
    def _():
        order_blocks(mine_ref, theirs_ref, core, kv_scr)
        keep_ref[...] = jnp.zeros_like(keep_ref)
        give_ref[...] = jnp.zeros_like(give_ref)

        def prepare(kb, _):
            rows = pl.ds(pl.multiple_of(kb * KEY_BLOCK, KEY_BLOCK), KEY_BLOCK)
            kt_scr[kb] = kv_scr[rows, 0:256].T
            return 0

        lax.fori_loop(low, high + 1, prepare, 0)
        inverse = jnp.concatenate(
            [linv_ref[...], jnp.zeros((128 - QUERY_HEADS, tokens), f32)], axis=0
        ).T
        ones = jnp.ones((8, HEAD_SIZE), bf16)
        for h in range(QUERY_HEADS):
            columns = slice(h * HEAD_SIZE, (h + 1) * HEAD_SIZE)
            rows = slice(h * tokens, (h + 1) * tokens)
            q_scr[rows, :] = q_ref[:, columns]
            scaled = (grad_ref[:, columns].astype(f32) * inverse[:, h : h + 1]).astype(bf16)
            do_scr[rows, :] = scaled
            product = scaled.astype(f32) * att_ref[:, columns].astype(f32)
            head = product.astype(bf16)
            tail = (product - head.astype(f32)).astype(bf16)
            rd_scr[:, rows] = dot32(ones, head, NT) + dot32(ones, tail, NT)

    @pl.when(step == 0)
    def _():
        dqt_scr[...] = jnp.zeros_like(dqt_scr)

    @pl.when(low + step <= high)
    def _():
        kb = low + step
        rows = pl.ds(pl.multiple_of(kb * KEY_BLOCK, KEY_BLOCK), KEY_BLOCK)
        value_rows = kv_scr[rows, lanes(256 + group * HEAD_SIZE, HEAD_SIZE)]
        key_cols = kt_scr[kb, pl.ds(pl.multiple_of(group * HEAD_SIZE, HEAD_SIZE), HEAD_SIZE), :]
        for p in range(HEADS_PER_GROUP // 2):
            here = pl.multiple_of(group * per_group + p * wide, wide)
            grads = do_scr[pl.ds(here, wide), :]
            dp = dot32(value_rows, grads, NT)
            per_octet = OCTET // 2
            c = (p % per_octet) * wide
            w = w_ref[p // per_octet, 0, :, c : c + wide].astype(f32)
            ds = (w * (dp - rd_scr[0:1, pl.ds(here, wide)])).astype(bf16)
            ds_scr[:, p * wide : (p + 1) * wide] = ds
        dqt_scr[...] += dot32(key_cols, ds_scr[...])
        base = pl.multiple_of(group * per_group, per_group)
        half = per_group // 2
        dv = dot32(w_ref[0, 0], do_scr[pl.ds(base, half), :]) + dot32(
            w_ref[1, 0], do_scr[pl.ds(base + half, half), :]
        )
        dk = dot32(ds_scr[...], q_scr[pl.ds(base, per_group), :]) * SCALE
        is_first = jnp.full((128, HEAD_SIZE), core, jnp.int32) == 0
        for part, column in ((dk, 0), (dv, 256)):
            columns = lanes(column + group * HEAD_SIZE, HEAD_SIZE)
            keep_ref[kb, :, columns] = jnp.where(is_first, part[:128], part[128:]).astype(bf16)
            give_ref[kb, :, columns] = jnp.where(is_first, part[128:], part[:128]).astype(bf16)

    @pl.when(step == pl.num_programs(1) - 1)
    def _():
        for h in range(HEADS_PER_GROUP):
            dq = dqt_scr[:, h * tokens : (h + 1) * tokens] * SCALE
            dq_ref[:, lanes(group * per_group + h * HEAD_SIZE, HEAD_SIZE)] = dq.T.astype(bf16)


def attend_back(meta, queries, grads, attended, linv, mine, theirs, weights):
    tokens, width = queries.shape
    blocks = mine.shape[0]
    bf16, f32 = jnp.bfloat16, jnp.float32
    per_group = HEADS_PER_GROUP * tokens
    octets_per_group = HEADS_PER_GROUP // OCTET
    span = OCTET * tokens
    return pl.pallas_call(
        attend_back_kernel,
        grid_spec=pltpu.PrefetchScalarGridSpec(
            num_scalar_prefetch=1,
            grid=(KEY_VALUE_HEADS, blocks),
            in_specs=[
                whole(queries.shape),
                whole(grads.shape),
                whole(attended.shape),
                whole(linv.shape),
                whole(mine.shape),
                whole(theirs.shape),
                pl.BlockSpec(
                    (octets_per_group, 1, KEY_BLOCK, span),
                    lambda g, j, meta: (g, jnp.minimum(meta[0] + j, meta[1]), 0, 0),
                ),
            ],
            out_specs=[whole((tokens, width)), whole(mine.shape), whole(mine.shape)],
            scratch_shapes=[
                pltpu.VMEM((blocks * KEY_BLOCK, mine.shape[2]), bf16),
                pltpu.VMEM((blocks, mine.shape[2] // 2, KEY_BLOCK), bf16),
                pltpu.VMEM((QUERY_HEADS * tokens, HEAD_SIZE), bf16),
                pltpu.VMEM((QUERY_HEADS * tokens, HEAD_SIZE), bf16),
                pltpu.VMEM((8, QUERY_HEADS * tokens), f32),
                pltpu.VMEM((KEY_BLOCK, per_group), bf16),
                pltpu.VMEM((HEAD_SIZE, per_group), f32),
            ],
        ),
        out_shape=[
            jax.ShapeDtypeStruct((tokens, width), bf16),
            jax.ShapeDtypeStruct(mine.shape, bf16),
            jax.ShapeDtypeStruct(mine.shape, bf16),
        ],
        compiler_params=pltpu.CompilerParams(
            dimension_semantics=("arbitrary", "arbitrary"), vmem_limit_bytes=VMEM_LIMIT
        ),
        cost_estimate=pl.CostEstimate(
            flops=8 * tokens * width * 1536, bytes_accessed=20 << 20, transcendentals=0
        ),
        name="attend_back",
    )(meta, queries, grads, attended, linv, mine, theirs, weights)


def expert_kernel(
    rows_ref,
    inner_grad_ref,
    gate_hbm,
    up_hbm,
    out_ref,
    gate_scr,
    up_scr,
    turn_scr,
    x_scr,
    da_scr,
    db_scr,
    score_scr,
    sems,
):
    f32, bf16 = jnp.float32, jnp.bfloat16
    peers, per_peer = rows_ref.shape[0], rows_ref.shape[1]
    count = x_scr.shape[0]
    hidden_units = gate_scr.shape[1]
    capacity = count // peers
    loads = [
        pltpu.make_async_copy(gate_hbm, gate_scr, sems.at[0]),
        pltpu.make_async_copy(up_hbm, up_scr, sems.at[1]),
    ]
    for load in loads:
        load.start()

    def widen(i, _):
        for c in range(capacity):
            row = rows_ref[i, c * QUERY_HEADS : (c + 1) * QUERY_HEADS, :].astype(f32)
            turn_scr[pl.ds((i * capacity + c) * PITCH, QUERY_HEADS), :] = row
        return 0

    lax.fori_loop(0, peers, widen, 0, unroll=2)

    def turn(j, _):
        x_scr[:, lanes(j * HEAD_SIZE, HEAD_SIZE)] = turn_scr[
            pl.ds(j, count, stride=PITCH), :
        ].astype(bf16)
        return 0

    lax.fori_loop(0, QUERY_HEADS, turn, 0, unroll=2)
    for load in loads:
        load.wait()
    score_scr[...] = jnp.zeros_like(score_scr)
    span = 256

    def hidden_part(n, _):
        columns = lanes(n * span, span)
        a = dot32(x_scr[...], gate_scr[:, columns])
        b = dot32(x_scr[...], up_scr[:, columns])
        u = inner_grad_ref[:, columns]
        sig = 1.0 / (1.0 + jnp.exp(-a))
        act = a * sig
        product = u * b
        scores = jnp.sum(product * act, axis=1, keepdims=True)
        score_scr[0:count, :] += jnp.broadcast_to(scores, (count, HEAD_SIZE))
        da_scr[:, columns] = (product * sig * (1.0 + a * (1.0 - sig))).astype(bf16)
        db_scr[:, columns] = (u * act).astype(bf16)
        return 0

    lax.fori_loop(0, hidden_units // span, hidden_part, 0)

    def grad_part(j, _):
        rows = pl.ds(pl.multiple_of(j * span, span), span)
        d = dot32(da_scr[...], gate_scr[rows, :], NT) + dot32(db_scr[...], up_scr[rows, :], NT)
        turn_scr[pl.ds(2 * j, count, stride=PITCH), :] = d[:, :HEAD_SIZE]
        turn_scr[pl.ds(2 * j + 1, count, stride=PITCH), :] = d[:, HEAD_SIZE:]
        return 0

    lax.fori_loop(0, QUERY_HEADS // 2, grad_part, 0)

    def narrow(i, _):
        for c in range(capacity):
            row = turn_scr[pl.ds((i * capacity + c) * PITCH, QUERY_HEADS), :]
            out_ref[i, c * QUERY_HEADS : (c + 1) * QUERY_HEADS, :] = row.astype(bf16)
        out_ref[i, per_peer : per_peer + 8, :] = score_scr[pl.ds(capacity * i, 8), :].astype(bf16)
        return 0

    lax.fori_loop(0, peers, narrow, 0, unroll=2)


def expert(rows, inner_grad, gate_mat, up_mat):
    peers, per_peer, _ = rows.shape
    count = inner_grad.shape[0]
    width, hidden_units = gate_mat.shape
    f32, bf16 = jnp.float32, jnp.bfloat16
    return pl.pallas_call(
        expert_kernel,
        in_specs=[
            pl.BlockSpec(memory_space=pltpu.VMEM),
            pl.BlockSpec(memory_space=pltpu.VMEM),
            pl.BlockSpec(memory_space=pltpu.HBM),
            pl.BlockSpec(memory_space=pltpu.HBM),
        ],
        out_specs=pl.BlockSpec(memory_space=pltpu.VMEM),
        scratch_shapes=[
            pltpu.VMEM((width, hidden_units), bf16),
            pltpu.VMEM((width, hidden_units), bf16),
            pltpu.VMEM((count * PITCH, HEAD_SIZE), f32),
            pltpu.VMEM((count, width), bf16),
            pltpu.VMEM((count, hidden_units), bf16),
            pltpu.VMEM((count, hidden_units), bf16),
            pltpu.VMEM((count + 16, HEAD_SIZE), f32),
            pltpu.SemaphoreType.DMA((2,)),
        ],
        out_shape=jax.ShapeDtypeStruct((peers, per_peer + 8, HEAD_SIZE), bf16),
        compiler_params=pltpu.CompilerParams(vmem_limit_bytes=50 << 20),
        cost_estimate=pl.CostEstimate(
            flops=8 * count * width * hidden_units, bytes_accessed=20 << 20, transcendentals=count * hidden_units
        ),
        name="expert",
    )(rows, inner_grad, gate_mat, up_mat)


def combine_kernel(
    slots,
    gates_smem,
    back_ref,
    gates_ref,
    ids_ref,
    hid_ref,
    norm_ref,
    rms_ref,
    og_ref,
    gain_ref,
    router_ref,
    res_ref,
    part_ref,
    rows_scr,
    score_scr,
    dn_scr,
    acc_scr,
):
    f32, bf16 = jnp.float32, jnp.bfloat16
    tokens = hid_ref.shape[0]
    capacity = 3
    per_peer = capacity * QUERY_HEADS

    def pick(t, _):
        total = None
        scores = []
        for k in range(2):
            slot = slots[2 * t + k]
            e = slot // capacity
            c = slot - e * capacity
            start = pl.multiple_of(c * QUERY_HEADS, QUERY_HEADS)
            row = back_ref[e, pl.ds(start, QUERY_HEADS), :].astype(f32) * gates_smem[2 * t + k]
            total = row if total is None else total + row
            tail = back_ref[e, per_peer : per_peer + 8, :].astype(f32)
            which = lax.broadcasted_iota(jnp.int32, tail.shape, 0) == c
            scores.append(jnp.sum(jnp.where(which, tail, 0.0), axis=0, keepdims=True))
        rows_scr[pl.ds(t * PITCH, QUERY_HEADS), :] = total
        score_scr[pl.ds(t, 1), :] = scores[0] - scores[1]
        return 0

    lax.fori_loop(0, tokens, pick, 0, unroll=8)
    first = gates_ref[:, 0:1]
    value = first * (1.0 - first) * score_scr[...]
    lane = lax.broadcasted_iota(jnp.int32, (tokens, HEAD_SIZE), 1)
    d_logits = jnp.where(lane == ids_ref[:, 0:1], value, 0.0) - jnp.where(
        lane == ids_ref[:, 1:2], value, 0.0
    )
    d_logits = d_logits.astype(bf16)
    acc_scr[...] = jnp.zeros_like(acc_scr)

    def gather(h, _):
        columns = lanes(h * HEAD_SIZE, HEAD_SIZE)
        rows = pl.ds(pl.multiple_of(h * HEAD_SIZE, HEAD_SIZE), HEAD_SIZE)
        dn = rows_scr[pl.ds(h, tokens, stride=PITCH), :] + dot32(
            d_logits, router_ref[rows, :], NT
        )
        scaled = dn * gain_ref[:, columns]
        dn_scr[:, columns] = scaled
        acc_scr[...] += hid_ref[:, columns].astype(f32) * scaled
        part_ref[rows, :] = dot32(norm_ref[:, columns], d_logits, TN).astype(bf16)
        return 0

    lax.fori_loop(0, QUERY_HEADS, gather, 0, unroll=2)
    r = rms_ref[...]
    mean = jnp.sum(acc_scr[...], axis=1, keepdims=True) * (1.0 / (QUERY_HEADS * HEAD_SIZE))
    pull = r * r * r * mean

    def finish(h, _):
        columns = lanes(h * HEAD_SIZE, HEAD_SIZE)
        res = og_ref[:, columns].astype(f32) + r * dn_scr[:, columns] - hid_ref[:, columns].astype(f32) * pull
        res_ref[:, columns] = res.astype(bf16)
        return 0

    lax.fori_loop(0, QUERY_HEADS, finish, 0, unroll=2)


def combine(slots, gates, ids, back, hidden, normed, inv_rms, out_grad, gain, router):
    tokens, width = hidden.shape
    experts = router.shape[1]
    f32, bf16 = jnp.float32, jnp.bfloat16
    return pl.pallas_call(
        combine_kernel,
        in_specs=[pl.BlockSpec(memory_space=pltpu.SMEM)] * 2
        + [pl.BlockSpec(memory_space=pltpu.VMEM)] * 9,
        out_specs=[pl.BlockSpec(memory_space=pltpu.VMEM)] * 2,
        scratch_shapes=[
            pltpu.VMEM((tokens * PITCH, HEAD_SIZE), f32),
            pltpu.VMEM((tokens, HEAD_SIZE), f32),
            pltpu.VMEM((tokens, width), f32),
            pltpu.VMEM((tokens, HEAD_SIZE), f32),
        ],
        out_shape=[
            jax.ShapeDtypeStruct((tokens, width), bf16),
            jax.ShapeDtypeStruct((width, experts), bf16),
        ],
        compiler_params=pltpu.CompilerParams(vmem_limit_bytes=50 << 20),
        cost_estimate=pl.CostEstimate(
            flops=4 * tokens * width * experts, bytes_accessed=9 << 20, transcendentals=0
        ),
        name="combine",
    )(slots, gates.reshape(-1), back, gates, ids, hidden, normed, inv_rms, out_grad, gain, router)


def swap_cores(array):
    return lax.ppermute(array, CORE, [(0, 1), (1, 0)])


def exchange(array, axes):
    return lax.all_to_all(array, axes, split_axis=0, concat_axis=0, tiled=True)


def layer(
    queries,
    keys,
    values,
    stream,
    norm_gain,
    router_weight,
    gate_weight,
    up_weight,
    down_weight,
    doc_lengths,
    expert_ids,
    out_grad,
):
    token_rows = queries.shape[1]
    model_width = queries.shape[2]
    chips = lax.axis_size("blk_0") * lax.axis_size("blk_1")
    core = lax.axis_index(CORE)
    both = jnp.concatenate([keys[0], values[0]], axis=1)
    mine = exchange(jnp.broadcast_to(both[None], (chips, *both.shape)), ZX)
    theirs = swap_cores(mine)

    doc_ends = jnp.cumsum(doc_lengths[0], dtype=jnp.int32)
    first_query = lax.axis_index(BLK) * token_rows
    first_start = jnp.max(jnp.where(doc_ends <= first_query, doc_ends, 0))
    meta = jnp.concatenate(
        [
            jnp.stack(
                [
                    first_start // KEY_BLOCK,
                    (first_query + token_rows - 1) // KEY_BLOCK,
                    core,
                    first_query,
                ]
            ).astype(jnp.int32),
            doc_ends,
        ]
    )
    experts = router_weight.shape[1]
    chosen_ids = expert_ids[0]
    top_count = chosen_ids.shape[1]
    capacity = max(2, 3 * token_rows * top_count // (2 * experts))
    flat_ids = chosen_ids.reshape(-1)
    same = flat_ids[:, None] == flat_ids[None, :]
    order = jnp.arange(flat_ids.shape[0], dtype=jnp.int32)
    slot_rank = jnp.sum((same & (order[None, :] < order[:, None])).astype(jnp.int32), axis=1, dtype=jnp.int32)
    slots = flat_ids * capacity + slot_rank
    slot_count = experts * capacity

    send_grads = place(slots, out_grad[0], slot_count)
    got_grads = exchange(send_grads.reshape(experts, -1, HEAD_SIZE), GRP_BLK)

    weights, linv, attended, hidden, normed, inv_rms, send_rows = attend(
        meta, slots, queries[0], mine, theirs, stream[0], norm_gain[None], slot_count
    )
    got_rows = exchange(send_rows.reshape(experts, -1, HEAD_SIZE), GRP_BLK)

    logits = jnp.dot(normed, router_weight, preferred_element_type=jnp.float32)
    hits = chosen_ids[:, :, None] == jnp.arange(experts, dtype=jnp.int32)[None, None, :]
    chosen = jnp.sum(jnp.where(hits, logits[:, None, :], 0.0), axis=-1)
    first_gate = jax.nn.sigmoid(chosen[:, 0] - chosen[:, 1])
    gates = jnp.stack([first_gate, 1.0 - first_gate], axis=1)

    inner_grad = dot32(got_grads.reshape(slot_count, model_width), down_weight[0], NT)
    back = exchange(expert(got_rows, inner_grad, gate_weight[0], up_weight[0]), GRP_BLK)
    residual_gradient, router_parts = combine(
        slots, gates, chosen_ids, back, hidden, normed, inv_rms, out_grad[0], norm_gain[None], router_weight
    )
    got_parts = exchange(router_parts.reshape(experts, -1, experts), GRP_BLK)
    query_grad, keep, give = attend_back(
        meta, queries[0], residual_gradient, attended, linv, mine, theirs, weights
    )
    pair_sum = (keep.astype(jnp.float32) + swap_cores(give).astype(jnp.float32)).astype(jnp.bfloat16)
    summed = jnp.sum(exchange(pair_sum, ZX).astype(jnp.float32), axis=0).astype(jnp.bfloat16)
    router_grad = jnp.sum(got_parts.astype(jnp.float32), axis=0)
    half = KEY_VALUE_HEADS * HEAD_SIZE
    return (
        query_grad[None],
        summed[None, :, :half],
        summed[None, :, half:],
        residual_gradient[None],
        router_grad,
    )


def solution(mesh):
    split = Mesh(mesh.devices.reshape(2, 4, 4, 2, 2), ("grp_0", "grp_1", "blk_0", "blk_1", "blk_2"))
    return jax.shard_map(
        layer,
        mesh=split,
        in_specs=(
            P(GRP, BLK, None),
            P(GRP, BLK, None),
            P(GRP, BLK, None),
            P(GRP, BLK, None),
            P(),
            P(),
            P(GRP_BLK, None, None),
            P(GRP_BLK, None, None),
            P(GRP_BLK, None, None),
            P(GRP, None),
            P(GRP, BLK, None),
            P(GRP, BLK, None),
        ),
        out_specs=(
            P(GRP, BLK, None),
            P(GRP, BLK, None),
            P(GRP, BLK, None),
            P(GRP, BLK, None),
            P(GRP_BLK, None),
        ),
        check_vma=False,
    )
```

```python
import math

import jax
import jax.numpy as jnp
from jax import lax
from jax.experimental import pallas as pl
from jax.experimental.pallas import tpu as pltpu
from jax.sharding import Mesh
from jax.sharding import PartitionSpec as P


HEAD_SIZE = 128
QUERY_HEADS = 32
KEY_VALUE_HEADS = 2
HEADS_PER_GROUP = QUERY_HEADS // KEY_VALUE_HEADS
BLK = ("blk_0", "blk_1", "blk_2")
GRP_BLK = ("grp_0", "grp_1", "blk_0", "blk_1", "blk_2")
GRP = ("grp_0", "grp_1")
ZX = ("blk_0", "blk_1")
CORE = "blk_2"

NEGATIVE_HUGE = -1e30
EPSILON = 1e-06
SCALE = HEAD_SIZE ** (-0.5)
KEY_BLOCK = 256
OCTET = 8
VMEM_LIMIT = 60 * 1024 * 1024
PITCH = QUERY_HEADS + 1

NT = (((1,), (1,)), ((), ()))
TN = (((0,), (0,)), ((), ()))


def dot32(a, b, dims=(((1,), (0,)), ((), ()))):
    return lax.dot_general(a, b, dims, preferred_element_type=jnp.float32)


def lanes(start, size):
    return pl.ds(pl.multiple_of(start, 128), size)


def bounds(meta):
    place = meta[0] & 15
    first_query = place * 128
    ends = [meta[1]]
    for d in range(1, 4):
        ends.append(ends[-1] + meta[1 + d])
    start = jnp.int32(0)
    for end in ends:
        start = jnp.where(end <= first_query, end, start)
    return start // KEY_BLOCK, (first_query + 127) // KEY_BLOCK, meta[0] & 1, first_query, ends


def order_blocks(mine_ref, theirs_ref, core, kv_scr):
    is_first = jnp.full((128, mine_ref.shape[2]), core, jnp.int32) == 0

    def place(b, _):
        mine = mine_ref[b].astype(jnp.float32)
        theirs = theirs_ref[b].astype(jnp.float32)
        start = pl.multiple_of(b * KEY_BLOCK, KEY_BLOCK)
        kv_scr[pl.ds(start, 128), :] = jnp.where(is_first, mine, theirs).astype(jnp.bfloat16)
        kv_scr[pl.ds(start + 128, 128), :] = jnp.where(is_first, theirs, mine).astype(jnp.bfloat16)
        return 0

    lax.fori_loop(0, mine_ref.shape[0], place, 0)


def attend_kernel(
    meta,
    slots,
    q_ref,
    mine_ref,
    theirs_ref,
    stream_ref,
    gain_ref,
    w_ref,
    linv_ref,
    att_ref,
    hid_ref,
    norm_ref,
    rms_ref,
    send_ref,
    kv_scr,
    vt_scr,
    bias_scr,
    s_scr,
    ot_scr,
    ss_scr,
    rows_scr,
):
    octet = pl.program_id(0)
    group = octet // (HEADS_PER_GROUP // OCTET)
    low, high, core, first_query, ends = bounds(meta)
    tokens = q_ref.shape[0]
    factor = SCALE * math.log2(math.e)

    @pl.when(octet == 0)
    def _():
        order_blocks(mine_ref, theirs_ref, core, kv_scr)
        ss_scr[...] = jnp.zeros_like(ss_scr)
        query = first_query + lax.broadcasted_iota(jnp.int32, (KEY_BLOCK, tokens), 1)
        start = jnp.zeros((KEY_BLOCK, tokens), jnp.int32)
        for d in range(4):
            start = jnp.maximum(start, jnp.where(query >= ends[d], ends[d], 0))

        def prepare(kb, _):
            rows = pl.ds(pl.multiple_of(kb * KEY_BLOCK, KEY_BLOCK), KEY_BLOCK)
            vt_scr[kb] = kv_scr[rows, 256:512].T
            key = kb * KEY_BLOCK + lax.broadcasted_iota(jnp.int32, (KEY_BLOCK, tokens), 0)
            seen = (key <= query) & (key >= start)
            bias_scr[kb] = jnp.where(seen, 0.0, NEGATIVE_HUGE)
            return 0

        lax.fori_loop(low, high + 1, prepare, 0)

    pairs = OCTET // 2
    wide = 2 * tokens

    def score(kb, tops):
        rows = pl.ds(pl.multiple_of(kb * KEY_BLOCK, KEY_BLOCK), KEY_BLOCK)
        key_rows = kv_scr[rows, lanes(group * HEAD_SIZE, HEAD_SIZE)]
        bias = bias_scr[kb]
        bias = jnp.concatenate([bias, bias], axis=1)
        new = []
        for p in range(pairs):
            c = 2 * p * HEAD_SIZE
            both = jnp.concatenate(
                [q_ref[:, c : c + HEAD_SIZE], q_ref[:, c + HEAD_SIZE : c + 2 * HEAD_SIZE]], axis=0
            )
            s = dot32(key_rows, both, NT) + bias
            s_scr[kb, :, p * wide : (p + 1) * wide] = s
            new.append(jnp.maximum(tops[p], jnp.max(s.reshape(-1, 8, wide), axis=0)))
        return tuple(new)

    tops = lax.fori_loop(
        low, high + 1, score, tuple(jnp.full((8, wide), NEGATIVE_HUGE, jnp.float32) for _ in range(pairs))
    )
    tops = tuple(jnp.max(t, axis=0, keepdims=True) * factor for t in tops)
    ot_scr[...] = jnp.zeros_like(ot_scr)

    def weigh(kb, sums):
        value_cols = vt_scr[kb, pl.ds(pl.multiple_of(group * HEAD_SIZE, HEAD_SIZE), HEAD_SIZE), :]
        new = []
        for p in range(pairs):
            span = slice(p * wide, (p + 1) * wide)
            w = jnp.exp2(s_scr[kb, :, span] * factor - tops[p])
            new.append(sums[p] + jnp.sum(w.reshape(-1, 8, wide), axis=0))
            low_w = w.astype(jnp.bfloat16)
            w_ref[0, kb, :, span] = low_w
            ot_scr[:, span] += dot32(value_cols, low_w)
        return tuple(new)

    sums = lax.fori_loop(
        low, high + 1, weigh, tuple(jnp.zeros((8, wide), jnp.float32) for _ in range(pairs))
    )
    for p in range(pairs):
        inverse = 1.0 / jnp.sum(sums[p], axis=0, keepdims=True)
        mixed = ot_scr[:, p * wide : (p + 1) * wide] * inverse
        for i in range(2):
            h = 2 * p + i
            linv_ref[h : h + 1, :] = inverse[:, i * tokens : (i + 1) * tokens]
            columns = lanes((octet * OCTET + h) * HEAD_SIZE, HEAD_SIZE)
            att = mixed[:, i * tokens : (i + 1) * tokens].T.astype(jnp.bfloat16)
            att_ref[:, columns] = att
            hid = (stream_ref[:, columns].astype(jnp.float32) + att.astype(jnp.float32)).astype(
                jnp.bfloat16
            )
            hid_ref[:, columns] = hid
            wide_hid = hid.astype(jnp.float32)
            ss_scr[...] += wide_hid * wide_hid

    @pl.when(octet == pl.num_programs(0) - 1)
    def _():
        mean = jnp.sum(ss_scr[...], axis=1, keepdims=True) * (1.0 / (QUERY_HEADS * HEAD_SIZE))
        inv_rms = jnp.broadcast_to(lax.rsqrt(mean + EPSILON), (tokens, HEAD_SIZE))
        rms_ref[...] = inv_rms

        def norm(h, _):
            columns = lanes(h * HEAD_SIZE, HEAD_SIZE)
            n = (hid_ref[:, columns].astype(jnp.float32) * inv_rms * gain_ref[:, columns]).astype(
                jnp.bfloat16
            )
            norm_ref[:, columns] = n
            rows_scr[pl.ds(h, tokens, stride=PITCH), :] = n.astype(jnp.float32)
            return 0

        lax.fori_loop(0, QUERY_HEADS, norm, 0, unroll=2)
        scatter_rows(slots, rows_scr, send_ref, tokens)


def scatter_rows(slots, rows_scr, send_ref, tokens):
    def send(t, _):
        row = rows_scr[pl.ds(t * PITCH, QUERY_HEADS), :].astype(jnp.bfloat16)
        send_ref[slots[2 * t]] = row
        send_ref[slots[2 * t + 1]] = row
        return 0

    lax.fori_loop(0, tokens, send, 0, unroll=8)


def whole(shape):
    zero = (0,) * len(shape)
    return pl.BlockSpec(shape, lambda *_: zero)


def attend(meta, slots, queries, mine, theirs, stream, gain, slot_count):
    tokens, width = queries.shape
    octets = QUERY_HEADS // OCTET
    blocks = mine.shape[0]
    span = OCTET * tokens
    bf16, f32 = jnp.bfloat16, jnp.float32
    return pl.pallas_call(
        attend_kernel,
        grid_spec=pltpu.PrefetchScalarGridSpec(
            num_scalar_prefetch=2,
            grid=(octets,),
            in_specs=[
                pl.BlockSpec((tokens, OCTET * HEAD_SIZE), lambda o, *_: (0, o)),
                whole(mine.shape),
                whole(theirs.shape),
                whole(stream.shape),
                whole((1, width)),
            ],
            out_specs=[
                pl.BlockSpec((1, blocks, KEY_BLOCK, span), lambda o, *_: (o, 0, 0, 0)),
                pl.BlockSpec((OCTET, tokens), lambda o, *_: (o, 0)),
                whole((tokens, width)),
                whole((tokens, width)),
                whole((tokens, width)),
                whole((tokens, HEAD_SIZE)),
                whole((slot_count, QUERY_HEADS, HEAD_SIZE)),
            ],
            scratch_shapes=[
                pltpu.VMEM((blocks * KEY_BLOCK, mine.shape[2]), bf16),
                pltpu.VMEM((blocks, mine.shape[2] // 2, KEY_BLOCK), bf16),
                pltpu.VMEM((blocks, KEY_BLOCK, tokens), f32),
                pltpu.VMEM((blocks, KEY_BLOCK, span), f32),
                pltpu.VMEM((HEAD_SIZE, span), f32),
                pltpu.VMEM((tokens, HEAD_SIZE), f32),
                pltpu.VMEM((tokens * PITCH, HEAD_SIZE), f32),
            ],
        ),
        out_shape=[
            jax.ShapeDtypeStruct((octets, blocks, KEY_BLOCK, span), bf16),
            jax.ShapeDtypeStruct((QUERY_HEADS, tokens), f32),
            jax.ShapeDtypeStruct((tokens, width), bf16),
            jax.ShapeDtypeStruct((tokens, width), bf16),
            jax.ShapeDtypeStruct((tokens, width), bf16),
            jax.ShapeDtypeStruct((tokens, HEAD_SIZE), f32),
            jax.ShapeDtypeStruct((slot_count, QUERY_HEADS, HEAD_SIZE), bf16),
        ],
        compiler_params=pltpu.CompilerParams(
            dimension_semantics=("arbitrary",), vmem_limit_bytes=VMEM_LIMIT
        ),
        cost_estimate=pl.CostEstimate(
            flops=4 * tokens * width * 1536, bytes_accessed=24 << 20, transcendentals=tokens * 32 * 1536
        ),
        name="attend",
    )(meta, slots, queries, mine, theirs, stream, gain)


def place_kernel(slots, rows_ref, send_ref, rows_scr):
    tokens = rows_ref.shape[0]

    def turn(h, _):
        rows_scr[pl.ds(h, tokens, stride=PITCH), :] = rows_ref[
            :, lanes(h * HEAD_SIZE, HEAD_SIZE)
        ].astype(jnp.float32)
        return 0

    lax.fori_loop(0, QUERY_HEADS, turn, 0, unroll=2)
    scatter_rows(slots, rows_scr, send_ref, tokens)


def place(slots, rows, slot_count):
    tokens, _ = rows.shape
    return pl.pallas_call(
        place_kernel,
        grid_spec=pltpu.PrefetchScalarGridSpec(
            num_scalar_prefetch=1,
            grid=(1,),
            in_specs=[whole(rows.shape)],
            out_specs=whole((slot_count, QUERY_HEADS, HEAD_SIZE)),
            scratch_shapes=[pltpu.VMEM((tokens * PITCH, HEAD_SIZE), jnp.float32)],
        ),
        out_shape=jax.ShapeDtypeStruct((slot_count, QUERY_HEADS, HEAD_SIZE), jnp.bfloat16),
        compiler_params=pltpu.CompilerParams(vmem_limit_bytes=VMEM_LIMIT),
        cost_estimate=pl.CostEstimate(flops=0, bytes_accessed=4 << 20, transcendentals=0),
        name="place",
    )(slots, rows)


def attend_back_kernel(
    meta,
    q_hbm,
    grad_hbm,
    att_hbm,
    linv_ref,
    mine_hbm,
    theirs_hbm,
    w_hbm,
    dq_ref,
    keep_ref,
    give_ref,
    kv_scr,
    kt_scr,
    q_scr,
    do_scr,
    rd_scr,
    ds_scr,
    dqt_scr,
    w_buf,
    mine_ref,
    theirs_ref,
    q_ref,
    grad_ref,
    att_ref,
    sems,
):
    operands = ((mine_hbm, mine_ref), (theirs_hbm, theirs_ref), (q_hbm, q_ref), (grad_hbm, grad_ref), (att_hbm, att_ref))
    loads = [pltpu.make_async_copy(a, b, sems.at[2 + i]) for i, (a, b) in enumerate(operands)]
    for copy in loads:
        copy.start()
    low, high, core, _, _ = bounds(meta)
    count = high - low + 1
    tokens = q_ref.shape[0]
    wide = 2 * tokens
    per_group = HEADS_PER_GROUP * tokens
    octets = HEADS_PER_GROUP // OCTET
    f32, bf16 = jnp.float32, jnp.bfloat16

    def load(group, kb, slot):
        return pltpu.make_async_copy(
            w_hbm.at[pl.ds(group * octets, octets), kb], w_buf.at[slot], sems.at[slot]
        )

    load(0, low, 0).start()
    loads[0].wait()
    loads[1].wait()
    order_blocks(mine_ref, theirs_ref, core, kv_scr)
    keep_ref[...] = jnp.zeros_like(keep_ref)
    give_ref[...] = jnp.zeros_like(give_ref)

    def prepare(kb, _):
        rows = pl.ds(pl.multiple_of(kb * KEY_BLOCK, KEY_BLOCK), KEY_BLOCK)
        kt_scr[kb] = kv_scr[rows, 0:256].T
        return 0

    lax.fori_loop(low, high + 1, prepare, 0)
    inverse = jnp.concatenate(
        [linv_ref[...], jnp.zeros((128 - QUERY_HEADS, tokens), f32)], axis=0
    ).T
    ones = jnp.ones((8, HEAD_SIZE), bf16)
    for copy in loads[2:]:
        copy.wait()
    for h in range(QUERY_HEADS):
        columns = slice(h * HEAD_SIZE, (h + 1) * HEAD_SIZE)
        rows = slice(h * tokens, (h + 1) * tokens)
        q_scr[rows, :] = q_ref[:, columns]
        scaled = (grad_ref[:, columns].astype(f32) * inverse[:, h : h + 1]).astype(bf16)
        do_scr[rows, :] = scaled
        product = scaled.astype(f32) * att_ref[:, columns].astype(f32)
        head = product.astype(bf16)
        tail = (product - head.astype(f32)).astype(bf16)
        rd_scr[:, rows] = dot32(ones, head, NT) + dot32(ones, tail, NT)

    is_first = jnp.full((128, HEAD_SIZE), core, jnp.int32) == 0

    def one_group(group, _):
        dqt_scr[...] = jnp.zeros_like(dqt_scr)
        base = pl.multiple_of(group * per_group, per_group)
        half = per_group // octets

        def one_block(j, _):
            kb = low + j
            turn = group * count + j
            slot = lax.rem(turn, 2)
            load(group, kb, slot).wait()

            @pl.when(turn + 1 < KEY_VALUE_HEADS * count)
            def _():
                wrap = j + 1 == count
                load(
                    jnp.where(wrap, group + 1, group), low + jnp.where(wrap, 0, j + 1), 1 - slot
                ).start()

            rows = pl.ds(pl.multiple_of(kb * KEY_BLOCK, KEY_BLOCK), KEY_BLOCK)
            value_rows = kv_scr[rows, lanes(256 + group * HEAD_SIZE, HEAD_SIZE)]
            key_cols = kt_scr[kb, pl.ds(pl.multiple_of(group * HEAD_SIZE, HEAD_SIZE), HEAD_SIZE), :]
            for p in range(HEADS_PER_GROUP // 2):
                here = pl.multiple_of(group * per_group + p * wide, wide)
                dp = dot32(value_rows, do_scr[pl.ds(here, wide), :], NT)
                per_octet = OCTET // 2
                c = (p % per_octet) * wide
                w = w_buf[slot, p // per_octet, :, c : c + wide].astype(f32)
                ds = (w * (dp - rd_scr[0:1, pl.ds(here, wide)])).astype(bf16)
                ds_scr[:, p * wide : (p + 1) * wide] = ds
            dqt_scr[...] += dot32(key_cols, ds_scr[...])
            dv = dot32(w_buf[slot, 0], do_scr[pl.ds(base, half), :]) + dot32(
                w_buf[slot, 1], do_scr[pl.ds(base + half, half), :]
            )
            dk = dot32(ds_scr[...], q_scr[pl.ds(base, per_group), :]) * SCALE
            for part, column in ((dk, 0), (dv, 256)):
                columns = lanes(column + group * HEAD_SIZE, HEAD_SIZE)
                keep_ref[kb, :, columns] = jnp.where(is_first, part[:128], part[128:]).astype(bf16)
                give_ref[kb, :, columns] = jnp.where(is_first, part[128:], part[:128]).astype(bf16)
            return 0

        lax.fori_loop(0, count, one_block, 0)
        for h in range(HEADS_PER_GROUP):
            dq = dqt_scr[:, h * tokens : (h + 1) * tokens] * SCALE
            dq_ref[:, lanes(group * per_group + h * HEAD_SIZE, HEAD_SIZE)] = dq.T.astype(bf16)
        return 0

    lax.fori_loop(0, KEY_VALUE_HEADS, one_group, 0)


def attend_back(meta, queries, grads, attended, linv, mine, theirs, weights):
    tokens, width = queries.shape
    blocks = mine.shape[0]
    bf16, f32 = jnp.bfloat16, jnp.float32
    per_group = HEADS_PER_GROUP * tokens
    octets = HEADS_PER_GROUP // OCTET
    span = OCTET * tokens
    vmem, hbm = pl.BlockSpec(memory_space=pltpu.VMEM), pl.BlockSpec(memory_space=pltpu.HBM)
    return pl.pallas_call(
        attend_back_kernel,
        in_specs=[pl.BlockSpec(memory_space=pltpu.SMEM)] + [hbm] * 3 + [vmem] + [hbm] * 3,
        out_specs=[vmem] * 3,
        scratch_shapes=[
            pltpu.VMEM((blocks * KEY_BLOCK, mine.shape[2]), bf16),
            pltpu.VMEM((blocks, mine.shape[2] // 2, KEY_BLOCK), bf16),
            pltpu.VMEM((QUERY_HEADS * tokens, HEAD_SIZE), bf16),
            pltpu.VMEM((QUERY_HEADS * tokens, HEAD_SIZE), bf16),
            pltpu.VMEM((8, QUERY_HEADS * tokens), f32),
            pltpu.VMEM((KEY_BLOCK, per_group), bf16),
            pltpu.VMEM((HEAD_SIZE, per_group), f32),
            pltpu.VMEM((2, octets, KEY_BLOCK, span), bf16),
            pltpu.VMEM(mine.shape, bf16),
            pltpu.VMEM(mine.shape, bf16),
            pltpu.VMEM((tokens, width), bf16),
            pltpu.VMEM((tokens, width), bf16),
            pltpu.VMEM((tokens, width), bf16),
            pltpu.SemaphoreType.DMA((7,)),
        ],
        out_shape=[
            jax.ShapeDtypeStruct((tokens, width), bf16),
            jax.ShapeDtypeStruct(mine.shape, bf16),
            jax.ShapeDtypeStruct(mine.shape, bf16),
        ],
        compiler_params=pltpu.CompilerParams(vmem_limit_bytes=58 << 20),
        cost_estimate=pl.CostEstimate(
            flops=8 * tokens * width * 1536, bytes_accessed=20 << 20, transcendentals=0
        ),
        name="attend_back",
    )(meta, queries, grads, attended, linv, mine, theirs, weights)


def turn_rows(rows_ref, turn_scr, x_scr):
    peers, per_peer = rows_ref.shape[0], rows_ref.shape[1]
    capacity = per_peer // QUERY_HEADS
    count = peers * capacity

    def widen(i, _):
        for c in range(capacity):
            row = rows_ref[i, c * QUERY_HEADS : (c + 1) * QUERY_HEADS, :].astype(jnp.float32)
            turn_scr[pl.ds((i * capacity + c) * PITCH, QUERY_HEADS), :] = row
        return 0

    lax.fori_loop(0, peers, widen, 0, unroll=2)

    def turn(j, _):
        x_scr[:, lanes(j * HEAD_SIZE, HEAD_SIZE)] = turn_scr[
            pl.ds(j, count, stride=PITCH), :
        ].astype(jnp.bfloat16)
        return 0

    lax.fori_loop(0, QUERY_HEADS, turn, 0, unroll=2)


def down_kernel(rows_ref, down_ref, out_ref, turn_scr, x_scr):
    turn_rows(rows_ref, turn_scr, x_scr)
    span = 256

    def part(n, _):
        rows = pl.ds(pl.multiple_of(n * span, span), span)
        out_ref[:, lanes(n * span, span)] = dot32(x_scr[...], down_ref[rows, :], NT)
        return 0

    lax.fori_loop(0, down_ref.shape[0] // span, part, 0)


def down(rows, down_mat):
    peers, per_peer, _ = rows.shape
    hidden_units, width = down_mat.shape
    count = peers * per_peer // QUERY_HEADS
    vmem = pl.BlockSpec(memory_space=pltpu.VMEM)
    return pl.pallas_call(
        down_kernel,
        in_specs=[vmem] * 2,
        out_specs=vmem,
        scratch_shapes=[
            pltpu.VMEM((count * PITCH, HEAD_SIZE), jnp.float32),
            pltpu.VMEM((count, width), jnp.bfloat16),
        ],
        out_shape=jax.ShapeDtypeStruct((count, hidden_units), jnp.float32),
        compiler_params=pltpu.CompilerParams(vmem_limit_bytes=50 << 20),
        cost_estimate=pl.CostEstimate(
            flops=2 * count * width * hidden_units, bytes_accessed=11 << 20, transcendentals=0
        ),
        name="down",
    )(rows, down_mat)


def expert_kernel(
    rows_ref,
    inner_grad_ref,
    gate_hbm,
    up_hbm,
    out_ref,
    gate_ref,
    up_ref,
    turn_scr,
    x_scr,
    da_scr,
    db_scr,
    score_scr,
    sems,
):
    bf16 = jnp.bfloat16
    peers, per_peer = rows_ref.shape[0], rows_ref.shape[1]
    count = x_scr.shape[0]
    hidden_units = gate_ref.shape[1]
    capacity = count // peers

    span = 256
    parts = hidden_units // span

    def load(n):
        columns = lanes(n * span, span)
        return (
            pltpu.make_async_copy(gate_hbm.at[:, columns], gate_ref.at[:, columns], sems.at[0, n]),
            pltpu.make_async_copy(up_hbm.at[:, columns], up_ref.at[:, columns], sems.at[1, n]),
        )

    for n in range(parts):
        for copy in load(n):
            copy.start()
    turn_rows(rows_ref, turn_scr, x_scr)
    score_scr[...] = jnp.zeros_like(score_scr)

    def hidden_part(n, _):
        for copy in load(n):
            copy.wait()
        columns = lanes(n * span, span)
        a = dot32(x_scr[...], gate_ref[:, columns])
        b = dot32(x_scr[...], up_ref[:, columns])
        u = inner_grad_ref[:, columns]
        sig = 1.0 / (1.0 + jnp.exp(-a))
        act = a * sig
        product = u * b
        scores = jnp.sum(product * act, axis=1, keepdims=True)
        score_scr[0:count, :] += jnp.broadcast_to(scores, (count, HEAD_SIZE))
        da_scr[:, columns] = (product * sig * (1.0 + a * (1.0 - sig))).astype(bf16)
        db_scr[:, columns] = (u * act).astype(bf16)
        return 0

    lax.fori_loop(0, parts, hidden_part, 0)

    def grad_part(j, _):
        rows = pl.ds(pl.multiple_of(j * span, span), span)
        d = dot32(da_scr[...], gate_ref[rows, :], NT) + dot32(db_scr[...], up_ref[rows, :], NT)
        turn_scr[pl.ds(2 * j, count, stride=PITCH), :] = d[:, :HEAD_SIZE]
        turn_scr[pl.ds(2 * j + 1, count, stride=PITCH), :] = d[:, HEAD_SIZE:]
        return 0

    lax.fori_loop(0, QUERY_HEADS // 2, grad_part, 0)

    def narrow(i, _):
        for c in range(capacity):
            row = turn_scr[pl.ds((i * capacity + c) * PITCH, QUERY_HEADS), :]
            out_ref[i, c * QUERY_HEADS : (c + 1) * QUERY_HEADS, :] = row.astype(bf16)
        out_ref[i, per_peer : per_peer + 8, :] = score_scr[pl.ds(capacity * i, 8), :].astype(bf16)
        return 0

    lax.fori_loop(0, peers, narrow, 0, unroll=2)


def expert(rows, inner_grad, gate_mat, up_mat):
    peers, per_peer, _ = rows.shape
    count = inner_grad.shape[0]
    width, hidden_units = gate_mat.shape
    f32, bf16 = jnp.float32, jnp.bfloat16
    return pl.pallas_call(
        expert_kernel,
        in_specs=[pl.BlockSpec(memory_space=pltpu.VMEM)] * 2
        + [pl.BlockSpec(memory_space=pltpu.HBM)] * 2,
        out_specs=pl.BlockSpec(memory_space=pltpu.VMEM),
        scratch_shapes=[
            pltpu.VMEM((width, hidden_units), bf16),
            pltpu.VMEM((width, hidden_units), bf16),
            pltpu.VMEM((count * PITCH, HEAD_SIZE), f32),
            pltpu.VMEM((count, width), bf16),
            pltpu.VMEM((count, hidden_units), bf16),
            pltpu.VMEM((count, hidden_units), bf16),
            pltpu.VMEM((count + 16, HEAD_SIZE), f32),
            pltpu.SemaphoreType.DMA((2, hidden_units // 256)),
        ],
        out_shape=jax.ShapeDtypeStruct((peers, per_peer + 8, HEAD_SIZE), bf16),
        compiler_params=pltpu.CompilerParams(vmem_limit_bytes=50 << 20),
        cost_estimate=pl.CostEstimate(
            flops=8 * count * width * hidden_units, bytes_accessed=20 << 20, transcendentals=count * hidden_units
        ),
        name="expert",
    )(rows, inner_grad, gate_mat, up_mat)


def combine_kernel(
    ids_smem,
    ranks,
    gates_smem,
    back_ref,
    gates_ref,
    ids_ref,
    hid_ref,
    norm_ref,
    rms_ref,
    og_ref,
    gain_ref,
    router_ref,
    res_ref,
    part_ref,
    rows_scr,
    score_scr,
    dn_scr,
    acc_scr,
):
    f32, bf16 = jnp.float32, jnp.bfloat16
    tokens = hid_ref.shape[0]
    capacity = 3
    per_peer = capacity * QUERY_HEADS

    def pick(t, _):
        total = None
        scores = []
        for k in range(2):
            e = ids_smem[2 * t + k]
            c = ranks[2 * t + k]
            start = pl.multiple_of(c * QUERY_HEADS, QUERY_HEADS)
            row = back_ref[e, pl.ds(start, QUERY_HEADS), :].astype(f32) * gates_smem[2 * t + k]
            total = row if total is None else total + row
            tail = back_ref[e, per_peer : per_peer + 8, :].astype(f32)
            which = lax.broadcasted_iota(jnp.int32, tail.shape, 0) == c
            scores.append(jnp.sum(jnp.where(which, tail, 0.0), axis=0, keepdims=True))
        rows_scr[pl.ds(t * PITCH, QUERY_HEADS), :] = total
        score_scr[pl.ds(t, 1), :] = scores[0] - scores[1]
        return 0

    lax.fori_loop(0, tokens, pick, 0, unroll=8)
    first = gates_ref[:, 0:1]
    value = first * (1.0 - first) * score_scr[...]
    lane = lax.broadcasted_iota(jnp.int32, (tokens, HEAD_SIZE), 1)
    d_logits = jnp.where(lane == ids_ref[:, 0:1], value, 0.0) - jnp.where(
        lane == ids_ref[:, 1:2], value, 0.0
    )
    d_logits = d_logits.astype(bf16)
    acc_scr[...] = jnp.zeros_like(acc_scr)

    def gather(h, _):
        columns = lanes(h * HEAD_SIZE, HEAD_SIZE)
        rows = pl.ds(pl.multiple_of(h * HEAD_SIZE, HEAD_SIZE), HEAD_SIZE)
        dn = rows_scr[pl.ds(h, tokens, stride=PITCH), :] + dot32(
            d_logits, router_ref[rows, :], NT
        )
        scaled = dn * gain_ref[:, columns]
        dn_scr[:, columns] = scaled
        acc_scr[...] += hid_ref[:, columns].astype(f32) * scaled
        part_ref[rows, :] = dot32(norm_ref[:, columns], d_logits, TN).astype(bf16)
        return 0

    lax.fori_loop(0, QUERY_HEADS, gather, 0, unroll=2)
    r = rms_ref[...]
    mean = jnp.sum(acc_scr[...], axis=1, keepdims=True) * (1.0 / (QUERY_HEADS * HEAD_SIZE))
    pull = r * r * r * mean

    def finish(h, _):
        columns = lanes(h * HEAD_SIZE, HEAD_SIZE)
        res = og_ref[:, columns].astype(f32) + r * dn_scr[:, columns] - hid_ref[:, columns].astype(f32) * pull
        res_ref[:, columns] = res.astype(bf16)
        return 0

    lax.fori_loop(0, QUERY_HEADS, finish, 0, unroll=2)


def combine(ranks, gates, ids, back, hidden, normed, inv_rms, out_grad, gain, router):
    tokens, width = hidden.shape
    experts = router.shape[1]
    f32, bf16 = jnp.float32, jnp.bfloat16
    return pl.pallas_call(
        combine_kernel,
        in_specs=[pl.BlockSpec(memory_space=pltpu.SMEM)] * 3
        + [pl.BlockSpec(memory_space=pltpu.VMEM)] * 9,
        out_specs=[pl.BlockSpec(memory_space=pltpu.VMEM)] * 2,
        scratch_shapes=[
            pltpu.VMEM((tokens * PITCH, HEAD_SIZE), f32),
            pltpu.VMEM((tokens, HEAD_SIZE), f32),
            pltpu.VMEM((tokens, width), f32),
            pltpu.VMEM((tokens, HEAD_SIZE), f32),
        ],
        out_shape=[
            jax.ShapeDtypeStruct((tokens, width), bf16),
            jax.ShapeDtypeStruct((width, experts), bf16),
        ],
        compiler_params=pltpu.CompilerParams(vmem_limit_bytes=50 << 20),
        cost_estimate=pl.CostEstimate(
            flops=4 * tokens * width * experts, bytes_accessed=9 << 20, transcendentals=0
        ),
        name="combine",
    )(ids.reshape(-1), ranks, gates.reshape(-1), back, gates, ids, hidden, normed, inv_rms, out_grad, gain, router)


def swap_cores(array):
    return lax.ppermute(array, CORE, [(0, 1), (1, 0)])


def exchange(array, axes):
    return lax.all_to_all(array, axes, split_axis=0, concat_axis=0, tiled=True)


def layer(
    queries,
    keys,
    values,
    stream,
    norm_gain,
    router_weight,
    gate_weight,
    up_weight,
    down_weight,
    doc_lengths,
    expert_ids,
    out_grad,
):
    token_rows = queries.shape[1]
    chips = lax.axis_size("blk_0") * lax.axis_size("blk_1")
    both = jnp.concatenate([keys[0], values[0]], axis=1)
    mine = exchange(jnp.broadcast_to(both[None], (chips, *both.shape)), ZX)
    theirs = swap_cores(mine)

    meta = jnp.concatenate([lax.axis_index(GRP_BLK).astype(jnp.int32)[None], doc_lengths[0]])
    experts = router_weight.shape[1]
    chosen_ids = expert_ids[0]
    top_count = chosen_ids.shape[1]
    capacity = max(2, 3 * token_rows * top_count // (2 * experts))
    flat_ids = chosen_ids.reshape(-1)
    same = flat_ids[:, None] == flat_ids[None, :]
    order = jnp.arange(flat_ids.shape[0], dtype=jnp.int32)
    slot_rank = jnp.sum((same & (order[None, :] < order[:, None])).astype(jnp.int32), axis=1, dtype=jnp.int32)
    slots = flat_ids * capacity + slot_rank
    slot_count = experts * capacity

    send_grads = place(slots, out_grad[0], slot_count)
    got_grads = exchange(send_grads.reshape(experts, -1, HEAD_SIZE), GRP_BLK)

    weights, linv, attended, hidden, normed, inv_rms, send_rows = attend(
        meta, slots, queries[0], mine, theirs, stream[0], norm_gain[None], slot_count
    )
    got_rows = exchange(send_rows.reshape(experts, -1, HEAD_SIZE), GRP_BLK)

    logits = jnp.dot(normed, router_weight, preferred_element_type=jnp.float32)
    hits = chosen_ids[:, :, None] == jnp.arange(experts, dtype=jnp.int32)[None, None, :]
    chosen = jnp.sum(jnp.where(hits, logits[:, None, :], 0.0), axis=-1)
    first_gate = jax.nn.sigmoid(chosen[:, 0] - chosen[:, 1])
    gates = jnp.stack([first_gate, 1.0 - first_gate], axis=1)

    inner_grad = down(got_grads, down_weight[0])
    back = exchange(expert(got_rows, inner_grad, gate_weight[0], up_weight[0]), GRP_BLK)
    residual_gradient, router_parts = combine(
        slot_rank, gates, chosen_ids, back, hidden, normed, inv_rms, out_grad[0], norm_gain[None], router_weight
    )
    got_parts = exchange(router_parts.reshape(experts, -1, experts), GRP_BLK)
    query_grad, keep, give = attend_back(
        meta, queries[0], residual_gradient, attended, linv, mine, theirs, weights
    )
    pair_sum = (keep.astype(jnp.float32) + swap_cores(give).astype(jnp.float32)).astype(jnp.bfloat16)
    summed = jnp.sum(exchange(pair_sum, ZX).astype(jnp.float32), axis=0).astype(jnp.bfloat16)
    router_grad = jnp.sum(got_parts.astype(jnp.float32), axis=0)
    half = KEY_VALUE_HEADS * HEAD_SIZE
    return (
        query_grad[None],
        summed[None, :, :half],
        summed[None, :, half:],
        residual_gradient[None],
        router_grad,
    )


def solution(mesh):
    split = Mesh(mesh.devices.reshape(2, 4, 4, 2, 2), ("grp_0", "grp_1", "blk_0", "blk_1", "blk_2"))
    return jax.shard_map(
        layer,
        mesh=split,
        in_specs=(
            P(GRP, BLK, None),
            P(GRP, BLK, None),
            P(GRP, BLK, None),
            P(GRP, BLK, None),
            P(),
            P(),
            P(GRP_BLK, None, None),
            P(GRP_BLK, None, None),
            P(GRP_BLK, None, None),
            P(GRP, None),
            P(GRP, BLK, None),
            P(GRP, BLK, None),
        ),
        out_specs=(
            P(GRP, BLK, None),
            P(GRP, BLK, None),
            P(GRP, BLK, None),
            P(GRP, BLK, None),
            P(GRP_BLK, None),
        ),
        check_vma=False,
    )
```

```python
import math

import jax
import jax.numpy as jnp
from jax import lax
from jax.experimental import pallas as pl
from jax.experimental.pallas import tpu as pltpu
from jax.sharding import Mesh
from jax.sharding import PartitionSpec as P


HEAD_SIZE = 128
QUERY_HEADS = 32
KEY_VALUE_HEADS = 2
HEADS_PER_GROUP = QUERY_HEADS // KEY_VALUE_HEADS
BLK = ("blk_0", "blk_1", "blk_2")
GRP_BLK = ("grp_0", "grp_1", "blk_0", "blk_1", "blk_2")
GRP = ("grp_0", "grp_1")
ZX = ("blk_0", "blk_1")
CORE = "blk_2"

NEGATIVE_HUGE = -1e30
EPSILON = 1e-06
SCALE = HEAD_SIZE ** (-0.5)
KEY_BLOCK = 256
OCTET = 8
VMEM_LIMIT = 60 * 1024 * 1024
PITCH = QUERY_HEADS + 1

NT = (((1,), (1,)), ((), ()))
TN = (((0,), (0,)), ((), ()))


def dot32(a, b, dims=(((1,), (0,)), ((), ()))):
    return lax.dot_general(a, b, dims, preferred_element_type=jnp.float32)


def lanes(start, size):
    return pl.ds(pl.multiple_of(start, 128), size)


def bounds(meta):
    place = meta[0] & 15
    first_query = place * 128
    ends = [meta[1]]
    for d in range(1, 4):
        ends.append(ends[-1] + meta[1 + d])
    start = jnp.int32(0)
    for end in ends:
        start = jnp.where(end <= first_query, end, start)
    return start // KEY_BLOCK, (first_query + 127) // KEY_BLOCK, meta[0] & 1, first_query, ends


def block_loads(meta, sources, kv_scr, sems):
    core, x = meta[0] & 1, (meta[0] >> 1) & 1
    copies = []
    for i, source in enumerate(sources):
        for z in range(source.shape[0]):
            block = (z * 2 + ((x + i) & 1)) * 2 + ((core + i // 2) & 1)
            rows = pl.ds(pl.multiple_of(block * 128, 128), 128)
            copies.append(
                pltpu.make_async_copy(
                    source.at[z], kv_scr.at[rows, :], sems.at[i * source.shape[0] + z]
                )
            )
    return copies


def attend_kernel(
    meta,
    slots,
    q_ref,
    near_hbm,
    far_hbm,
    near_other_hbm,
    far_other_hbm,
    stream_ref,
    gain_ref,
    w_ref,
    linv_ref,
    att_ref,
    hid_ref,
    norm_ref,
    rms_ref,
    send_ref,
    kv_scr,
    vt_scr,
    bias_scr,
    s_scr,
    ot_scr,
    ss_scr,
    rows_scr,
    sems,
):
    octet = pl.program_id(0)
    group = octet // (HEADS_PER_GROUP // OCTET)
    low, high, _, first_query, ends = bounds(meta)
    tokens = q_ref.shape[0]
    factor = SCALE * math.log2(math.e)

    @pl.when(octet == 0)
    def _():
        sources = (near_hbm, far_hbm, near_other_hbm, far_other_hbm)
        copies = block_loads(meta, sources, kv_scr, sems)
        for copy in copies:
            copy.start()
        ss_scr[...] = jnp.zeros_like(ss_scr)
        query = first_query + lax.broadcasted_iota(jnp.int32, (KEY_BLOCK, tokens), 1)
        start = jnp.zeros((KEY_BLOCK, tokens), jnp.int32)
        for d in range(4):
            start = jnp.maximum(start, jnp.where(query >= ends[d], ends[d], 0))

        for copy in copies:
            copy.wait()

        def prepare(kb, _):
            rows = pl.ds(pl.multiple_of(kb * KEY_BLOCK, KEY_BLOCK), KEY_BLOCK)
            vt_scr[kb] = kv_scr[rows, 256:512].T
            key = kb * KEY_BLOCK + lax.broadcasted_iota(jnp.int32, (KEY_BLOCK, tokens), 0)
            seen = (key <= query) & (key >= start)
            bias_scr[kb] = jnp.where(seen, 0.0, NEGATIVE_HUGE)
            return 0

        lax.fori_loop(low, high + 1, prepare, 0)

    pairs = OCTET // 2
    wide = 2 * tokens

    def score(kb, tops):
        rows = pl.ds(pl.multiple_of(kb * KEY_BLOCK, KEY_BLOCK), KEY_BLOCK)
        key_rows = kv_scr[rows, lanes(group * HEAD_SIZE, HEAD_SIZE)]
        bias = bias_scr[kb]
        bias = jnp.concatenate([bias, bias], axis=1)
        new = []
        for p in range(pairs):
            c = 2 * p * HEAD_SIZE
            both = jnp.concatenate(
                [q_ref[:, c : c + HEAD_SIZE], q_ref[:, c + HEAD_SIZE : c + 2 * HEAD_SIZE]], axis=0
            )
            s = dot32(key_rows, both, NT) + bias
            s_scr[kb, :, p * wide : (p + 1) * wide] = s
            new.append(jnp.maximum(tops[p], jnp.max(s.reshape(-1, 8, wide), axis=0)))
        return tuple(new)

    tops = lax.fori_loop(
        low, high + 1, score, tuple(jnp.full((8, wide), NEGATIVE_HUGE, jnp.float32) for _ in range(pairs))
    )
    tops = tuple(jnp.max(t, axis=0, keepdims=True) * factor for t in tops)
    ot_scr[...] = jnp.zeros_like(ot_scr)

    def weigh(kb, sums):
        value_cols = vt_scr[kb, pl.ds(pl.multiple_of(group * HEAD_SIZE, HEAD_SIZE), HEAD_SIZE), :]
        new = []
        for p in range(pairs):
            span = slice(p * wide, (p + 1) * wide)
            w = jnp.exp2(s_scr[kb, :, span] * factor - tops[p])
            new.append(sums[p] + jnp.sum(w.reshape(-1, 8, wide), axis=0))
            low_w = w.astype(jnp.bfloat16)
            w_ref[0, kb, :, span] = low_w
            ot_scr[:, span] += dot32(value_cols, low_w)
        return tuple(new)

    sums = lax.fori_loop(
        low, high + 1, weigh, tuple(jnp.zeros((8, wide), jnp.float32) for _ in range(pairs))
    )
    for p in range(pairs):
        inverse = 1.0 / jnp.sum(sums[p], axis=0, keepdims=True)
        mixed = ot_scr[:, p * wide : (p + 1) * wide] * inverse
        for i in range(2):
            h = 2 * p + i
            linv_ref[h : h + 1, :] = inverse[:, i * tokens : (i + 1) * tokens]
            columns = lanes((octet * OCTET + h) * HEAD_SIZE, HEAD_SIZE)
            att = mixed[:, i * tokens : (i + 1) * tokens].T.astype(jnp.bfloat16)
            att_ref[:, columns] = att
            hid = (stream_ref[:, columns].astype(jnp.float32) + att.astype(jnp.float32)).astype(
                jnp.bfloat16
            )
            hid_ref[:, columns] = hid
            wide_hid = hid.astype(jnp.float32)
            ss_scr[...] += wide_hid * wide_hid

    @pl.when(octet == pl.num_programs(0) - 1)
    def _():
        mean = jnp.sum(ss_scr[...], axis=1, keepdims=True) * (1.0 / (QUERY_HEADS * HEAD_SIZE))
        inv_rms = jnp.broadcast_to(lax.rsqrt(mean + EPSILON), (tokens, HEAD_SIZE))
        rms_ref[...] = inv_rms

        def norm(h, _):
            columns = lanes(h * HEAD_SIZE, HEAD_SIZE)
            n = (hid_ref[:, columns].astype(jnp.float32) * inv_rms * gain_ref[:, columns]).astype(
                jnp.bfloat16
            )
            norm_ref[:, columns] = n
            rows_scr[pl.ds(h, tokens, stride=PITCH), :] = n.astype(jnp.float32)
            return 0

        lax.fori_loop(0, QUERY_HEADS, norm, 0, unroll=2)
        scatter_rows(slots, rows_scr, send_ref, tokens)


def scatter_rows(slots, rows_scr, send_ref, tokens):
    def send(t, _):
        row = rows_scr[pl.ds(t * PITCH, QUERY_HEADS), :].astype(jnp.bfloat16)
        send_ref[slots[2 * t]] = row
        send_ref[slots[2 * t + 1]] = row
        return 0

    lax.fori_loop(0, tokens, send, 0, unroll=8)


def whole(shape):
    zero = (0,) * len(shape)
    return pl.BlockSpec(shape, lambda *_: zero)


def attend(meta, slots, queries, sources, stream, gain, slot_count):
    tokens, width = queries.shape
    octets = QUERY_HEADS // OCTET
    blocks = 2 * sources[0].shape[0]
    columns = sources[0].shape[2]
    span = OCTET * tokens
    bf16, f32 = jnp.bfloat16, jnp.float32
    return pl.pallas_call(
        attend_kernel,
        grid_spec=pltpu.PrefetchScalarGridSpec(
            num_scalar_prefetch=2,
            grid=(octets,),
            in_specs=[
                pl.BlockSpec((tokens, OCTET * HEAD_SIZE), lambda o, *_: (0, o)),
                *[pl.BlockSpec(memory_space=pltpu.HBM)] * 4,
                whole(stream.shape),
                whole((1, width)),
            ],
            out_specs=[
                pl.BlockSpec((1, blocks, KEY_BLOCK, span), lambda o, *_: (o, 0, 0, 0)),
                pl.BlockSpec((OCTET, tokens), lambda o, *_: (o, 0)),
                whole((tokens, width)),
                whole((tokens, width)),
                whole((tokens, width)),
                whole((tokens, HEAD_SIZE)),
                whole((slot_count, QUERY_HEADS, HEAD_SIZE)),
            ],
            scratch_shapes=[
                pltpu.VMEM((blocks * KEY_BLOCK, columns), bf16),
                pltpu.VMEM((blocks, columns // 2, KEY_BLOCK), bf16),
                pltpu.VMEM((blocks, KEY_BLOCK, tokens), f32),
                pltpu.VMEM((blocks, KEY_BLOCK, span), f32),
                pltpu.VMEM((HEAD_SIZE, span), f32),
                pltpu.VMEM((tokens, HEAD_SIZE), f32),
                pltpu.VMEM((tokens * PITCH, HEAD_SIZE), f32),
                pltpu.SemaphoreType.DMA((16,)),
            ],
        ),
        out_shape=[
            jax.ShapeDtypeStruct((octets, blocks, KEY_BLOCK, span), bf16),
            jax.ShapeDtypeStruct((QUERY_HEADS, tokens), f32),
            jax.ShapeDtypeStruct((tokens, width), bf16),
            jax.ShapeDtypeStruct((tokens, width), bf16),
            jax.ShapeDtypeStruct((tokens, width), bf16),
            jax.ShapeDtypeStruct((tokens, HEAD_SIZE), f32),
            jax.ShapeDtypeStruct((slot_count, QUERY_HEADS, HEAD_SIZE), bf16),
        ],
        compiler_params=pltpu.CompilerParams(
            dimension_semantics=("arbitrary",), vmem_limit_bytes=VMEM_LIMIT
        ),
        cost_estimate=pl.CostEstimate(
            flops=4 * tokens * width * 1536, bytes_accessed=24 << 20, transcendentals=tokens * 32 * 1536
        ),
        name="attend",
    )(meta, slots, queries, *sources, stream, gain)


def place_kernel(slots, rows_ref, send_ref, rows_scr):
    tokens = rows_ref.shape[0]

    def turn(h, _):
        rows_scr[pl.ds(h, tokens, stride=PITCH), :] = rows_ref[
            :, lanes(h * HEAD_SIZE, HEAD_SIZE)
        ].astype(jnp.float32)
        return 0

    lax.fori_loop(0, QUERY_HEADS, turn, 0, unroll=2)
    scatter_rows(slots, rows_scr, send_ref, tokens)


def place(slots, rows, slot_count):
    tokens, _ = rows.shape
    return pl.pallas_call(
        place_kernel,
        grid_spec=pltpu.PrefetchScalarGridSpec(
            num_scalar_prefetch=1,
            grid=(1,),
            in_specs=[whole(rows.shape)],
            out_specs=whole((slot_count, QUERY_HEADS, HEAD_SIZE)),
            scratch_shapes=[pltpu.VMEM((tokens * PITCH, HEAD_SIZE), jnp.float32)],
        ),
        out_shape=jax.ShapeDtypeStruct((slot_count, QUERY_HEADS, HEAD_SIZE), jnp.bfloat16),
        compiler_params=pltpu.CompilerParams(vmem_limit_bytes=VMEM_LIMIT),
        cost_estimate=pl.CostEstimate(flops=0, bytes_accessed=4 << 20, transcendentals=0),
        name="place",
    )(slots, rows)


def attend_back_kernel(
    meta,
    q_hbm,
    grad_hbm,
    att_hbm,
    linv_ref,
    near_hbm,
    far_hbm,
    near_other_hbm,
    far_other_hbm,
    w_hbm,
    dq_ref,
    keep_ref,
    give_ref,
    kv_scr,
    kt_scr,
    q_scr,
    do_scr,
    rd_scr,
    ds_scr,
    dqt_scr,
    w_buf,
    q_ref,
    grad_ref,
    att_ref,
    sems,
    block_sems,
):
    blocks = block_loads(
        meta, (near_hbm, far_hbm, near_other_hbm, far_other_hbm), kv_scr, block_sems
    )
    for copy in blocks:
        copy.start()

    operands = ((q_hbm, q_ref), (grad_hbm, grad_ref), (att_hbm, att_ref))
    loads = [pltpu.make_async_copy(a, b, sems.at[2 + i]) for i, (a, b) in enumerate(operands)]
    for copy in loads:
        copy.start()
    low, high, core, _, _ = bounds(meta)
    count = high - low + 1
    tokens = q_ref.shape[0]
    wide = 2 * tokens
    per_group = HEADS_PER_GROUP * tokens
    octets = HEADS_PER_GROUP // OCTET
    f32, bf16 = jnp.float32, jnp.bfloat16

    def load(group, kb, slot):
        return pltpu.make_async_copy(
            w_hbm.at[pl.ds(group * octets, octets), kb], w_buf.at[slot], sems.at[slot]
        )

    load(0, low, 0).start()
    keep_ref[...] = jnp.zeros_like(keep_ref)
    give_ref[...] = jnp.zeros_like(give_ref)
    for copy in blocks:
        copy.wait()

    def prepare(kb, _):
        rows = pl.ds(pl.multiple_of(kb * KEY_BLOCK, KEY_BLOCK), KEY_BLOCK)
        kt_scr[kb] = kv_scr[rows, 0:256].T
        return 0

    lax.fori_loop(low, high + 1, prepare, 0)
    inverse = jnp.concatenate(
        [linv_ref[...], jnp.zeros((128 - QUERY_HEADS, tokens), f32)], axis=0
    ).T
    ones = jnp.ones((8, HEAD_SIZE), bf16)
    for copy in loads:
        copy.wait()
    for h in range(QUERY_HEADS):
        columns = slice(h * HEAD_SIZE, (h + 1) * HEAD_SIZE)
        rows = slice(h * tokens, (h + 1) * tokens)
        q_scr[rows, :] = q_ref[:, columns]
        scaled = (grad_ref[:, columns].astype(f32) * inverse[:, h : h + 1]).astype(bf16)
        do_scr[rows, :] = scaled
        product = scaled.astype(f32) * att_ref[:, columns].astype(f32)
        head = product.astype(bf16)
        tail = (product - head.astype(f32)).astype(bf16)
        rd_scr[:, rows] = dot32(ones, head, NT) + dot32(ones, tail, NT)

    is_first = jnp.full((128, HEAD_SIZE), core, jnp.int32) == 0

    def one_group(group, _):
        dqt_scr[...] = jnp.zeros_like(dqt_scr)
        base = pl.multiple_of(group * per_group, per_group)
        half = per_group // octets

        def one_block(j, _):
            kb = low + j
            turn = group * count + j
            slot = lax.rem(turn, 2)
            load(group, kb, slot).wait()

            @pl.when(turn + 1 < KEY_VALUE_HEADS * count)
            def _():
                wrap = j + 1 == count
                load(
                    jnp.where(wrap, group + 1, group), low + jnp.where(wrap, 0, j + 1), 1 - slot
                ).start()

            rows = pl.ds(pl.multiple_of(kb * KEY_BLOCK, KEY_BLOCK), KEY_BLOCK)
            value_rows = kv_scr[rows, lanes(256 + group * HEAD_SIZE, HEAD_SIZE)]
            key_cols = kt_scr[kb, pl.ds(pl.multiple_of(group * HEAD_SIZE, HEAD_SIZE), HEAD_SIZE), :]
            for p in range(HEADS_PER_GROUP // 2):
                here = pl.multiple_of(group * per_group + p * wide, wide)
                dp = dot32(value_rows, do_scr[pl.ds(here, wide), :], NT)
                per_octet = OCTET // 2
                c = (p % per_octet) * wide
                w = w_buf[slot, p // per_octet, :, c : c + wide].astype(f32)
                ds = (w * (dp - rd_scr[0:1, pl.ds(here, wide)])).astype(bf16)
                ds_scr[:, p * wide : (p + 1) * wide] = ds
            dqt_scr[...] += dot32(key_cols, ds_scr[...])
            dv = dot32(w_buf[slot, 0], do_scr[pl.ds(base, half), :]) + dot32(
                w_buf[slot, 1], do_scr[pl.ds(base + half, half), :]
            )
            dk = dot32(ds_scr[...], q_scr[pl.ds(base, per_group), :]) * SCALE
            for part, column in ((dk, 0), (dv, 256)):
                columns = lanes(column + group * HEAD_SIZE, HEAD_SIZE)
                keep_ref[kb, :, columns] = jnp.where(is_first, part[:128], part[128:]).astype(bf16)
                give_ref[kb, :, columns] = jnp.where(is_first, part[128:], part[:128]).astype(bf16)
            return 0

        lax.fori_loop(0, count, one_block, 0)
        for h in range(HEADS_PER_GROUP):
            dq = dqt_scr[:, h * tokens : (h + 1) * tokens] * SCALE
            dq_ref[:, lanes(group * per_group + h * HEAD_SIZE, HEAD_SIZE)] = dq.T.astype(bf16)
        return 0

    lax.fori_loop(0, KEY_VALUE_HEADS, one_group, 0)


def attend_back(meta, queries, grads, attended, linv, sources, weights):
    tokens, width = queries.shape
    blocks = 2 * sources[0].shape[0]
    columns = sources[0].shape[2]
    parts = (blocks, 128, columns)
    bf16, f32 = jnp.bfloat16, jnp.float32
    per_group = HEADS_PER_GROUP * tokens
    octets = HEADS_PER_GROUP // OCTET
    span = OCTET * tokens
    vmem, hbm = pl.BlockSpec(memory_space=pltpu.VMEM), pl.BlockSpec(memory_space=pltpu.HBM)
    return pl.pallas_call(
        attend_back_kernel,
        in_specs=[pl.BlockSpec(memory_space=pltpu.SMEM)] + [hbm] * 3 + [vmem] + [hbm] * 5,
        out_specs=[vmem] * 3,
        scratch_shapes=[
            pltpu.VMEM((blocks * KEY_BLOCK, columns), bf16),
            pltpu.VMEM((blocks, columns // 2, KEY_BLOCK), bf16),
            pltpu.VMEM((QUERY_HEADS * tokens, HEAD_SIZE), bf16),
            pltpu.VMEM((QUERY_HEADS * tokens, HEAD_SIZE), bf16),
            pltpu.VMEM((8, QUERY_HEADS * tokens), f32),
            pltpu.VMEM((KEY_BLOCK, per_group), bf16),
            pltpu.VMEM((HEAD_SIZE, per_group), f32),
            pltpu.VMEM((2, octets, KEY_BLOCK, span), bf16),
            pltpu.VMEM((tokens, width), bf16),
            pltpu.VMEM((tokens, width), bf16),
            pltpu.VMEM((tokens, width), bf16),
            pltpu.SemaphoreType.DMA((5,)),
            pltpu.SemaphoreType.DMA((16,)),
        ],
        out_shape=[
            jax.ShapeDtypeStruct((tokens, width), bf16),
            jax.ShapeDtypeStruct(parts, bf16),
            jax.ShapeDtypeStruct(parts, bf16),
        ],
        compiler_params=pltpu.CompilerParams(vmem_limit_bytes=58 << 20),
        cost_estimate=pl.CostEstimate(
            flops=8 * tokens * width * 1536, bytes_accessed=20 << 20, transcendentals=0
        ),
        name="attend_back",
    )(meta, queries, grads, attended, linv, *sources, weights)


def turn_rows(rows_ref, turn_scr, x_scr):
    peers, per_peer = rows_ref.shape[0], rows_ref.shape[1]
    capacity = per_peer // QUERY_HEADS
    count = peers * capacity

    def widen(i, _):
        for c in range(capacity):
            row = rows_ref[i, c * QUERY_HEADS : (c + 1) * QUERY_HEADS, :].astype(jnp.float32)
            turn_scr[pl.ds((i * capacity + c) * PITCH, QUERY_HEADS), :] = row
        return 0

    lax.fori_loop(0, peers, widen, 0, unroll=2)

    def turn(j, _):
        x_scr[:, lanes(j * HEAD_SIZE, HEAD_SIZE)] = turn_scr[
            pl.ds(j, count, stride=PITCH), :
        ].astype(jnp.bfloat16)
        return 0

    lax.fori_loop(0, QUERY_HEADS, turn, 0, unroll=2)


def down_kernel(rows_ref, down_ref, out_ref, turn_scr, x_scr):
    turn_rows(rows_ref, turn_scr, x_scr)
    span = 256

    def part(n, _):
        rows = pl.ds(pl.multiple_of(n * span, span), span)
        out_ref[:, lanes(n * span, span)] = dot32(x_scr[...], down_ref[rows, :], NT)
        return 0

    lax.fori_loop(0, down_ref.shape[0] // span, part, 0)


def down(rows, down_mat):
    peers, per_peer, _ = rows.shape
    hidden_units, width = down_mat.shape
    count = peers * per_peer // QUERY_HEADS
    vmem = pl.BlockSpec(memory_space=pltpu.VMEM)
    return pl.pallas_call(
        down_kernel,
        in_specs=[vmem] * 2,
        out_specs=vmem,
        scratch_shapes=[
            pltpu.VMEM((count * PITCH, HEAD_SIZE), jnp.float32),
            pltpu.VMEM((count, width), jnp.bfloat16),
        ],
        out_shape=jax.ShapeDtypeStruct((count, hidden_units), jnp.float32),
        compiler_params=pltpu.CompilerParams(vmem_limit_bytes=24 << 20),
        cost_estimate=pl.CostEstimate(
            flops=2 * count * width * hidden_units, bytes_accessed=11 << 20, transcendentals=0
        ),
        name="down",
    )(rows, down_mat)


def expert_kernel(
    rows_ref,
    inner_grad_ref,
    gate_hbm,
    up_hbm,
    out_ref,
    gate_ref,
    up_ref,
    turn_scr,
    x_scr,
    da_scr,
    db_scr,
    score_scr,
    sems,
):
    bf16 = jnp.bfloat16
    peers, per_peer = rows_ref.shape[0], rows_ref.shape[1]
    count = x_scr.shape[0]
    hidden_units = gate_ref.shape[1]
    capacity = count // peers

    span = 256
    parts = hidden_units // span

    def load(n):
        columns = lanes(n * span, span)
        return (
            pltpu.make_async_copy(gate_hbm.at[:, columns], gate_ref.at[:, columns], sems.at[0, n]),
            pltpu.make_async_copy(up_hbm.at[:, columns], up_ref.at[:, columns], sems.at[1, n]),
        )

    for n in range(parts):
        for copy in load(n):
            copy.start()
    turn_rows(rows_ref, turn_scr, x_scr)
    score_scr[...] = jnp.zeros_like(score_scr)

    def hidden_part(n, _):
        for copy in load(n):
            copy.wait()
        columns = lanes(n * span, span)
        a = dot32(x_scr[...], gate_ref[:, columns])
        b = dot32(x_scr[...], up_ref[:, columns])
        u = inner_grad_ref[:, columns]
        sig = 1.0 / (1.0 + jnp.exp(-a))
        act = a * sig
        product = u * b
        scores = jnp.sum(product * act, axis=1, keepdims=True)
        score_scr[0:count, :] += jnp.broadcast_to(scores, (count, HEAD_SIZE))
        da_scr[:, columns] = (product * sig * (1.0 + a * (1.0 - sig))).astype(bf16)
        db_scr[:, columns] = (u * act).astype(bf16)
        return 0

    lax.fori_loop(0, parts, hidden_part, 0)

    def grad_part(j, _):
        rows = pl.ds(pl.multiple_of(j * span, span), span)
        d = dot32(da_scr[...], gate_ref[rows, :], NT) + dot32(db_scr[...], up_ref[rows, :], NT)
        turn_scr[pl.ds(2 * j, count, stride=PITCH), :] = d[:, :HEAD_SIZE]
        turn_scr[pl.ds(2 * j + 1, count, stride=PITCH), :] = d[:, HEAD_SIZE:]
        return 0

    lax.fori_loop(0, QUERY_HEADS // 2, grad_part, 0)

    def narrow(i, _):
        for c in range(capacity):
            row = turn_scr[pl.ds((i * capacity + c) * PITCH, QUERY_HEADS), :]
            out_ref[i, c * QUERY_HEADS : (c + 1) * QUERY_HEADS, :] = row.astype(bf16)
        out_ref[i, per_peer : per_peer + 8, :] = score_scr[pl.ds(capacity * i, 8), :].astype(bf16)
        return 0

    lax.fori_loop(0, peers, narrow, 0, unroll=2)


def expert(rows, inner_grad, gate_mat, up_mat):
    peers, per_peer, _ = rows.shape
    count = inner_grad.shape[0]
    width, hidden_units = gate_mat.shape
    f32, bf16 = jnp.float32, jnp.bfloat16
    return pl.pallas_call(
        expert_kernel,
        in_specs=[pl.BlockSpec(memory_space=pltpu.VMEM)] * 2
        + [pl.BlockSpec(memory_space=pltpu.HBM)] * 2,
        out_specs=pl.BlockSpec(memory_space=pltpu.VMEM),
        scratch_shapes=[
            pltpu.VMEM((width, hidden_units), bf16),
            pltpu.VMEM((width, hidden_units), bf16),
            pltpu.VMEM((count * PITCH, HEAD_SIZE), f32),
            pltpu.VMEM((count, width), bf16),
            pltpu.VMEM((count, hidden_units), bf16),
            pltpu.VMEM((count, hidden_units), bf16),
            pltpu.VMEM((count + 16, HEAD_SIZE), f32),
            pltpu.SemaphoreType.DMA((2, hidden_units // 256)),
        ],
        out_shape=jax.ShapeDtypeStruct((peers, per_peer + 8, HEAD_SIZE), bf16),
        compiler_params=pltpu.CompilerParams(vmem_limit_bytes=50 << 20),
        cost_estimate=pl.CostEstimate(
            flops=8 * count * width * hidden_units, bytes_accessed=20 << 20, transcendentals=count * hidden_units
        ),
        name="expert",
    )(rows, inner_grad, gate_mat, up_mat)


def combine_kernel(
    ids_smem,
    ranks,
    gates_smem,
    back_ref,
    gates_ref,
    ids_ref,
    hid_ref,
    norm_ref,
    rms_ref,
    og_ref,
    gain_ref,
    router_ref,
    res_ref,
    part_ref,
    rows_scr,
    score_scr,
    dn_scr,
    acc_scr,
):
    f32, bf16 = jnp.float32, jnp.bfloat16
    tokens = hid_ref.shape[0]
    capacity = 3
    per_peer = capacity * QUERY_HEADS

    def pick(t, _):
        total = None
        scores = []
        for k in range(2):
            e = ids_smem[2 * t + k]
            c = ranks[2 * t + k]
            start = pl.multiple_of(c * QUERY_HEADS, QUERY_HEADS)
            row = back_ref[e, pl.ds(start, QUERY_HEADS), :].astype(f32) * gates_smem[2 * t + k]
            total = row if total is None else total + row
            tail = back_ref[e, per_peer : per_peer + 8, :].astype(f32)
            which = lax.broadcasted_iota(jnp.int32, tail.shape, 0) == c
            scores.append(jnp.sum(jnp.where(which, tail, 0.0), axis=0, keepdims=True))
        rows_scr[pl.ds(t * PITCH, QUERY_HEADS), :] = total
        score_scr[pl.ds(t, 1), :] = scores[0] - scores[1]
        return 0

    lax.fori_loop(0, tokens, pick, 0, unroll=8)
    first = gates_ref[:, 0:1]
    value = first * (1.0 - first) * score_scr[...]
    lane = lax.broadcasted_iota(jnp.int32, (tokens, HEAD_SIZE), 1)
    d_logits = jnp.where(lane == ids_ref[:, 0:1], value, 0.0) - jnp.where(
        lane == ids_ref[:, 1:2], value, 0.0
    )
    d_logits = d_logits.astype(bf16)
    acc_scr[...] = jnp.zeros_like(acc_scr)

    def gather(h, _):
        columns = lanes(h * HEAD_SIZE, HEAD_SIZE)
        rows = pl.ds(pl.multiple_of(h * HEAD_SIZE, HEAD_SIZE), HEAD_SIZE)
        dn = rows_scr[pl.ds(h, tokens, stride=PITCH), :] + dot32(
            d_logits, router_ref[rows, :], NT
        )
        scaled = dn * gain_ref[:, columns]
        dn_scr[:, columns] = scaled
        acc_scr[...] += hid_ref[:, columns].astype(f32) * scaled
        part_ref[rows, :] = dot32(norm_ref[:, columns], d_logits, TN).astype(bf16)
        return 0

    lax.fori_loop(0, QUERY_HEADS, gather, 0, unroll=2)
    r = rms_ref[...]
    mean = jnp.sum(acc_scr[...], axis=1, keepdims=True) * (1.0 / (QUERY_HEADS * HEAD_SIZE))
    pull = r * r * r * mean

    def finish(h, _):
        columns = lanes(h * HEAD_SIZE, HEAD_SIZE)
        res = og_ref[:, columns].astype(f32) + r * dn_scr[:, columns] - hid_ref[:, columns].astype(f32) * pull
        res_ref[:, columns] = res.astype(bf16)
        return 0

    lax.fori_loop(0, QUERY_HEADS, finish, 0, unroll=2)


def combine(ranks, gates, ids, back, hidden, normed, inv_rms, out_grad, gain, router):
    tokens, width = hidden.shape
    experts = router.shape[1]
    f32, bf16 = jnp.float32, jnp.bfloat16
    return pl.pallas_call(
        combine_kernel,
        in_specs=[pl.BlockSpec(memory_space=pltpu.SMEM)] * 3
        + [pl.BlockSpec(memory_space=pltpu.VMEM)] * 9,
        out_specs=[pl.BlockSpec(memory_space=pltpu.VMEM)] * 2,
        scratch_shapes=[
            pltpu.VMEM((tokens * PITCH, HEAD_SIZE), f32),
            pltpu.VMEM((tokens, HEAD_SIZE), f32),
            pltpu.VMEM((tokens, width), f32),
            pltpu.VMEM((tokens, HEAD_SIZE), f32),
        ],
        out_shape=[
            jax.ShapeDtypeStruct((tokens, width), bf16),
            jax.ShapeDtypeStruct((width, experts), bf16),
        ],
        compiler_params=pltpu.CompilerParams(vmem_limit_bytes=50 << 20),
        cost_estimate=pl.CostEstimate(
            flops=4 * tokens * width * experts, bytes_accessed=9 << 20, transcendentals=0
        ),
        name="combine",
    )(ids.reshape(-1), ranks, gates.reshape(-1), back, gates, ids, hidden, normed, inv_rms, out_grad, gain, router)


def swap_cores(array):
    return lax.ppermute(array, CORE, [(0, 1), (1, 0)])


def exchange(array, axes):
    return lax.all_to_all(array, axes, split_axis=0, concat_axis=0, tiled=True)


def layer(
    queries,
    keys,
    values,
    stream,
    norm_gain,
    router_weight,
    gate_weight,
    up_weight,
    down_weight,
    doc_lengths,
    expert_ids,
    out_grad,
):
    token_rows = queries.shape[1]
    both = jnp.concatenate([keys[0], values[0]], axis=1)
    near = exchange(jnp.broadcast_to(both[None], (lax.axis_size("blk_0"), *both.shape)), "blk_0")
    far = lax.ppermute(near, "blk_1", [(0, 1), (1, 0)])
    near_other = swap_cores(near)
    sources = (near, far, near_other, swap_cores(far))

    meta = jnp.concatenate([lax.axis_index(GRP_BLK).astype(jnp.int32)[None], doc_lengths[0]])
    experts = router_weight.shape[1]
    chosen_ids = expert_ids[0]
    top_count = chosen_ids.shape[1]
    capacity = max(2, 3 * token_rows * top_count // (2 * experts))
    flat_ids = chosen_ids.reshape(-1)
    same = flat_ids[:, None] == flat_ids[None, :]
    order = jnp.arange(flat_ids.shape[0], dtype=jnp.int32)
    slot_rank = jnp.sum((same & (order[None, :] < order[:, None])).astype(jnp.int32), axis=1, dtype=jnp.int32)
    slots = flat_ids * capacity + slot_rank
    slot_count = experts * capacity

    send_grads = place(slots, out_grad[0], slot_count)
    got_grads = exchange(send_grads.reshape(experts, -1, HEAD_SIZE), GRP_BLK)

    weights, linv, attended, hidden, normed, inv_rms, send_rows = attend(
        meta, slots, queries[0], sources, stream[0], norm_gain[None], slot_count
    )
    got_rows = exchange(send_rows.reshape(experts, -1, HEAD_SIZE), GRP_BLK)

    logits = jnp.dot(normed, router_weight, preferred_element_type=jnp.float32)
    hits = chosen_ids[:, :, None] == jnp.arange(experts, dtype=jnp.int32)[None, None, :]
    chosen = jnp.sum(jnp.where(hits, logits[:, None, :], 0.0), axis=-1)
    first_gate = jax.nn.sigmoid(chosen[:, 0] - chosen[:, 1])
    gates = jnp.stack([first_gate, 1.0 - first_gate], axis=1)

    inner_grad = down(got_grads, down_weight[0])
    back = exchange(expert(got_rows, inner_grad, gate_weight[0], up_weight[0]), GRP_BLK)
    residual_gradient, router_parts = combine(
        slot_rank, gates, chosen_ids, back, hidden, normed, inv_rms, out_grad[0], norm_gain[None], router_weight
    )
    got_parts = exchange(router_parts.reshape(experts, -1, experts), GRP_BLK)
    query_grad, keep, give = attend_back(
        meta, queries[0], residual_gradient, attended, linv, sources, weights
    )
    pair_sum = (keep.astype(jnp.float32) + swap_cores(give).astype(jnp.float32)).astype(jnp.bfloat16)
    summed = jnp.sum(exchange(pair_sum, ZX).astype(jnp.float32), axis=0).astype(jnp.bfloat16)
    router_grad = jnp.sum(got_parts.astype(jnp.float32), axis=0)
    half = KEY_VALUE_HEADS * HEAD_SIZE
    return (
        query_grad[None],
        summed[None, :, :half],
        summed[None, :, half:],
        residual_gradient[None],
        router_grad,
    )


def solution(mesh):
    split = Mesh(mesh.devices.reshape(2, 4, 4, 2, 2), ("grp_0", "grp_1", "blk_0", "blk_1", "blk_2"))
    return jax.shard_map(
        layer,
        mesh=split,
        in_specs=(
            P(GRP, BLK, None),
            P(GRP, BLK, None),
            P(GRP, BLK, None),
            P(GRP, BLK, None),
            P(),
            P(),
            P(GRP_BLK, None, None),
            P(GRP_BLK, None, None),
            P(GRP_BLK, None, None),
            P(GRP, None),
            P(GRP, BLK, None),
            P(GRP, BLK, None),
        ),
        out_specs=(
            P(GRP, BLK, None),
            P(GRP, BLK, None),
            P(GRP, BLK, None),
            P(GRP, BLK, None),
            P(GRP_BLK, None),
        ),
        check_vma=False,
    )
```

```python
import math

import jax
import jax.numpy as jnp
from jax import lax
from jax.experimental import pallas as pl
from jax.experimental.pallas import tpu as pltpu
from jax.sharding import Mesh
from jax.sharding import PartitionSpec as P


HEAD_SIZE = 128
QUERY_HEADS = 32
KEY_VALUE_HEADS = 2
HEADS_PER_GROUP = QUERY_HEADS // KEY_VALUE_HEADS
BLK = ("blk_0", "blk_1", "blk_2")
GRP_BLK = ("grp_0", "grp_1", "blk_0", "blk_1", "blk_2")
GRP = ("grp_0", "grp_1")
ZX = ("blk_0", "blk_1")
CORE = "blk_2"

NEGATIVE_HUGE = -1e30
EPSILON = 1e-06
SCALE = HEAD_SIZE ** (-0.5)
KEY_BLOCK = 256
OCTET = 8
VMEM_LIMIT = 60 * 1024 * 1024
PITCH = QUERY_HEADS + 1

NT = (((1,), (1,)), ((), ()))
TN = (((0,), (0,)), ((), ()))


def dot32(a, b, dims=(((1,), (0,)), ((), ()))):
    return lax.dot_general(a, b, dims, preferred_element_type=jnp.float32)


def lanes(start, size):
    return pl.ds(pl.multiple_of(start, 128), size)


def bounds(meta):
    place = meta[0] & 15
    first_query = place * 128
    ends = [meta[1]]
    for d in range(1, 4):
        ends.append(ends[-1] + meta[1 + d])
    start = jnp.int32(0)
    for end in ends:
        start = jnp.where(end <= first_query, end, start)
    return start // KEY_BLOCK, (first_query + 127) // KEY_BLOCK, meta[0] & 1, first_query, ends


def block_loads(meta, sources, kv_scr, sems):
    core, x = meta[0] & 1, (meta[0] >> 1) & 1
    copies = []
    for i, source in enumerate(sources):
        for z in range(source.shape[0]):
            block = (z * 2 + ((x + i) & 1)) * 2 + ((core + i // 2) & 1)
            rows = pl.ds(pl.multiple_of(block * 128, 128), 128)
            copies.append(
                pltpu.make_async_copy(
                    source.at[z], kv_scr.at[rows, :], sems.at[i * source.shape[0] + z]
                )
            )
    return copies


def attend_kernel(
    meta,
    slots,
    q_ref,
    near_hbm,
    far_hbm,
    near_other_hbm,
    far_other_hbm,
    stream_ref,
    gain_ref,
    w_ref,
    linv_ref,
    att_ref,
    hid_ref,
    norm_ref,
    rms_ref,
    send_ref,
    kv_scr,
    vt_scr,
    bias_scr,
    s_scr,
    ot_scr,
    ss_scr,
    rows_scr,
    sems,
):
    octet = pl.program_id(0)
    group = octet // (HEADS_PER_GROUP // OCTET)
    low, high, _, first_query, ends = bounds(meta)
    tokens = q_ref.shape[0]
    factor = SCALE * math.log2(math.e)

    @pl.when(octet == 0)
    def _():
        sources = (near_hbm, far_hbm, near_other_hbm, far_other_hbm)
        copies = block_loads(meta, sources, kv_scr, sems)
        for copy in copies:
            copy.start()
        ss_scr[...] = jnp.zeros_like(ss_scr)
        query = first_query + lax.broadcasted_iota(jnp.int32, (KEY_BLOCK, tokens), 1)
        start = jnp.zeros((KEY_BLOCK, tokens), jnp.int32)
        for d in range(4):
            start = jnp.maximum(start, jnp.where(query >= ends[d], ends[d], 0))

        for copy in copies:
            copy.wait()

        def prepare(kb, _):
            rows = pl.ds(pl.multiple_of(kb * KEY_BLOCK, KEY_BLOCK), KEY_BLOCK)
            vt_scr[kb] = kv_scr[rows, 256:512].T
            key = kb * KEY_BLOCK + lax.broadcasted_iota(jnp.int32, (KEY_BLOCK, tokens), 0)
            seen = (key <= query) & (key >= start)
            bias_scr[kb] = jnp.where(seen, 0.0, NEGATIVE_HUGE)
            return 0

        lax.fori_loop(low, high + 1, prepare, 0)

    pairs = OCTET // 2
    wide = 2 * tokens

    def score(kb, tops):
        rows = pl.ds(pl.multiple_of(kb * KEY_BLOCK, KEY_BLOCK), KEY_BLOCK)
        key_rows = kv_scr[rows, lanes(group * HEAD_SIZE, HEAD_SIZE)]
        bias = bias_scr[kb]
        bias = jnp.concatenate([bias, bias], axis=1)
        new = []
        for p in range(pairs):
            c = 2 * p * HEAD_SIZE
            both = jnp.concatenate(
                [q_ref[:, c : c + HEAD_SIZE], q_ref[:, c + HEAD_SIZE : c + 2 * HEAD_SIZE]], axis=0
            )
            s = dot32(key_rows, both, NT) + bias
            s_scr[kb, :, p * wide : (p + 1) * wide] = s
            new.append(jnp.maximum(tops[p], jnp.max(s.reshape(-1, 8, wide), axis=0)))
        return tuple(new)

    tops = lax.fori_loop(
        low, high + 1, score, tuple(jnp.full((8, wide), NEGATIVE_HUGE, jnp.float32) for _ in range(pairs))
    )
    tops = tuple(jnp.max(t, axis=0, keepdims=True) * factor for t in tops)
    ot_scr[...] = jnp.zeros_like(ot_scr)

    def weigh(kb, sums):
        value_cols = vt_scr[kb, pl.ds(pl.multiple_of(group * HEAD_SIZE, HEAD_SIZE), HEAD_SIZE), :]
        new = []
        for p in range(pairs):
            span = slice(p * wide, (p + 1) * wide)
            w = jnp.exp2(s_scr[kb, :, span] * factor - tops[p])
            new.append(sums[p] + jnp.sum(w.reshape(-1, 8, wide), axis=0))
            low_w = w.astype(jnp.bfloat16)
            w_ref[0, kb, :, span] = low_w
            ot_scr[:, span] += dot32(value_cols, low_w)
        return tuple(new)

    sums = lax.fori_loop(
        low, high + 1, weigh, tuple(jnp.zeros((8, wide), jnp.float32) for _ in range(pairs))
    )
    for p in range(pairs):
        inverse = 1.0 / jnp.sum(sums[p], axis=0, keepdims=True)
        mixed = ot_scr[:, p * wide : (p + 1) * wide] * inverse
        for i in range(2):
            h = 2 * p + i
            linv_ref[h : h + 1, :] = inverse[:, i * tokens : (i + 1) * tokens]
            columns = lanes((octet * OCTET + h) * HEAD_SIZE, HEAD_SIZE)
            att = mixed[:, i * tokens : (i + 1) * tokens].T.astype(jnp.bfloat16)
            att_ref[:, columns] = att
            hid = (stream_ref[:, columns].astype(jnp.float32) + att.astype(jnp.float32)).astype(
                jnp.bfloat16
            )
            hid_ref[:, columns] = hid
            wide_hid = hid.astype(jnp.float32)
            ss_scr[...] += wide_hid * wide_hid

    @pl.when(octet == pl.num_programs(0) - 1)
    def _():
        mean = jnp.sum(ss_scr[...], axis=1, keepdims=True) * (1.0 / (QUERY_HEADS * HEAD_SIZE))
        inv_rms = jnp.broadcast_to(lax.rsqrt(mean + EPSILON), (tokens, HEAD_SIZE))
        rms_ref[...] = inv_rms

        def norm(h, _):
            columns = lanes(h * HEAD_SIZE, HEAD_SIZE)
            n = (hid_ref[:, columns].astype(jnp.float32) * inv_rms * gain_ref[:, columns]).astype(
                jnp.bfloat16
            )
            norm_ref[:, columns] = n
            rows_scr[pl.ds(h, tokens, stride=PITCH), :] = n.astype(jnp.float32)
            return 0

        lax.fori_loop(0, QUERY_HEADS, norm, 0, unroll=2)
        scatter_rows(slots, rows_scr, send_ref, tokens)


def scatter_rows(slots, rows_scr, send_ref, tokens):
    def send(t, _):
        row = rows_scr[pl.ds(t * PITCH, QUERY_HEADS), :].astype(jnp.bfloat16)
        send_ref[slots[2 * t]] = row
        send_ref[slots[2 * t + 1]] = row
        return 0

    lax.fori_loop(0, tokens, send, 0, unroll=8)


def whole(shape):
    zero = (0,) * len(shape)
    return pl.BlockSpec(shape, lambda *_: zero)


def attend(meta, slots, queries, sources, stream, gain, slot_count):
    tokens, width = queries.shape
    octets = QUERY_HEADS // OCTET
    blocks = 2 * sources[0].shape[0]
    columns = sources[0].shape[2]
    span = OCTET * tokens
    bf16, f32 = jnp.bfloat16, jnp.float32
    return pl.pallas_call(
        attend_kernel,
        grid_spec=pltpu.PrefetchScalarGridSpec(
            num_scalar_prefetch=2,
            grid=(octets,),
            in_specs=[
                pl.BlockSpec((tokens, OCTET * HEAD_SIZE), lambda o, *_: (0, o)),
                *[pl.BlockSpec(memory_space=pltpu.HBM)] * 4,
                whole(stream.shape),
                whole((1, width)),
            ],
            out_specs=[
                pl.BlockSpec((1, blocks, KEY_BLOCK, span), lambda o, *_: (o, 0, 0, 0)),
                pl.BlockSpec((OCTET, tokens), lambda o, *_: (o, 0)),
                whole((tokens, width)),
                whole((tokens, width)),
                whole((tokens, width)),
                whole((tokens, HEAD_SIZE)),
                whole((slot_count, QUERY_HEADS, HEAD_SIZE)),
            ],
            scratch_shapes=[
                pltpu.VMEM((blocks * KEY_BLOCK, columns), bf16),
                pltpu.VMEM((blocks, columns // 2, KEY_BLOCK), bf16),
                pltpu.VMEM((blocks, KEY_BLOCK, tokens), f32),
                pltpu.VMEM((blocks, KEY_BLOCK, span), f32),
                pltpu.VMEM((HEAD_SIZE, span), f32),
                pltpu.VMEM((tokens, HEAD_SIZE), f32),
                pltpu.VMEM((tokens * PITCH, HEAD_SIZE), f32),
                pltpu.SemaphoreType.DMA((16,)),
            ],
        ),
        out_shape=[
            jax.ShapeDtypeStruct((octets, blocks, KEY_BLOCK, span), bf16),
            jax.ShapeDtypeStruct((QUERY_HEADS, tokens), f32),
            jax.ShapeDtypeStruct((tokens, width), bf16),
            jax.ShapeDtypeStruct((tokens, width), bf16),
            jax.ShapeDtypeStruct((tokens, width), bf16),
            jax.ShapeDtypeStruct((tokens, HEAD_SIZE), f32),
            jax.ShapeDtypeStruct((slot_count, QUERY_HEADS, HEAD_SIZE), bf16),
        ],
        compiler_params=pltpu.CompilerParams(
            dimension_semantics=("arbitrary",), vmem_limit_bytes=VMEM_LIMIT
        ),
        cost_estimate=pl.CostEstimate(
            flops=4 * tokens * width * 1536, bytes_accessed=24 << 20, transcendentals=tokens * 32 * 1536
        ),
        name="attend",
    )(meta, slots, queries, *sources, stream, gain)


def place_kernel(slots, rows_ref, send_ref, rows_scr):
    tokens = rows_ref.shape[0]

    def turn(h, _):
        rows_scr[pl.ds(h, tokens, stride=PITCH), :] = rows_ref[
            :, lanes(h * HEAD_SIZE, HEAD_SIZE)
        ].astype(jnp.float32)
        return 0

    lax.fori_loop(0, QUERY_HEADS, turn, 0, unroll=2)
    scatter_rows(slots, rows_scr, send_ref, tokens)


def place(slots, rows, slot_count):
    tokens, _ = rows.shape
    return pl.pallas_call(
        place_kernel,
        grid_spec=pltpu.PrefetchScalarGridSpec(
            num_scalar_prefetch=1,
            grid=(1,),
            in_specs=[whole(rows.shape)],
            out_specs=whole((slot_count, QUERY_HEADS, HEAD_SIZE)),
            scratch_shapes=[pltpu.VMEM((tokens * PITCH, HEAD_SIZE), jnp.float32)],
        ),
        out_shape=jax.ShapeDtypeStruct((slot_count, QUERY_HEADS, HEAD_SIZE), jnp.bfloat16),
        compiler_params=pltpu.CompilerParams(vmem_limit_bytes=VMEM_LIMIT),
        cost_estimate=pl.CostEstimate(flops=0, bytes_accessed=4 << 20, transcendentals=0),
        name="place",
    )(slots, rows)


def attend_back_kernel(
    meta,
    q_hbm,
    grad_hbm,
    att_hbm,
    linv_ref,
    near_hbm,
    far_hbm,
    near_other_hbm,
    far_other_hbm,
    w_hbm,
    dq_ref,
    keep_ref,
    give_ref,
    kv_scr,
    kt_scr,
    q_scr,
    do_scr,
    rd_scr,
    ds_scr,
    dqt_scr,
    w_buf,
    q_ref,
    grad_ref,
    att_ref,
    sems,
    block_sems,
):
    blocks = block_loads(
        meta, (near_hbm, far_hbm, near_other_hbm, far_other_hbm), kv_scr, block_sems
    )
    for copy in blocks:
        copy.start()

    operands = ((q_hbm, q_ref), (grad_hbm, grad_ref), (att_hbm, att_ref))
    loads = [pltpu.make_async_copy(a, b, sems.at[2 + i]) for i, (a, b) in enumerate(operands)]
    for copy in loads:
        copy.start()
    low, high, core, _, _ = bounds(meta)
    count = high - low + 1
    tokens = q_ref.shape[0]
    wide = 2 * tokens
    per_group = HEADS_PER_GROUP * tokens
    octets = HEADS_PER_GROUP // OCTET
    f32, bf16 = jnp.float32, jnp.bfloat16

    def load(group, kb, slot):
        return pltpu.make_async_copy(
            w_hbm.at[pl.ds(group * octets, octets), kb], w_buf.at[slot], sems.at[slot]
        )

    load(0, low, 0).start()
    keep_ref[...] = jnp.zeros_like(keep_ref)
    give_ref[...] = jnp.zeros_like(give_ref)
    for copy in blocks:
        copy.wait()

    def prepare(kb, _):
        rows = pl.ds(pl.multiple_of(kb * KEY_BLOCK, KEY_BLOCK), KEY_BLOCK)
        kt_scr[kb] = kv_scr[rows, 0:256].T
        return 0

    lax.fori_loop(low, high + 1, prepare, 0)
    inverse = jnp.concatenate(
        [linv_ref[...], jnp.zeros((128 - QUERY_HEADS, tokens), f32)], axis=0
    ).T
    lane = lax.broadcasted_iota(jnp.int32, (HEAD_SIZE, HEAD_SIZE), 1)
    dots = jnp.zeros((tokens, HEAD_SIZE), f32)
    for copy in loads:
        copy.wait()
    for h in range(QUERY_HEADS):
        columns = slice(h * HEAD_SIZE, (h + 1) * HEAD_SIZE)
        rows = slice(h * tokens, (h + 1) * tokens)
        q_scr[rows, :] = q_ref[:, columns]
        scaled = (grad_ref[:, columns].astype(f32) * inverse[:, h : h + 1]).astype(bf16)
        do_scr[rows, :] = scaled
        product = scaled.astype(f32) * att_ref[:, columns].astype(f32)
        head = product.astype(bf16)
        tail = (product - head.astype(f32)).astype(bf16)
        ones = jnp.where(lane == h, 1.0, 0.0).astype(bf16)
        dots = dots + dot32(head, ones) + dot32(tail, ones)
    dots = dots.T
    for h in range(QUERY_HEADS):
        rd_scr[0:1, h * tokens : (h + 1) * tokens] = dots[h : h + 1, :]

    is_first = jnp.full((128, HEAD_SIZE), core, jnp.int32) == 0

    def one_group(group, _):
        dqt_scr[...] = jnp.zeros_like(dqt_scr)
        base = pl.multiple_of(group * per_group, per_group)
        half = per_group // octets

        def one_block(j, _):
            kb = low + j
            turn = group * count + j
            slot = lax.rem(turn, 2)
            load(group, kb, slot).wait()

            @pl.when(turn + 1 < KEY_VALUE_HEADS * count)
            def _():
                wrap = j + 1 == count
                load(
                    jnp.where(wrap, group + 1, group), low + jnp.where(wrap, 0, j + 1), 1 - slot
                ).start()

            rows = pl.ds(pl.multiple_of(kb * KEY_BLOCK, KEY_BLOCK), KEY_BLOCK)
            value_rows = kv_scr[rows, lanes(256 + group * HEAD_SIZE, HEAD_SIZE)]
            key_cols = kt_scr[kb, pl.ds(pl.multiple_of(group * HEAD_SIZE, HEAD_SIZE), HEAD_SIZE), :]
            for p in range(HEADS_PER_GROUP // 2):
                here = pl.multiple_of(group * per_group + p * wide, wide)
                dp = dot32(value_rows, do_scr[pl.ds(here, wide), :], NT)
                per_octet = OCTET // 2
                c = (p % per_octet) * wide
                w = w_buf[slot, p // per_octet, :, c : c + wide].astype(f32)
                ds = (w * (dp - rd_scr[0:1, pl.ds(here, wide)])).astype(bf16)
                ds_scr[:, p * wide : (p + 1) * wide] = ds
            dqt_scr[...] += dot32(key_cols, ds_scr[...])
            dv = dot32(w_buf[slot, 0], do_scr[pl.ds(base, half), :]) + dot32(
                w_buf[slot, 1], do_scr[pl.ds(base + half, half), :]
            )
            dk = dot32(ds_scr[...], q_scr[pl.ds(base, per_group), :]) * SCALE
            for part, column in ((dk, 0), (dv, 256)):
                columns = lanes(column + group * HEAD_SIZE, HEAD_SIZE)
                keep_ref[kb, :, columns] = jnp.where(is_first, part[:128], part[128:]).astype(bf16)
                give_ref[kb, :, columns] = jnp.where(is_first, part[128:], part[:128]).astype(bf16)
            return 0

        lax.fori_loop(0, count, one_block, 0)
        for h in range(HEADS_PER_GROUP):
            dq = dqt_scr[:, h * tokens : (h + 1) * tokens] * SCALE
            dq_ref[:, lanes(group * per_group + h * HEAD_SIZE, HEAD_SIZE)] = dq.T.astype(bf16)
        return 0

    lax.fori_loop(0, KEY_VALUE_HEADS, one_group, 0)


def attend_back(meta, queries, grads, attended, linv, sources, weights):
    tokens, width = queries.shape
    blocks = 2 * sources[0].shape[0]
    columns = sources[0].shape[2]
    parts = (blocks, 128, columns)
    bf16, f32 = jnp.bfloat16, jnp.float32
    per_group = HEADS_PER_GROUP * tokens
    octets = HEADS_PER_GROUP // OCTET
    span = OCTET * tokens
    vmem, hbm = pl.BlockSpec(memory_space=pltpu.VMEM), pl.BlockSpec(memory_space=pltpu.HBM)
    return pl.pallas_call(
        attend_back_kernel,
        in_specs=[pl.BlockSpec(memory_space=pltpu.SMEM)] + [hbm] * 3 + [vmem] + [hbm] * 5,
        out_specs=[vmem] * 3,
        scratch_shapes=[
            pltpu.VMEM((blocks * KEY_BLOCK, columns), bf16),
            pltpu.VMEM((blocks, columns // 2, KEY_BLOCK), bf16),
            pltpu.VMEM((QUERY_HEADS * tokens, HEAD_SIZE), bf16),
            pltpu.VMEM((QUERY_HEADS * tokens, HEAD_SIZE), bf16),
            pltpu.VMEM((8, QUERY_HEADS * tokens), f32),
            pltpu.VMEM((KEY_BLOCK, per_group), bf16),
            pltpu.VMEM((HEAD_SIZE, per_group), f32),
            pltpu.VMEM((2, octets, KEY_BLOCK, span), bf16),
            pltpu.VMEM((tokens, width), bf16),
            pltpu.VMEM((tokens, width), bf16),
            pltpu.VMEM((tokens, width), bf16),
            pltpu.SemaphoreType.DMA((5,)),
            pltpu.SemaphoreType.DMA((16,)),
        ],
        out_shape=[
            jax.ShapeDtypeStruct((tokens, width), bf16),
            jax.ShapeDtypeStruct(parts, bf16),
            jax.ShapeDtypeStruct(parts, bf16),
        ],
        compiler_params=pltpu.CompilerParams(vmem_limit_bytes=58 << 20),
        cost_estimate=pl.CostEstimate(
            flops=8 * tokens * width * 1536, bytes_accessed=20 << 20, transcendentals=0
        ),
        name="attend_back",
    )(meta, queries, grads, attended, linv, *sources, weights)


def turn_rows(rows_ref, turn_scr, x_scr, between=lambda: None):
    peers, per_peer = rows_ref.shape[0], rows_ref.shape[1]
    capacity = per_peer // QUERY_HEADS
    count = peers * capacity

    def widen(i, _):
        for c in range(capacity):
            row = rows_ref[i, c * QUERY_HEADS : (c + 1) * QUERY_HEADS, :].astype(jnp.float32)
            turn_scr[pl.ds((i * capacity + c) * PITCH, QUERY_HEADS), :] = row
        return 0

    lax.fori_loop(0, peers, widen, 0, unroll=4)
    between()

    def turn(j, _):
        x_scr[:, lanes(j * HEAD_SIZE, HEAD_SIZE)] = turn_scr[
            pl.ds(j, count, stride=PITCH), :
        ].astype(jnp.bfloat16)
        return 0

    lax.fori_loop(0, QUERY_HEADS, turn, 0, unroll=2)


def down_kernel(rows_ref, down_ref, out_ref, turn_scr, x_scr):
    turn_rows(rows_ref, turn_scr, x_scr)
    span = 256

    def part(n, _):
        rows = pl.ds(pl.multiple_of(n * span, span), span)
        out_ref[:, lanes(n * span, span)] = dot32(x_scr[...], down_ref[rows, :], NT)
        return 0

    lax.fori_loop(0, down_ref.shape[0] // span, part, 0)


def down(rows, down_mat):
    peers, per_peer, _ = rows.shape
    hidden_units, width = down_mat.shape
    count = peers * per_peer // QUERY_HEADS
    vmem = pl.BlockSpec(memory_space=pltpu.VMEM)
    return pl.pallas_call(
        down_kernel,
        in_specs=[vmem] * 2,
        out_specs=vmem,
        scratch_shapes=[
            pltpu.VMEM((count * PITCH, HEAD_SIZE), jnp.float32),
            pltpu.VMEM((count, width), jnp.bfloat16),
        ],
        out_shape=jax.ShapeDtypeStruct((count, hidden_units), jnp.float32),
        compiler_params=pltpu.CompilerParams(vmem_limit_bytes=24 << 20),
        cost_estimate=pl.CostEstimate(
            flops=2 * count * width * hidden_units, bytes_accessed=11 << 20, transcendentals=0
        ),
        name="down",
    )(rows, down_mat)


def expert_kernel(
    rows_ref,
    inner_grad_ref,
    gate_hbm,
    up_hbm,
    out_ref,
    gate_ref,
    up_ref,
    turn_scr,
    x_scr,
    da_scr,
    db_scr,
    score_scr,
    sems,
):
    bf16 = jnp.bfloat16
    peers, per_peer = rows_ref.shape[0], rows_ref.shape[1]
    count = x_scr.shape[0]
    hidden_units = gate_ref.shape[1]
    capacity = count // peers

    span = 256
    parts = hidden_units // span

    def load(n):
        columns = lanes(n * span, span)
        return (
            pltpu.make_async_copy(gate_hbm.at[:, columns], gate_ref.at[:, columns], sems.at[0, n]),
            pltpu.make_async_copy(up_hbm.at[:, columns], up_ref.at[:, columns], sems.at[1, n]),
        )

    def start(n):
        for copy in load(n):
            copy.start()

    start(0)
    turn_rows(rows_ref, turn_scr, x_scr, lambda: start(1))
    for n in range(2, parts):
        start(n)
    score_scr[...] = jnp.zeros_like(score_scr)

    def hidden_part(n, _):
        for copy in load(n):
            copy.wait()
        columns = lanes(n * span, span)
        a = dot32(x_scr[...], gate_ref[:, columns])
        b = dot32(x_scr[...], up_ref[:, columns])
        u = inner_grad_ref[:, columns]
        sig = 1.0 / (1.0 + jnp.exp(-a))
        act = a * sig
        product = u * b
        scores = jnp.sum(product * act, axis=1, keepdims=True)
        score_scr[0:count, :] += jnp.broadcast_to(scores, (count, HEAD_SIZE))
        da_scr[:, columns] = (product * sig * (1.0 + a * (1.0 - sig))).astype(bf16)
        db_scr[:, columns] = (u * act).astype(bf16)
        return 0

    lax.fori_loop(0, parts, hidden_part, 0)

    def grad_part(j, _):
        rows = pl.ds(pl.multiple_of(j * 2 * span, 2 * span), 2 * span)
        d = dot32(da_scr[...], gate_ref[rows, :], NT) + dot32(db_scr[...], up_ref[rows, :], NT)
        for i in range(4):
            turn_scr[pl.ds(4 * j + i, count, stride=PITCH), :] = d[
                :, i * HEAD_SIZE : (i + 1) * HEAD_SIZE
            ]
        return 0

    lax.fori_loop(0, QUERY_HEADS // 4, grad_part, 0)

    def narrow(i, _):
        for c in range(capacity):
            row = turn_scr[pl.ds((i * capacity + c) * PITCH, QUERY_HEADS), :]
            out_ref[i, c * QUERY_HEADS : (c + 1) * QUERY_HEADS, :] = row.astype(bf16)
        out_ref[i, per_peer : per_peer + 8, :] = score_scr[pl.ds(capacity * i, 8), :].astype(bf16)
        return 0

    lax.fori_loop(0, peers, narrow, 0, unroll=2)


def expert(rows, inner_grad, gate_mat, up_mat):
    peers, per_peer, _ = rows.shape
    count = inner_grad.shape[0]
    width, hidden_units = gate_mat.shape
    f32, bf16 = jnp.float32, jnp.bfloat16
    return pl.pallas_call(
        expert_kernel,
        in_specs=[pl.BlockSpec(memory_space=pltpu.VMEM)] * 2
        + [pl.BlockSpec(memory_space=pltpu.HBM)] * 2,
        out_specs=pl.BlockSpec(memory_space=pltpu.VMEM),
        scratch_shapes=[
            pltpu.VMEM((width, hidden_units), bf16),
            pltpu.VMEM((width, hidden_units), bf16),
            pltpu.VMEM((count * PITCH, HEAD_SIZE), f32),
            pltpu.VMEM((count, width), bf16),
            pltpu.VMEM((count, hidden_units), bf16),
            pltpu.VMEM((count, hidden_units), bf16),
            pltpu.VMEM((count + 16, HEAD_SIZE), f32),
            pltpu.SemaphoreType.DMA((2, hidden_units // 256)),
        ],
        out_shape=jax.ShapeDtypeStruct((peers, per_peer + 8, HEAD_SIZE), bf16),
        compiler_params=pltpu.CompilerParams(vmem_limit_bytes=50 << 20),
        cost_estimate=pl.CostEstimate(
            flops=8 * count * width * hidden_units, bytes_accessed=20 << 20, transcendentals=count * hidden_units
        ),
        name="expert",
    )(rows, inner_grad, gate_mat, up_mat)


def combine_kernel(
    ids_smem,
    ranks,
    gates_smem,
    back_ref,
    gates_ref,
    ids_ref,
    hid_ref,
    norm_ref,
    rms_ref,
    og_ref,
    gain_ref,
    router_ref,
    res_ref,
    part_ref,
    rows_scr,
    score_scr,
    dn_scr,
    acc_scr,
):
    f32, bf16 = jnp.float32, jnp.bfloat16
    tokens = hid_ref.shape[0]
    capacity = 3
    per_peer = capacity * QUERY_HEADS

    def pick(t, _):
        total = None
        scores = []
        for k in range(2):
            e = ids_smem[2 * t + k]
            c = ranks[2 * t + k]
            start = pl.multiple_of(c * QUERY_HEADS, QUERY_HEADS)
            row = back_ref[e, pl.ds(start, QUERY_HEADS), :].astype(f32) * gates_smem[2 * t + k]
            total = row if total is None else total + row
            tail = back_ref[e, per_peer : per_peer + 8, :].astype(f32)
            which = lax.broadcasted_iota(jnp.int32, tail.shape, 0) == c
            scores.append(jnp.sum(jnp.where(which, tail, 0.0), axis=0, keepdims=True))
        rows_scr[pl.ds(t * PITCH, QUERY_HEADS), :] = total
        score_scr[pl.ds(t, 1), :] = scores[0] - scores[1]
        return 0

    lax.fori_loop(0, tokens, pick, 0, unroll=8)
    first = gates_ref[:, 0:1]
    value = first * (1.0 - first) * score_scr[...]
    lane = lax.broadcasted_iota(jnp.int32, (tokens, HEAD_SIZE), 1)
    d_logits = jnp.where(lane == ids_ref[:, 0:1], value, 0.0) - jnp.where(
        lane == ids_ref[:, 1:2], value, 0.0
    )
    d_logits = d_logits.astype(bf16)
    acc_scr[...] = jnp.zeros_like(acc_scr)

    def gather(h, _):
        columns = lanes(h * HEAD_SIZE, HEAD_SIZE)
        rows = pl.ds(pl.multiple_of(h * HEAD_SIZE, HEAD_SIZE), HEAD_SIZE)
        dn = rows_scr[pl.ds(h, tokens, stride=PITCH), :] + dot32(
            d_logits, router_ref[rows, :], NT
        )
        scaled = dn * gain_ref[:, columns]
        dn_scr[:, columns] = scaled
        acc_scr[...] += hid_ref[:, columns].astype(f32) * scaled
        part_ref[rows, :] = dot32(norm_ref[:, columns], d_logits, TN).astype(bf16)
        return 0

    lax.fori_loop(0, QUERY_HEADS, gather, 0, unroll=2)
    r = rms_ref[...]
    mean = jnp.sum(acc_scr[...], axis=1, keepdims=True) * (1.0 / (QUERY_HEADS * HEAD_SIZE))
    pull = r * r * r * mean

    def finish(h, _):
        columns = lanes(h * HEAD_SIZE, HEAD_SIZE)
        res = og_ref[:, columns].astype(f32) + r * dn_scr[:, columns] - hid_ref[:, columns].astype(f32) * pull
        res_ref[:, columns] = res.astype(bf16)
        return 0

    lax.fori_loop(0, QUERY_HEADS, finish, 0, unroll=2)


def combine(ranks, gates, ids, back, hidden, normed, inv_rms, out_grad, gain, router):
    tokens, width = hidden.shape
    experts = router.shape[1]
    f32, bf16 = jnp.float32, jnp.bfloat16
    return pl.pallas_call(
        combine_kernel,
        in_specs=[pl.BlockSpec(memory_space=pltpu.SMEM)] * 3
        + [pl.BlockSpec(memory_space=pltpu.VMEM)] * 9,
        out_specs=[pl.BlockSpec(memory_space=pltpu.VMEM)] * 2,
        scratch_shapes=[
            pltpu.VMEM((tokens * PITCH, HEAD_SIZE), f32),
            pltpu.VMEM((tokens, HEAD_SIZE), f32),
            pltpu.VMEM((tokens, width), f32),
            pltpu.VMEM((tokens, HEAD_SIZE), f32),
        ],
        out_shape=[
            jax.ShapeDtypeStruct((tokens, width), bf16),
            jax.ShapeDtypeStruct((width, experts), bf16),
        ],
        compiler_params=pltpu.CompilerParams(vmem_limit_bytes=50 << 20),
        cost_estimate=pl.CostEstimate(
            flops=4 * tokens * width * experts, bytes_accessed=9 << 20, transcendentals=0
        ),
        name="combine",
    )(ids.reshape(-1), ranks, gates.reshape(-1), back, gates, ids, hidden, normed, inv_rms, out_grad, gain, router)


def pair_kernel(keep_ref, came_ref, out_ref):
    def one(b, _):
        out_ref[b] = (keep_ref[b].astype(jnp.float32) + came_ref[b].astype(jnp.float32)).astype(
            jnp.bfloat16
        )
        return 0

    lax.fori_loop(0, keep_ref.shape[0], one, 0)


def pair_sum(keep, came):
    vmem = pl.BlockSpec(memory_space=pltpu.VMEM)
    return pl.pallas_call(
        pair_kernel,
        in_specs=[vmem] * 2,
        out_specs=vmem,
        out_shape=jax.ShapeDtypeStruct(keep.shape, keep.dtype),
        compiler_params=pltpu.CompilerParams(vmem_limit_bytes=50 << 20),
        cost_estimate=pl.CostEstimate(flops=keep.size, bytes_accessed=3 << 20, transcendentals=0),
        name="pair_sum",
    )(keep, came)


def block_sum_kernel(parts_ref, keys_ref, values_ref):
    total = parts_ref[0].astype(jnp.float32)
    for b in range(1, parts_ref.shape[0]):
        total = total + parts_ref[b].astype(jnp.float32)
    half = keys_ref.shape[1]
    keys_ref[...] = total[:, :half].astype(jnp.bfloat16)
    values_ref[...] = total[:, half:].astype(jnp.bfloat16)


def block_sum(parts):
    vmem = pl.BlockSpec(memory_space=pltpu.VMEM)
    shape = jax.ShapeDtypeStruct((parts.shape[1], parts.shape[2] // 2), parts.dtype)
    return pl.pallas_call(
        block_sum_kernel,
        in_specs=[vmem],
        out_specs=[vmem] * 2,
        out_shape=[shape, shape],
        compiler_params=pltpu.CompilerParams(vmem_limit_bytes=50 << 20),
        cost_estimate=pl.CostEstimate(flops=parts.size, bytes_accessed=2 << 20, transcendentals=0),
        name="block_sum",
    )(parts)


def swap_cores(array):
    return lax.ppermute(array, CORE, [(0, 1), (1, 0)])


def exchange(array, axes):
    return lax.all_to_all(array, axes, split_axis=0, concat_axis=0, tiled=True)


def layer(
    queries,
    keys,
    values,
    stream,
    norm_gain,
    router_weight,
    gate_weight,
    up_weight,
    down_weight,
    doc_lengths,
    expert_ids,
    out_grad,
):
    token_rows = queries.shape[1]
    steps = (lax.axis_size("blk_0"), *keys.shape[1:])
    both = jnp.concatenate(
        [jnp.broadcast_to(keys, steps), jnp.broadcast_to(values, steps)], axis=2
    )
    near = exchange(both, "blk_0")
    far = lax.ppermute(near, "blk_1", [(0, 1), (1, 0)])
    near_other = swap_cores(near)
    sources = (near, far, near_other, swap_cores(far))

    meta = jnp.concatenate([lax.axis_index(GRP_BLK).astype(jnp.int32)[None], doc_lengths[0]])
    experts = router_weight.shape[1]
    chosen_ids = expert_ids[0]
    top_count = chosen_ids.shape[1]
    capacity = max(2, 3 * token_rows * top_count // (2 * experts))
    flat_ids = chosen_ids.reshape(-1)
    same = flat_ids[:, None] == flat_ids[None, :]
    order = jnp.arange(flat_ids.shape[0], dtype=jnp.int32)
    slot_rank = jnp.sum((same & (order[None, :] < order[:, None])).astype(jnp.int32), axis=1, dtype=jnp.int32)
    slots = flat_ids * capacity + slot_rank
    slot_count = experts * capacity

    send_grads = place(slots, out_grad[0], slot_count)
    got_grads = exchange(send_grads.reshape(experts, -1, HEAD_SIZE), GRP_BLK)

    weights, linv, attended, hidden, normed, inv_rms, send_rows = attend(
        meta, slots, queries[0], sources, stream[0], norm_gain[None], slot_count
    )
    got_rows = exchange(send_rows.reshape(experts, -1, HEAD_SIZE), GRP_BLK)

    logits = jnp.dot(normed, router_weight, preferred_element_type=jnp.float32)
    hits = chosen_ids[:, :, None] == jnp.arange(experts, dtype=jnp.int32)[None, None, :]
    chosen = jnp.sum(jnp.where(hits, logits[:, None, :], 0.0), axis=-1)
    first_gate = jax.nn.sigmoid(chosen[:, 0] - chosen[:, 1])
    gates = jnp.stack([first_gate, 1.0 - first_gate], axis=1)

    inner_grad = down(got_grads, down_weight[0])
    back = exchange(expert(got_rows, inner_grad, gate_weight[0], up_weight[0]), GRP_BLK)
    residual_gradient, router_parts = combine(
        slot_rank, gates, chosen_ids, back, hidden, normed, inv_rms, out_grad[0], norm_gain[None], router_weight
    )
    got_parts = exchange(router_parts.reshape(experts, -1, experts), GRP_BLK)
    query_grad, keep, give = attend_back(
        meta, queries[0], residual_gradient, attended, linv, sources, weights
    )
    pairs = pair_sum(keep, swap_cores(give))
    key_grad, value_grad = block_sum(exchange(pairs, ZX))
    router_grad = jnp.sum(got_parts.astype(jnp.float32), axis=0)
    return (
        query_grad[None],
        key_grad[None],
        value_grad[None],
        residual_gradient[None],
        router_grad,
    )


def solution(mesh):
    split = Mesh(mesh.devices.reshape(2, 4, 4, 2, 2), ("grp_0", "grp_1", "blk_0", "blk_1", "blk_2"))
    return jax.shard_map(
        layer,
        mesh=split,
        in_specs=(
            P(GRP, BLK, None),
            P(GRP, BLK, None),
            P(GRP, BLK, None),
            P(GRP, BLK, None),
            P(),
            P(),
            P(GRP_BLK, None, None),
            P(GRP_BLK, None, None),
            P(GRP_BLK, None, None),
            P(GRP, None),
            P(GRP, BLK, None),
            P(GRP, BLK, None),
        ),
        out_specs=(
            P(GRP, BLK, None),
            P(GRP, BLK, None),
            P(GRP, BLK, None),
            P(GRP, BLK, None),
            P(GRP_BLK, None),
        ),
        check_vma=False,
    )
```

```python
import math

import jax
import jax.numpy as jnp
from jax import lax
from jax.experimental import pallas as pl
from jax.experimental.pallas import tpu as pltpu
from jax.sharding import Mesh
from jax.sharding import PartitionSpec as P


HEAD_SIZE = 128
QUERY_HEADS = 32
KEY_VALUE_HEADS = 2
HEADS_PER_GROUP = QUERY_HEADS // KEY_VALUE_HEADS
BLK = ("blk_0", "blk_1", "blk_2")
GRP_BLK = ("grp_0", "grp_1", "blk_0", "blk_1", "blk_2")
GRP = ("grp_0", "grp_1")
ZX = ("blk_0", "blk_1")
CORE = "blk_2"

NEGATIVE_HUGE = -1e30
EPSILON = 1e-06
SCALE = HEAD_SIZE ** (-0.5)
KEY_BLOCK = 256
OCTET = 8
VMEM_LIMIT = 60 * 1024 * 1024
PITCH = QUERY_HEADS + 1

NT = (((1,), (1,)), ((), ()))
TN = (((0,), (0,)), ((), ()))


def dot32(a, b, dims=(((1,), (0,)), ((), ()))):
    return lax.dot_general(a, b, dims, preferred_element_type=jnp.float32)


def lanes(start, size):
    return pl.ds(pl.multiple_of(start, 128), size)


def bounds(meta):
    place = meta[0] & 15
    first_query = place * 128
    ends = [meta[1]]
    for d in range(1, 4):
        ends.append(ends[-1] + meta[1 + d])
    start = jnp.int32(0)
    for end in ends:
        start = jnp.where(end <= first_query, end, start)
    return start // KEY_BLOCK, (first_query + 127) // KEY_BLOCK, meta[0] & 1, first_query, ends


def block_loads(meta, sources, kv_scr, sems):
    core, x = meta[0] & 1, (meta[0] >> 1) & 1
    copies = []
    for i, source in enumerate(sources):
        for z in range(source.shape[0]):
            block = (z * 2 + ((x + i) & 1)) * 2 + ((core + i // 2) & 1)
            rows = pl.ds(pl.multiple_of(block * 128, 128), 128)
            copies.append(
                pltpu.make_async_copy(
                    source.at[z], kv_scr.at[rows, :], sems.at[i * source.shape[0] + z]
                )
            )
    return copies


def attend_kernel(
    meta,
    slots,
    q_ref,
    near_hbm,
    far_hbm,
    near_other_hbm,
    far_other_hbm,
    stream_ref,
    gain_ref,
    w_ref,
    linv_ref,
    att_ref,
    hid_ref,
    norm_ref,
    rms_ref,
    send_ref,
    kv_scr,
    vt_scr,
    bias_scr,
    s_scr,
    ot_scr,
    ss_scr,
    rows_scr,
    sems,
):
    octet = pl.program_id(0)
    group = octet // (HEADS_PER_GROUP // OCTET)
    low, high, _, first_query, ends = bounds(meta)
    tokens = q_ref.shape[0]
    factor = SCALE * math.log2(math.e)

    @pl.when(octet == 0)
    def _():
        sources = (near_hbm, far_hbm, near_other_hbm, far_other_hbm)
        copies = block_loads(meta, sources, kv_scr, sems)
        for copy in copies:
            copy.start()
        ss_scr[...] = jnp.zeros_like(ss_scr)
        query = first_query + lax.broadcasted_iota(jnp.int32, (KEY_BLOCK, tokens), 1)
        start = jnp.zeros((KEY_BLOCK, tokens), jnp.int32)
        for d in range(4):
            start = jnp.maximum(start, jnp.where(query >= ends[d], ends[d], 0))

        for copy in copies:
            copy.wait()

        def prepare(kb, _):
            rows = pl.ds(pl.multiple_of(kb * KEY_BLOCK, KEY_BLOCK), KEY_BLOCK)
            vt_scr[kb] = kv_scr[rows, 256:512].T
            key = kb * KEY_BLOCK + lax.broadcasted_iota(jnp.int32, (KEY_BLOCK, tokens), 0)
            seen = (key <= query) & (key >= start)
            bias_scr[kb] = jnp.where(seen, 0.0, NEGATIVE_HUGE)
            return 0

        lax.fori_loop(low, high + 1, prepare, 0)

    pairs = OCTET // 2
    wide = 2 * tokens

    def score(kb, tops):
        rows = pl.ds(pl.multiple_of(kb * KEY_BLOCK, KEY_BLOCK), KEY_BLOCK)
        key_rows = kv_scr[rows, lanes(group * HEAD_SIZE, HEAD_SIZE)]
        bias = bias_scr[kb]
        bias = jnp.concatenate([bias, bias], axis=1)
        new = []
        for p in range(pairs):
            c = 2 * p * HEAD_SIZE
            both = jnp.concatenate(
                [q_ref[:, c : c + HEAD_SIZE], q_ref[:, c + HEAD_SIZE : c + 2 * HEAD_SIZE]], axis=0
            )
            s = dot32(key_rows, both, NT) + bias
            s_scr[kb, :, p * wide : (p + 1) * wide] = s
            new.append(jnp.maximum(tops[p], jnp.max(s.reshape(-1, 8, wide), axis=0)))
        return tuple(new)

    tops = lax.fori_loop(
        low, high + 1, score, tuple(jnp.full((8, wide), NEGATIVE_HUGE, jnp.float32) for _ in range(pairs))
    )
    tops = tuple(jnp.max(t, axis=0, keepdims=True) * factor for t in tops)
    ot_scr[...] = jnp.zeros_like(ot_scr)

    def weigh(kb, sums):
        value_cols = vt_scr[kb, pl.ds(pl.multiple_of(group * HEAD_SIZE, HEAD_SIZE), HEAD_SIZE), :]
        new = []
        for p in range(pairs):
            span = slice(p * wide, (p + 1) * wide)
            w = jnp.exp2(s_scr[kb, :, span] * factor - tops[p])
            new.append(sums[p] + jnp.sum(w.reshape(-1, 8, wide), axis=0))
            low_w = w.astype(jnp.bfloat16)
            w_ref[0, kb, :, span] = low_w
            ot_scr[:, span] += dot32(value_cols, low_w)
        return tuple(new)

    sums = lax.fori_loop(
        low, high + 1, weigh, tuple(jnp.zeros((8, wide), jnp.float32) for _ in range(pairs))
    )
    for p in range(pairs):
        inverse = 1.0 / jnp.sum(sums[p], axis=0, keepdims=True)
        mixed = ot_scr[:, p * wide : (p + 1) * wide] * inverse
        for i in range(2):
            h = 2 * p + i
            linv_ref[h : h + 1, :] = inverse[:, i * tokens : (i + 1) * tokens]
            columns = lanes((octet * OCTET + h) * HEAD_SIZE, HEAD_SIZE)
            att = mixed[:, i * tokens : (i + 1) * tokens].T.astype(jnp.bfloat16)
            att_ref[:, columns] = att
            hid = (stream_ref[:, columns].astype(jnp.float32) + att.astype(jnp.float32)).astype(
                jnp.bfloat16
            )
            hid_ref[:, columns] = hid
            wide_hid = hid.astype(jnp.float32)
            ss_scr[...] += wide_hid * wide_hid

    @pl.when(octet == pl.num_programs(0) - 1)
    def _():
        mean = jnp.sum(ss_scr[...], axis=1, keepdims=True) * (1.0 / (QUERY_HEADS * HEAD_SIZE))
        inv_rms = jnp.broadcast_to(lax.rsqrt(mean + EPSILON), (tokens, HEAD_SIZE))
        rms_ref[...] = inv_rms

        def norm(h, _):
            columns = lanes(h * HEAD_SIZE, HEAD_SIZE)
            n = (hid_ref[:, columns].astype(jnp.float32) * inv_rms * gain_ref[:, columns]).astype(
                jnp.bfloat16
            )
            norm_ref[:, columns] = n
            rows_scr[pl.ds(h, tokens, stride=PITCH), :] = n.astype(jnp.float32)
            return 0

        lax.fori_loop(0, QUERY_HEADS, norm, 0, unroll=2)
        scatter_rows(slots, rows_scr, send_ref, tokens)


def scatter_rows(slots, rows_scr, send_ref, tokens):
    def send(t, _):
        row = rows_scr[pl.ds(t * PITCH, QUERY_HEADS), :].astype(jnp.bfloat16)
        send_ref[slots[2 * t]] = row
        send_ref[slots[2 * t + 1]] = row
        return 0

    lax.fori_loop(0, tokens, send, 0, unroll=8)


def whole(shape):
    zero = (0,) * len(shape)
    return pl.BlockSpec(shape, lambda *_: zero)


def attend(meta, slots, queries, sources, stream, gain, slot_count):
    tokens, width = queries.shape
    octets = QUERY_HEADS // OCTET
    blocks = 2 * sources[0].shape[0]
    columns = sources[0].shape[2]
    span = OCTET * tokens
    bf16, f32 = jnp.bfloat16, jnp.float32
    return pl.pallas_call(
        attend_kernel,
        grid_spec=pltpu.PrefetchScalarGridSpec(
            num_scalar_prefetch=2,
            grid=(octets,),
            in_specs=[
                pl.BlockSpec((tokens, OCTET * HEAD_SIZE), lambda o, *_: (0, o)),
                *[pl.BlockSpec(memory_space=pltpu.HBM)] * 4,
                whole(stream.shape),
                whole((1, width)),
            ],
            out_specs=[
                pl.BlockSpec((1, blocks, KEY_BLOCK, span), lambda o, *_: (o, 0, 0, 0)),
                pl.BlockSpec((OCTET, tokens), lambda o, *_: (o, 0)),
                whole((tokens, width)),
                whole((tokens, width)),
                whole((tokens, width)),
                whole((tokens, HEAD_SIZE)),
                whole((slot_count, QUERY_HEADS, HEAD_SIZE)),
            ],
            scratch_shapes=[
                pltpu.VMEM((blocks * KEY_BLOCK, columns), bf16),
                pltpu.VMEM((blocks, columns // 2, KEY_BLOCK), bf16),
                pltpu.VMEM((blocks, KEY_BLOCK, tokens), f32),
                pltpu.VMEM((blocks, KEY_BLOCK, span), f32),
                pltpu.VMEM((HEAD_SIZE, span), f32),
                pltpu.VMEM((tokens, HEAD_SIZE), f32),
                pltpu.VMEM((tokens * PITCH, HEAD_SIZE), f32),
                pltpu.SemaphoreType.DMA((16,)),
            ],
        ),
        out_shape=[
            jax.ShapeDtypeStruct((octets, blocks, KEY_BLOCK, span), bf16),
            jax.ShapeDtypeStruct((QUERY_HEADS, tokens), f32),
            jax.ShapeDtypeStruct((tokens, width), bf16),
            jax.ShapeDtypeStruct((tokens, width), bf16),
            jax.ShapeDtypeStruct((tokens, width), bf16),
            jax.ShapeDtypeStruct((tokens, HEAD_SIZE), f32),
            jax.ShapeDtypeStruct((slot_count, QUERY_HEADS, HEAD_SIZE), bf16),
        ],
        compiler_params=pltpu.CompilerParams(
            dimension_semantics=("arbitrary",), vmem_limit_bytes=VMEM_LIMIT
        ),
        cost_estimate=pl.CostEstimate(
            flops=4 * tokens * width * 1536, bytes_accessed=24 << 20, transcendentals=tokens * 32 * 1536
        ),
        name="attend",
    )(meta, slots, queries, *sources, stream, gain)


def place_kernel(slots, rows_ref, send_ref, rows_scr):
    tokens = rows_ref.shape[0]

    def turn(h, _):
        rows_scr[pl.ds(h, tokens, stride=PITCH), :] = rows_ref[
            :, lanes(h * HEAD_SIZE, HEAD_SIZE)
        ].astype(jnp.float32)
        return 0

    lax.fori_loop(0, QUERY_HEADS, turn, 0, unroll=2)
    scatter_rows(slots, rows_scr, send_ref, tokens)


def place(slots, rows, slot_count):
    tokens, _ = rows.shape
    return pl.pallas_call(
        place_kernel,
        grid_spec=pltpu.PrefetchScalarGridSpec(
            num_scalar_prefetch=1,
            grid=(1,),
            in_specs=[whole(rows.shape)],
            out_specs=whole((slot_count, QUERY_HEADS, HEAD_SIZE)),
            scratch_shapes=[pltpu.VMEM((tokens * PITCH, HEAD_SIZE), jnp.float32)],
        ),
        out_shape=jax.ShapeDtypeStruct((slot_count, QUERY_HEADS, HEAD_SIZE), jnp.bfloat16),
        compiler_params=pltpu.CompilerParams(vmem_limit_bytes=VMEM_LIMIT),
        cost_estimate=pl.CostEstimate(flops=0, bytes_accessed=4 << 20, transcendentals=0),
        name="place",
    )(slots, rows)


def attend_back_kernel(
    meta,
    q_hbm,
    grad_hbm,
    att_hbm,
    linv_ref,
    near_hbm,
    far_hbm,
    near_other_hbm,
    far_other_hbm,
    w_hbm,
    dq_ref,
    keep_ref,
    give_ref,
    kv_scr,
    kt_scr,
    q_scr,
    do_scr,
    rd_scr,
    ds_scr,
    dqt_scr,
    w_buf,
    q_ref,
    grad_ref,
    att_ref,
    sems,
    block_sems,
):
    blocks = block_loads(
        meta, (near_hbm, far_hbm, near_other_hbm, far_other_hbm), kv_scr, block_sems
    )
    for copy in blocks:
        copy.start()

    operands = ((q_hbm, q_ref), (grad_hbm, grad_ref), (att_hbm, att_ref))
    loads = [pltpu.make_async_copy(a, b, sems.at[2 + i]) for i, (a, b) in enumerate(operands)]
    for copy in loads:
        copy.start()
    low, high, core, _, _ = bounds(meta)
    count = high - low + 1
    tokens = q_ref.shape[0]
    wide = 2 * tokens
    per_group = HEADS_PER_GROUP * tokens
    octets = HEADS_PER_GROUP // OCTET
    f32, bf16 = jnp.float32, jnp.bfloat16

    def load(group, kb, slot):
        return pltpu.make_async_copy(
            w_hbm.at[pl.ds(group * octets, octets), kb], w_buf.at[slot], sems.at[slot]
        )

    load(0, low, 0).start()
    keep_ref[...] = jnp.zeros_like(keep_ref)
    give_ref[...] = jnp.zeros_like(give_ref)
    for copy in blocks:
        copy.wait()

    def prepare(kb, _):
        rows = pl.ds(pl.multiple_of(kb * KEY_BLOCK, KEY_BLOCK), KEY_BLOCK)
        kt_scr[kb] = kv_scr[rows, 0:256].T
        return 0

    lax.fori_loop(low, high + 1, prepare, 0)
    inverse = jnp.concatenate(
        [linv_ref[...], jnp.zeros((128 - QUERY_HEADS, tokens), f32)], axis=0
    ).T
    lane = lax.broadcasted_iota(jnp.int32, (HEAD_SIZE, HEAD_SIZE), 1)
    dots = jnp.zeros((tokens, HEAD_SIZE), f32)
    for copy in loads:
        copy.wait()
    for h in range(QUERY_HEADS):
        columns = slice(h * HEAD_SIZE, (h + 1) * HEAD_SIZE)
        rows = slice(h * tokens, (h + 1) * tokens)
        q_scr[rows, :] = q_ref[:, columns]
        scaled = (grad_ref[:, columns].astype(f32) * inverse[:, h : h + 1]).astype(bf16)
        do_scr[rows, :] = scaled
        product = scaled.astype(f32) * att_ref[:, columns].astype(f32)
        head = product.astype(bf16)
        tail = (product - head.astype(f32)).astype(bf16)
        ones = jnp.where(lane == h, 1.0, 0.0).astype(bf16)
        dots = dots + dot32(head, ones) + dot32(tail, ones)
    dots = dots.T
    for h in range(QUERY_HEADS):
        rd_scr[0:1, h * tokens : (h + 1) * tokens] = dots[h : h + 1, :]

    is_first = jnp.full((128, HEAD_SIZE), core, jnp.int32) == 0

    def one_group(group, _):
        dqt_scr[...] = jnp.zeros_like(dqt_scr)
        base = pl.multiple_of(group * per_group, per_group)
        half = per_group // octets

        def one_block(j, _):
            kb = low + j
            turn = group * count + j
            slot = lax.rem(turn, 2)
            load(group, kb, slot).wait()

            @pl.when(turn + 1 < KEY_VALUE_HEADS * count)
            def _():
                wrap = j + 1 == count
                load(
                    jnp.where(wrap, group + 1, group), low + jnp.where(wrap, 0, j + 1), 1 - slot
                ).start()

            rows = pl.ds(pl.multiple_of(kb * KEY_BLOCK, KEY_BLOCK), KEY_BLOCK)
            value_rows = kv_scr[rows, lanes(256 + group * HEAD_SIZE, HEAD_SIZE)]
            key_cols = kt_scr[kb, pl.ds(pl.multiple_of(group * HEAD_SIZE, HEAD_SIZE), HEAD_SIZE), :]
            for p in range(HEADS_PER_GROUP // 2):
                here = pl.multiple_of(group * per_group + p * wide, wide)
                dp = dot32(value_rows, do_scr[pl.ds(here, wide), :], NT)
                per_octet = OCTET // 2
                c = (p % per_octet) * wide
                w = w_buf[slot, p // per_octet, :, c : c + wide].astype(f32)
                ds = (w * (dp - rd_scr[0:1, pl.ds(here, wide)])).astype(bf16)
                ds_scr[:, p * wide : (p + 1) * wide] = ds
            dqt_scr[...] += dot32(key_cols, ds_scr[...])
            dv = dot32(w_buf[slot, 0], do_scr[pl.ds(base, half), :]) + dot32(
                w_buf[slot, 1], do_scr[pl.ds(base + half, half), :]
            )
            dk = dot32(ds_scr[...], q_scr[pl.ds(base, per_group), :]) * SCALE
            for part, column in ((dk, 0), (dv, 256)):
                columns = lanes(column + group * HEAD_SIZE, HEAD_SIZE)
                keep_ref[kb, :, columns] = jnp.where(is_first, part[:128], part[128:]).astype(bf16)
                give_ref[kb, :, columns] = jnp.where(is_first, part[128:], part[:128]).astype(bf16)
            return 0

        lax.fori_loop(0, count, one_block, 0)
        for h in range(HEADS_PER_GROUP):
            dq = dqt_scr[:, h * tokens : (h + 1) * tokens] * SCALE
            dq_ref[:, lanes(group * per_group + h * HEAD_SIZE, HEAD_SIZE)] = dq.T.astype(bf16)
        return 0

    lax.fori_loop(0, KEY_VALUE_HEADS, one_group, 0)


def attend_back(meta, queries, grads, attended, linv, sources, weights):
    tokens, width = queries.shape
    blocks = 2 * sources[0].shape[0]
    columns = sources[0].shape[2]
    parts = (blocks, 128, columns)
    bf16, f32 = jnp.bfloat16, jnp.float32
    per_group = HEADS_PER_GROUP * tokens
    octets = HEADS_PER_GROUP // OCTET
    span = OCTET * tokens
    vmem, hbm = pl.BlockSpec(memory_space=pltpu.VMEM), pl.BlockSpec(memory_space=pltpu.HBM)
    return pl.pallas_call(
        attend_back_kernel,
        in_specs=[pl.BlockSpec(memory_space=pltpu.SMEM)] + [hbm] * 3 + [vmem] + [hbm] * 5,
        out_specs=[vmem] * 3,
        scratch_shapes=[
            pltpu.VMEM((blocks * KEY_BLOCK, columns), bf16),
            pltpu.VMEM((blocks, columns // 2, KEY_BLOCK), bf16),
            pltpu.VMEM((QUERY_HEADS * tokens, HEAD_SIZE), bf16),
            pltpu.VMEM((QUERY_HEADS * tokens, HEAD_SIZE), bf16),
            pltpu.VMEM((8, QUERY_HEADS * tokens), f32),
            pltpu.VMEM((KEY_BLOCK, per_group), bf16),
            pltpu.VMEM((HEAD_SIZE, per_group), f32),
            pltpu.VMEM((2, octets, KEY_BLOCK, span), bf16),
            pltpu.VMEM((tokens, width), bf16),
            pltpu.VMEM((tokens, width), bf16),
            pltpu.VMEM((tokens, width), bf16),
            pltpu.SemaphoreType.DMA((5,)),
            pltpu.SemaphoreType.DMA((16,)),
        ],
        out_shape=[
            jax.ShapeDtypeStruct((tokens, width), bf16),
            jax.ShapeDtypeStruct(parts, bf16),
            jax.ShapeDtypeStruct(parts, bf16),
        ],
        compiler_params=pltpu.CompilerParams(vmem_limit_bytes=58 << 20),
        cost_estimate=pl.CostEstimate(
            flops=8 * tokens * width * 1536, bytes_accessed=20 << 20, transcendentals=0
        ),
        name="attend_back",
    )(meta, queries, grads, attended, linv, *sources, weights)


def turn_rows(rows_ref, turn_scr, x_scr, between=lambda: None):
    peers, per_peer = rows_ref.shape[0], rows_ref.shape[1]
    capacity = per_peer // QUERY_HEADS
    count = peers * capacity

    def widen(i, _):
        for c in range(capacity):
            row = rows_ref[i, c * QUERY_HEADS : (c + 1) * QUERY_HEADS, :].astype(jnp.float32)
            turn_scr[pl.ds((i * capacity + c) * PITCH, QUERY_HEADS), :] = row
        return 0

    lax.fori_loop(0, peers, widen, 0, unroll=4)
    between()

    def turn(j, _):
        x_scr[:, lanes(j * HEAD_SIZE, HEAD_SIZE)] = turn_scr[
            pl.ds(j, count, stride=PITCH), :
        ].astype(jnp.bfloat16)
        return 0

    lax.fori_loop(0, QUERY_HEADS, turn, 0, unroll=2)


def down_kernel(rows_ref, down_ref, out_ref, turn_scr, x_scr):
    turn_rows(rows_ref, turn_scr, x_scr)
    span = 256

    def part(n, _):
        rows = pl.ds(pl.multiple_of(n * span, span), span)
        out_ref[:, lanes(n * span, span)] = dot32(x_scr[...], down_ref[rows, :], NT)
        return 0

    lax.fori_loop(0, down_ref.shape[0] // span, part, 0)


def down(rows, down_mat):
    peers, per_peer, _ = rows.shape
    hidden_units, width = down_mat.shape
    count = peers * per_peer // QUERY_HEADS
    vmem = pl.BlockSpec(memory_space=pltpu.VMEM)
    return pl.pallas_call(
        down_kernel,
        in_specs=[vmem] * 2,
        out_specs=vmem,
        scratch_shapes=[
            pltpu.VMEM((count * PITCH, HEAD_SIZE), jnp.float32),
            pltpu.VMEM((count, width), jnp.bfloat16),
        ],
        out_shape=jax.ShapeDtypeStruct((count, hidden_units), jnp.float32),
        compiler_params=pltpu.CompilerParams(vmem_limit_bytes=24 << 20),
        cost_estimate=pl.CostEstimate(
            flops=2 * count * width * hidden_units, bytes_accessed=11 << 20, transcendentals=0
        ),
        name="down",
    )(rows, down_mat)


def expert_kernel(
    rows_ref,
    inner_grad_ref,
    gate_hbm,
    up_hbm,
    out_ref,
    gate_ref,
    up_ref,
    turn_scr,
    x_scr,
    da_scr,
    db_scr,
    score_scr,
    sems,
):
    bf16 = jnp.bfloat16
    peers, per_peer = rows_ref.shape[0], rows_ref.shape[1]
    count = x_scr.shape[0]
    hidden_units = gate_ref.shape[1]
    capacity = count // peers

    span = 256
    parts = hidden_units // span

    def load(n):
        columns = lanes(n * span, span)
        return (
            pltpu.make_async_copy(gate_hbm.at[:, columns], gate_ref.at[:, columns], sems.at[0, n]),
            pltpu.make_async_copy(up_hbm.at[:, columns], up_ref.at[:, columns], sems.at[1, n]),
        )

    def start(n):
        for copy in load(n):
            copy.start()

    start(0)
    turn_rows(rows_ref, turn_scr, x_scr, lambda: start(1))
    for n in range(2, parts):
        start(n)
    score_scr[...] = jnp.zeros_like(score_scr)

    def hidden_part(n, _):
        for copy in load(n):
            copy.wait()
        columns = lanes(n * span, span)
        a = dot32(x_scr[...], gate_ref[:, columns])
        b = dot32(x_scr[...], up_ref[:, columns])
        u = inner_grad_ref[:, columns]
        sig = 1.0 / (1.0 + jnp.exp(-a))
        act = a * sig
        product = u * b
        scores = jnp.sum(product * act, axis=1, keepdims=True)
        score_scr[0:count, :] += jnp.broadcast_to(scores, (count, HEAD_SIZE))
        da_scr[:, columns] = (product * sig * (1.0 + a * (1.0 - sig))).astype(bf16)
        db_scr[:, columns] = (u * act).astype(bf16)
        return 0

    lax.fori_loop(0, parts, hidden_part, 0)

    def grad_part(j, _):
        rows = pl.ds(pl.multiple_of(j * 2 * span, 2 * span), 2 * span)
        d = dot32(da_scr[...], gate_ref[rows, :], NT) + dot32(db_scr[...], up_ref[rows, :], NT)
        for i in range(4):
            turn_scr[pl.ds(4 * j + i, count, stride=PITCH), :] = d[
                :, i * HEAD_SIZE : (i + 1) * HEAD_SIZE
            ]
        return 0

    lax.fori_loop(0, QUERY_HEADS // 4, grad_part, 0)

    def narrow(i, _):
        for c in range(capacity):
            row = turn_scr[pl.ds((i * capacity + c) * PITCH, QUERY_HEADS), :]
            out_ref[i, c * QUERY_HEADS : (c + 1) * QUERY_HEADS, :] = row.astype(bf16)
        out_ref[i, per_peer : per_peer + 8, :] = score_scr[pl.ds(capacity * i, 8), :].astype(bf16)
        return 0

    lax.fori_loop(0, peers, narrow, 0, unroll=2)


def expert(rows, inner_grad, gate_mat, up_mat):
    peers, per_peer, _ = rows.shape
    count = inner_grad.shape[0]
    width, hidden_units = gate_mat.shape
    f32, bf16 = jnp.float32, jnp.bfloat16
    return pl.pallas_call(
        expert_kernel,
        in_specs=[pl.BlockSpec(memory_space=pltpu.VMEM)] * 2
        + [pl.BlockSpec(memory_space=pltpu.HBM)] * 2,
        out_specs=pl.BlockSpec(memory_space=pltpu.VMEM),
        scratch_shapes=[
            pltpu.VMEM((width, hidden_units), bf16),
            pltpu.VMEM((width, hidden_units), bf16),
            pltpu.VMEM((count * PITCH, HEAD_SIZE), f32),
            pltpu.VMEM((count, width), bf16),
            pltpu.VMEM((count, hidden_units), bf16),
            pltpu.VMEM((count, hidden_units), bf16),
            pltpu.VMEM((count + 16, HEAD_SIZE), f32),
            pltpu.SemaphoreType.DMA((2, hidden_units // 256)),
        ],
        out_shape=jax.ShapeDtypeStruct((peers, per_peer + 8, HEAD_SIZE), bf16),
        compiler_params=pltpu.CompilerParams(vmem_limit_bytes=53 << 20),
        cost_estimate=pl.CostEstimate(
            flops=8 * count * width * hidden_units, bytes_accessed=20 << 20, transcendentals=count * hidden_units
        ),
        name="expert",
    )(rows, inner_grad, gate_mat, up_mat)


def combine_kernel(
    ids_smem,
    ranks,
    gates_smem,
    back_ref,
    gates_ref,
    ids_ref,
    hid_ref,
    norm_ref,
    rms_ref,
    og_ref,
    gain_ref,
    router_ref,
    res_ref,
    part_ref,
    rows_scr,
    score_scr,
    dn_scr,
    acc_scr,
):
    f32, bf16 = jnp.float32, jnp.bfloat16
    tokens = hid_ref.shape[0]
    capacity = 3
    per_peer = capacity * QUERY_HEADS

    def pick(t, _):
        total = None
        scores = []
        for k in range(2):
            e = ids_smem[2 * t + k]
            c = ranks[2 * t + k]
            start = pl.multiple_of(c * QUERY_HEADS, QUERY_HEADS)
            row = back_ref[e, pl.ds(start, QUERY_HEADS), :].astype(f32) * gates_smem[2 * t + k]
            total = row if total is None else total + row
            tail = back_ref[e, per_peer : per_peer + 8, :].astype(f32)
            which = lax.broadcasted_iota(jnp.int32, tail.shape, 0) == c
            scores.append(jnp.sum(jnp.where(which, tail, 0.0), axis=0, keepdims=True))
        rows_scr[pl.ds(t * PITCH, QUERY_HEADS), :] = total
        score_scr[pl.ds(t, 1), :] = scores[0] - scores[1]
        return 0

    lax.fori_loop(0, tokens, pick, 0, unroll=8)
    first = gates_ref[:, 0:1]
    value = first * (1.0 - first) * score_scr[...]
    lane = lax.broadcasted_iota(jnp.int32, (tokens, HEAD_SIZE), 1)
    d_logits = jnp.where(lane == ids_ref[:, 0:1], value, 0.0) - jnp.where(
        lane == ids_ref[:, 1:2], value, 0.0
    )
    d_logits = d_logits.astype(bf16)
    acc_scr[...] = jnp.zeros_like(acc_scr)

    def gather(h, _):
        columns = lanes(h * HEAD_SIZE, HEAD_SIZE)
        rows = pl.ds(pl.multiple_of(h * HEAD_SIZE, HEAD_SIZE), HEAD_SIZE)
        dn = rows_scr[pl.ds(h, tokens, stride=PITCH), :] + dot32(
            d_logits, router_ref[rows, :], NT
        )
        scaled = dn * gain_ref[:, columns]
        dn_scr[:, columns] = scaled
        acc_scr[...] += hid_ref[:, columns].astype(f32) * scaled
        part_ref[rows, :] = dot32(norm_ref[:, columns], d_logits, TN).astype(bf16)
        return 0

    lax.fori_loop(0, QUERY_HEADS, gather, 0, unroll=2)
    r = rms_ref[...]
    mean = jnp.sum(acc_scr[...], axis=1, keepdims=True) * (1.0 / (QUERY_HEADS * HEAD_SIZE))
    pull = r * r * r * mean

    def finish(h, _):
        columns = lanes(h * HEAD_SIZE, HEAD_SIZE)
        res = og_ref[:, columns].astype(f32) + r * dn_scr[:, columns] - hid_ref[:, columns].astype(f32) * pull
        res_ref[:, columns] = res.astype(bf16)
        return 0

    lax.fori_loop(0, QUERY_HEADS, finish, 0, unroll=2)


def combine(ranks, gates, ids, back, hidden, normed, inv_rms, out_grad, gain, router):
    tokens, width = hidden.shape
    experts = router.shape[1]
    f32, bf16 = jnp.float32, jnp.bfloat16
    return pl.pallas_call(
        combine_kernel,
        in_specs=[pl.BlockSpec(memory_space=pltpu.SMEM)] * 3
        + [pl.BlockSpec(memory_space=pltpu.VMEM)] * 9,
        out_specs=[pl.BlockSpec(memory_space=pltpu.VMEM)] * 2,
        scratch_shapes=[
            pltpu.VMEM((tokens * PITCH, HEAD_SIZE), f32),
            pltpu.VMEM((tokens, HEAD_SIZE), f32),
            pltpu.VMEM((tokens, width), f32),
            pltpu.VMEM((tokens, HEAD_SIZE), f32),
        ],
        out_shape=[
            jax.ShapeDtypeStruct((tokens, width), bf16),
            jax.ShapeDtypeStruct((width, experts), bf16),
        ],
        compiler_params=pltpu.CompilerParams(vmem_limit_bytes=50 << 20),
        cost_estimate=pl.CostEstimate(
            flops=4 * tokens * width * experts, bytes_accessed=9 << 20, transcendentals=0
        ),
        name="combine",
    )(ids.reshape(-1), ranks, gates.reshape(-1), back, gates, ids, hidden, normed, inv_rms, out_grad, gain, router)


def pair_kernel(keep_ref, came_ref, out_ref):
    def one(b, _):
        out_ref[b] = (keep_ref[b].astype(jnp.float32) + came_ref[b].astype(jnp.float32)).astype(
            jnp.bfloat16
        )
        return 0

    lax.fori_loop(0, keep_ref.shape[0], one, 0)


def pair_sum(keep, came):
    vmem = pl.BlockSpec(memory_space=pltpu.VMEM)
    return pl.pallas_call(
        pair_kernel,
        in_specs=[vmem] * 2,
        out_specs=vmem,
        out_shape=jax.ShapeDtypeStruct(keep.shape, keep.dtype),
        compiler_params=pltpu.CompilerParams(vmem_limit_bytes=59 << 20),
        cost_estimate=pl.CostEstimate(flops=keep.size, bytes_accessed=3 << 20, transcendentals=0),
        name="pair_sum",
    )(keep, came)


def block_sum_kernel(parts_ref, keys_ref, values_ref):
    total = parts_ref[0].astype(jnp.float32)
    for b in range(1, parts_ref.shape[0]):
        total = total + parts_ref[b].astype(jnp.float32)
    half = keys_ref.shape[1]
    keys_ref[...] = total[:, :half].astype(jnp.bfloat16)
    values_ref[...] = total[:, half:].astype(jnp.bfloat16)


def block_sum(parts):
    vmem = pl.BlockSpec(memory_space=pltpu.VMEM)
    shape = jax.ShapeDtypeStruct((parts.shape[1], parts.shape[2] // 2), parts.dtype)
    return pl.pallas_call(
        block_sum_kernel,
        in_specs=[vmem],
        out_specs=[vmem] * 2,
        out_shape=[shape, shape],
        compiler_params=pltpu.CompilerParams(vmem_limit_bytes=50 << 20),
        cost_estimate=pl.CostEstimate(flops=parts.size, bytes_accessed=2 << 20, transcendentals=0),
        name="block_sum",
    )(parts)


def swap_cores(array):
    return lax.ppermute(array, CORE, [(0, 1), (1, 0)])


def exchange(array, axes):
    return lax.all_to_all(array, axes, split_axis=0, concat_axis=0, tiled=True)


def layer(
    queries,
    keys,
    values,
    stream,
    norm_gain,
    router_weight,
    gate_weight,
    up_weight,
    down_weight,
    doc_lengths,
    expert_ids,
    out_grad,
):
    token_rows = queries.shape[1]
    both = jnp.concatenate([keys[0], values[0]], axis=1)
    near = exchange(jnp.broadcast_to(both[None], (lax.axis_size("blk_0"), *both.shape)), "blk_0")
    far = lax.ppermute(near, "blk_1", [(0, 1), (1, 0)])
    near_other = swap_cores(near)
    sources = (near, far, near_other, swap_cores(far))

    meta = jnp.concatenate([lax.axis_index(GRP_BLK).astype(jnp.int32)[None], doc_lengths[0]])
    experts = router_weight.shape[1]
    chosen_ids = expert_ids[0]
    top_count = chosen_ids.shape[1]
    capacity = max(2, 3 * token_rows * top_count // (2 * experts))
    flat_ids = chosen_ids.reshape(-1)
    same = flat_ids[:, None] == flat_ids[None, :]
    order = jnp.arange(flat_ids.shape[0], dtype=jnp.int32)
    slot_rank = jnp.sum((same & (order[None, :] < order[:, None])).astype(jnp.int32), axis=1, dtype=jnp.int32)
    slots = flat_ids * capacity + slot_rank
    slot_count = experts * capacity

    send_grads = place(slots, out_grad[0], slot_count)
    got_grads = exchange(send_grads.reshape(experts, -1, HEAD_SIZE), GRP_BLK)

    weights, linv, attended, hidden, normed, inv_rms, send_rows = attend(
        meta, slots, queries[0], sources, stream[0], norm_gain[None], slot_count
    )
    got_rows = exchange(send_rows.reshape(experts, -1, HEAD_SIZE), GRP_BLK)

    logits = jnp.dot(normed, router_weight, preferred_element_type=jnp.float32)
    hits = chosen_ids[:, :, None] == jnp.arange(experts, dtype=jnp.int32)[None, None, :]
    chosen = jnp.sum(jnp.where(hits, logits[:, None, :], 0.0), axis=-1)
    first_gate = jax.nn.sigmoid(chosen[:, 0] - chosen[:, 1])
    gates = jnp.stack([first_gate, 1.0 - first_gate], axis=1)

    inner_grad = down(got_grads, down_weight[0])
    back = exchange(expert(got_rows, inner_grad, gate_weight[0], up_weight[0]), GRP_BLK)
    residual_gradient, router_parts = combine(
        slot_rank, gates, chosen_ids, back, hidden, normed, inv_rms, out_grad[0], norm_gain[None], router_weight
    )
    got_parts = exchange(router_parts.reshape(experts, -1, experts), GRP_BLK)
    query_grad, keep, give = attend_back(
        meta, queries[0], residual_gradient, attended, linv, sources, weights
    )
    pairs = pair_sum(keep, swap_cores(give))
    key_grad, value_grad = block_sum(exchange(pairs, ZX))
    router_grad = jnp.sum(got_parts.astype(jnp.float32), axis=0)
    return (
        query_grad[None],
        key_grad[None],
        value_grad[None],
        residual_gradient[None],
        router_grad,
    )


def solution(mesh):
    split = Mesh(mesh.devices.reshape(2, 4, 4, 2, 2), ("grp_0", "grp_1", "blk_0", "blk_1", "blk_2"))
    return jax.shard_map(
        layer,
        mesh=split,
        in_specs=(
            P(GRP, BLK, None),
            P(GRP, BLK, None),
            P(GRP, BLK, None),
            P(GRP, BLK, None),
            P(),
            P(),
            P(GRP_BLK, None, None),
            P(GRP_BLK, None, None),
            P(GRP_BLK, None, None),
            P(GRP, None),
            P(GRP, BLK, None),
            P(GRP, BLK, None),
        ),
        out_specs=(
            P(GRP, BLK, None),
            P(GRP, BLK, None),
            P(GRP, BLK, None),
            P(GRP, BLK, None),
            P(GRP_BLK, None),
        ),
        check_vma=False,
    )
```
